32 devices in a mesh: shard: 2 (over x), ctx: 4 (over z), tp: 4 (over y, core).
Axes of the slice: x: 2, y: 2, z: 4, core: 2. Of those that a mesh axis runs over, the one named last changes fastest.
Arguments:
- tokens: bfloat16 [2, 1536, 1536], P('shard', 'ctx'), may hold values from -6 to 6
- seg_parents: int32 [2, 13], P('shard'), may hold values from -1 to 4, as said below
- seg_offsets: int32 [2, 14], P('shard'), may hold values from 0 to 1536, as said below
- tok_seg: int32 [2, 1536], P('shard', 'ctx'), may hold values from 0 to 12, as said below
- norm_gain: float32 [2, 1536], P(None, 'shard'), may hold values from 0.5 to 1.5
- w_attn: float32 [1536, 4, 1536], P('shard', None, 'tp'), may hold values from -0.15625 to 0.15625
- w_heads: float32 [1536, 3, 24], P('shard', None, 'tp'), may hold values from -0.15625 to 0.15625
- forget_bias: float32 [24], P('tp'), may hold values from 3 to 8
- qk_gain: float32 [2, 1536], P(None, 'tp'), may hold values from 0.5 to 1.5
- w_out: float32 [1536, 1536], P('tp', 'shard'), may hold values from -1.25 to 1.25
- w_gate_up: float32 [1536, 2, 4096], P('shard', None, 'tp'), may hold values from -0.15625 to 0.15625
- w_down: float32 [4096, 1536], P('tp', 'shard'), may hold values from -0.09375 to 0.09375
- cotangent: bfloat16 [2, 1536, 1536], P('shard', 'ctx'), may hold values from -6 to 6
Outputs:
- out: bfloat16 [2, 1536, 1536], P('shard', 'ctx')
- d_tokens: float32 [2, 1536, 1536], P('shard', 'ctx')
- d_norm_gain: float32 [2, 1536], P(None, 'shard')
- d_w_attn: float32 [1536, 4, 1536], P('shard', None, 'tp')
- d_w_heads: float32 [1536, 3, 24], P('shard', None, 'tp')
- d_forget_bias: float32 [24], P('tp')
- d_qk_gain: float32 [2, 1536], P(None, 'tp')
- d_w_out: float32 [1536, 1536], P('tp', 'shard')
- d_w_gate_up: float32 [1536, 2, 4096], P('shard', None, 'tp')
- d_w_down: float32 [4096, 1536], P('tp', 'shard')
The draws below stay inside these ranges and needn't reach their ends.
Inputs may be any that keep to these rules, and one draw needn't show every extreme that they name: `seg_parents`: in every tree segment 0 is the trunk with parent -1, segments 1 to 4 have parent 0, and each of segments 1 to 4 is the parent of exactly two of segments 5 to 12. Segment s holds tokens seg_offsets[s] to seg_offsets[s + 1] - 1; seg_offsets[0] is 0, seg_offsets[13] is 1536, and every segment holds one token or more. `tok_seg`: agrees with seg_offsets.
All inputs are finite; a program needn't handle non-finite values.
Results may differ from the reference program's by a relative error of at most 0.019.
Values may be sent and summed in bfloat16 or wider, within the bound.
No kernel may reach another device: no remote copies, remote signals or barrier semaphores. Data moves between devices by JAX's collectives and lax.ppermute only.
A program may use at most 192 MiB of HBM per device.

```python
import jax
import jax.numpy as jnp
from jax import lax

D = 1536
H = 24
HD = 64
FF = 4096
TOK_DEV = 384
NSEG = 13
TREE_TOK = 1536
TREES = 2


def tree_layout(key):
    unit_len = TREE_TOK // 24

    def one_layout(tree_key):
        branch_key, leaf_key, parent_key = jax.random.split(tree_key, 3)
        branch_delta = jax.random.randint(branch_key, (2,), 0, unit_len + 1).astype(jnp.int32)
        leaf_delta = jax.random.randint(leaf_key, (4,), 0, unit_len // 2 + 1).astype(jnp.int32)
        branch_len = jnp.stack([2 * unit_len + branch_delta[0], 2 * unit_len - branch_delta[0], 2 * unit_len + branch_delta[1], 2 * unit_len - branch_delta[1]])
        leaf_len = jnp.stack([unit_len + leaf_delta, unit_len - leaf_delta], axis=1).reshape(8)
        lengths = jnp.concatenate([jnp.full((1,), 8 * unit_len, jnp.int32), branch_len.astype(jnp.int32), leaf_len.astype(jnp.int32)])
        offsets = jnp.concatenate([jnp.zeros((1,), jnp.int32), jnp.cumsum(lengths).astype(jnp.int32)])
        leaf_parent = (1 + jax.random.permutation(parent_key, 8) // 2).astype(jnp.int32)
        parents = jnp.concatenate([jnp.full((1,), -1, jnp.int32), jnp.zeros((4,), jnp.int32), leaf_parent])
        position = jnp.arange(TREE_TOK, dtype=jnp.int32)
        segments = jnp.sum((position[:, None] >= offsets[None, 1:NSEG]).astype(jnp.int32), axis=1).astype(jnp.int32)
        return (parents, offsets, segments)
    tree_keys = jax.random.split(jax.random.fold_in(key, 7), TREES)
    return jax.vmap(one_layout)(tree_keys)


def draw_seg_parents(key, part):
    return tree_layout(key)[0]


def draw_seg_offsets(key, part):
    return tree_layout(key)[1]


def draw_tok_seg(key, part):
    return tree_layout(key)[2]


def level_of(stream_key, dims, shards, least, top_value):
    def one(dim, parts):
        heights = jax.random.uniform(jax.random.fold_in(jax.random.fold_in(stream_key, 6), dim), (parts,), jnp.float32, least / len(shards), top_value / len(shards))
        return jnp.repeat(jnp.exp(heights), dims[dim] // parts).reshape((-1,) + (1,) * (len(dims) - dim - 1))

    level = one(*shards[0])
    for cut in shards[1:]:
        level = level * one(*cut)
    return level


def gaussian(key, extent, width, reach, cuts=(), kind=jnp.bfloat16):
    loudness = level_of(key, extent, cuts, -0.22, 0.18) if cuts else 1.0
    entries = jax.random.normal(key, extent, jnp.float32) * width * loudness
    return jnp.minimum(jnp.maximum(entries, -reach), reach).astype(kind)


def setup_inputs(seed: int = 0) -> dict:
    key_list = jax.random.split(jax.random.key(seed), 14)
    return {
        "tokens": gaussian(key_list[0], (TREES, TREE_TOK, D), 1.0, 6.0, ((0, 2), (1, 4))),
        "seg_parents": draw_seg_parents(jax.random.fold_in(key_list[13], 71), 0),
        "seg_offsets": draw_seg_offsets(jax.random.fold_in(key_list[13], 71), 0),
        "tok_seg": draw_tok_seg(jax.random.fold_in(key_list[13], 71), 0),
        "norm_gain": jnp.clip(1.0 + 0.1 * jax.random.normal(key_list[4], (2, D), jnp.float32), 0.5, 1.5),
        "w_attn": gaussian(key_list[5], (D, 4, D), D ** -0.5, 0.15625, ((0, 2), (2, 4)), jnp.float32),
        "w_heads": gaussian(key_list[6], (D, 3, H), D ** -0.5, 0.15625, ((0, 2), (2, 4)), jnp.float32),
        "forget_bias": jnp.clip(3.0 + 5.0 * jax.random.uniform(key_list[7], (H,), jnp.float32) ** level_of(key_list[7], (H,), ((0, 4),), -0.2, 0.2), 3.0, 8.0),
        "qk_gain": jnp.clip(1.0 + 0.1 * jax.random.normal(key_list[8], (2, D), jnp.float32), 0.5, 1.5),
        "w_out": gaussian(key_list[9], (D, D), (D // 64) ** -0.5, 1.25, ((0, 4), (1, 2)), jnp.float32),
        "w_gate_up": gaussian(key_list[10], (D, 2, FF), D ** -0.5, 0.15625, ((0, 2), (2, 4)), jnp.float32),
        "w_down": gaussian(key_list[11], (FF, D), FF ** -0.5, 0.09375, ((0, 4), (1, 2)), jnp.float32),
        "cotangent": gaussian(key_list[12], (TREES, TREE_TOK, D), 1.0, 6.0, ((0, 2), (1, 4))),
    }


epsilon = 1e-06
neg_large = -1e+30
highest = lax.Precision.HIGHEST

@jax.custom_vjp
def low(v):
    return lax.optimization_barrier(v.astype(jnp.bfloat16)).astype(jnp.float32)

@jax.custom_vjp
def low_back(v):
    return v

def low_keep(v):
    return (low(v), None)

def low_pass(kept, grad):
    return (grad,)

def back_keep(v):
    return (v, None)

def back_low(kept, grad):
    return (low(grad),)
low.defvjp(low_keep, low_pass)
low_back.defvjp(back_keep, back_low)

def row_norm(values):
    return values * lax.rsqrt(lax.optimization_barrier(jnp.mean(values * values, axis=-1, keepdims=True)) + epsilon)

def head_norm(values):
    tok_rows = values.shape[0]
    return row_norm(values.reshape(tok_rows, H, HD)).reshape(tok_rows, H * HD)

def climb(parent_mat):
    identity = jnp.eye(parent_mat.shape[0], dtype=jnp.float32)

    def extend(level_index, reached):
        return identity + jnp.dot(parent_mat, reached, precision=highest)
    return lax.fori_loop(0, parent_mat.shape[0], extend, identity)

def tree_layer(inputs, parents, offsets, segments, params):
    norm_gain, w_attn, w_heads, forget_bias, qk_gain, w_out, w_gate_up, w_down = params
    tok_rows = inputs.shape[0]
    gain_rows = low(norm_gain)
    attn_mat = low(w_attn).reshape(D, 4 * D)
    heads_mat = low(w_heads).reshape(D, 3 * H)
    out_mat = low(w_out)
    gateup_mat = low(w_gate_up).reshape(D, 2 * FF)
    down_mat = low(w_down)
    first_in = low(row_norm(inputs) * gain_rows[0])
    projected = low_back(jnp.dot(first_in, attn_mat, precision=highest)).reshape(tok_rows, 4, D)
    head_lin = low_back(jnp.dot(first_in, heads_mat, precision=highest)).reshape(tok_rows, 3, H)
    forget_in = head_lin[:, 0] + forget_bias
    log_forget = jax.nn.log_sigmoid(forget_in)
    alphas = jax.nn.sigmoid(head_lin[:, 1:])
    alpha_full = jnp.repeat(alphas, HD, axis=2).reshape(tok_rows, 2 * D)
    positions = jnp.arange(tok_rows, dtype=jnp.int32)
    seg_start = offsets[segments]
    seg_parent = parents[segments]
    parent_end = offsets[jnp.maximum(seg_parent, 0) + 1] - 1
    previous = jnp.where(positions != seg_start, positions - 1, jnp.where(seg_parent >= 0, parent_end, -1))
    present = (previous >= 0).astype(jnp.float32)[:, None]
    raw_kv = projected[:, 1:3].reshape(tok_rows, 2 * D)
    before = raw_kv[jnp.maximum(previous, 0)] * present
    shifted = raw_kv + alpha_full * (before - raw_kv)
    query_all = low(head_norm(projected[:, 0]) * qk_gain[0])
    key_all = low(head_norm(shifted[:, :D]) * qk_gain[1])
    value_all = low(shifted[:, D:])
    seg_ids = jnp.arange(NSEG, dtype=jnp.int32)
    onehot = (segments[:, None] == seg_ids[None, :]).astype(jnp.float32)
    parent_mat = (parents[:, None] == seg_ids[None, :]).astype(jnp.float32)
    ancestry = climb(parent_mat)
    linked = jnp.dot(jnp.dot(onehot, ancestry, precision=highest), onehot.T, precision=highest) > 0.5
    visible = linked & (positions[None, :] <= positions[:, None])
    forget_sum = jnp.dot(visible.astype(jnp.float32), log_forget, precision=highest)
    key_heads = key_all.reshape(tok_rows, H, HD)
    value_heads = value_all.reshape(tok_rows, H, HD)

    def attend(block_item):
        query_rows, forget_rows, visible_rows = block_item
        products = jnp.einsum('qhe,khe->hqk', query_rows, key_heads, precision=highest) * HD ** (-0.5)
        scores = products + forget_rows.T[:, :, None] - forget_sum.T[:, None, :]
        scores = low_back(jnp.where(visible_rows[None], scores, neg_large))
        row_top = lax.optimization_barrier(jnp.max(scores, axis=2, keepdims=True))
        log_total = row_top + jnp.log(lax.optimization_barrier(jnp.sum(jnp.exp(scores - row_top), axis=2, keepdims=True)))
        weights = low(jnp.exp(scores - log_total))
        return low_back(jnp.einsum('hqk,khe->qhe', weights, value_heads, precision=highest))
    block_rows = TOK_DEV // 2
    block_total = tok_rows // block_rows
    attended = lax.map(jax.checkpoint(attend), (query_all.reshape(block_total, block_rows, H, HD), forget_sum.reshape(block_total, block_rows, H), visible.reshape(block_total, block_rows, tok_rows))).reshape(tok_rows, D)
    gate_sig = jax.nn.sigmoid(projected[:, 3])
    gated = low(attended * gate_sig)
    middle = inputs + low_back(jnp.dot(gated, out_mat, precision=highest))
    second_in = low(row_norm(middle) * gain_rows[1])
    gate_up = low_back(jnp.dot(second_in, gateup_mat, precision=highest)).reshape(tok_rows, 2, FF)
    hidden = low(jax.nn.silu(gate_up[:, 0]) * gate_up[:, 1])
    return middle + low_back(jnp.dot(hidden, down_mat, precision=highest))

def reference(tokens, seg_parents, seg_offsets, tok_seg, norm_gain, w_attn, w_heads, forget_bias, qk_gain, w_out, w_gate_up, w_down, cotangent):
    params = (norm_gain, w_attn, w_heads, forget_bias, qk_gain, w_out, w_gate_up, w_down)

    def one_tree(summed, tree_item):
        tree_tokens, tree_cot, parents, offsets, segments = tree_item

        def forward(inputs, weights):
            return tree_layer(inputs, parents, offsets, segments, weights)
        result, backward = jax.vjp(forward, tree_tokens.astype(jnp.float32), params)
        d_inputs, d_params = backward(tree_cot.astype(jnp.float32))
        summed = jax.tree.map(jnp.add, summed, d_params)
        return (summed, (result.astype(jnp.bfloat16), d_inputs))
    zero_grads = jax.tree.map(jnp.zeros_like, params)
    totals, (outputs, d_tokens) = lax.scan(one_tree, zero_grads, (tokens, cotangent, seg_parents, seg_offsets, tok_seg))
    return (outputs, d_tokens, totals[0], totals[1], totals[2], totals[3], totals[4], totals[5], totals[6], totals[7])
```

```python
import jax
import jax.numpy as jnp
from jax import lax
from jax.sharding import PartitionSpec as P

epsilon = 1e-06
neg_large = -1e30
highest = lax.Precision.HIGHEST
f32 = jnp.float32
bf16 = jnp.bfloat16


def from_ring(values, axis, step):
    count = lax.axis_size(axis)
    return lax.ppermute(values, axis, [((i + step) % count, i) for i in range(count)])


def along(values, axis, step):
    count = lax.axis_size(axis)
    return lax.ppermute(
        values, axis, [(i, i + step) for i in range(count) if 0 <= i + step < count]
    )


def partner(values, axis, bit):
    count = lax.axis_size(axis)
    return lax.ppermute(values, axis, [(i, i ^ bit) for i in range(count)])


def turned(values, axis, first, count):
    width = values.shape[axis] // count
    pieces = [
        lax.dynamic_slice_in_dim(values, ((first + i) % count) * width, width, axis)
        for i in range(count)
    ]
    return jnp.concatenate(pieces, axis=axis)


def mm(left, right):
    return jnp.dot(left, right, preferred_element_type=f32)


def mm_nt(left, right):
    return lax.dot_general(left, right, (((1,), (1,)), ((), ())), preferred_element_type=f32)


def mm_tn(left, right):
    return lax.dot_general(left, right, (((0,), (0,)), ((), ())), preferred_element_type=f32)


def exact(left, right):
    return jnp.dot(left, right, precision=highest)


def exact_tn(left, right):
    return lax.dot_general(left, right, (((0,), (0,)), ((), ())), precision=highest)


def rms_scale(values):
    return lax.rsqrt(jnp.mean(values * values, axis=-1, keepdims=True) + epsilon)


def norm_grad(values, scale, gain_row, d_result):
    normed = values * scale
    d_normed = d_result * gain_row
    d_values = scale * (d_normed - normed * jnp.mean(d_normed * normed, axis=-1, keepdims=True))
    return d_values, jnp.sum(d_result * normed, axis=0)


def ctx_sum(values):
    count = lax.axis_size("ctx")
    index = lax.axis_index("ctx")
    half = count // 2
    if half == 0:
        return values
    kind = values.dtype

    def add(left, right):
        return (left.astype(f32) + right.astype(f32)).astype(kind)

    total = values
    for k in range(half - 1):
        got = lax.ppermute(total, "ctx", [(k, k + 1), (count - 1 - k, count - 2 - k)])
        total = add(total, got)
    got = lax.ppermute(total, "ctx", [(half - 1, half), (half, half - 1)])
    total = add(total, got)
    for k in reversed(range(half - 1)):
        got = lax.ppermute(total, "ctx", [(k + 1, k), (count - 2 - k, count - 1 - k)])
        total = jnp.where((index == k) | (index == count - 1 - k), got, total)
    return total


def body(
    tokens,
    seg_parents,
    seg_offsets,
    tok_seg,
    norm_gain,
    w_attn,
    w_heads,
    forget_bias,
    qk_gain,
    w_out,
    w_gate_up,
    w_down,
    cotangent,
):
    shards = lax.axis_size("shard")
    shard = lax.axis_index("shard")
    ctxs = lax.axis_size("ctx")
    ctx = lax.axis_index("ctx")
    tps = lax.axis_size("tp")
    core = lax.axis_index("tp") % 2
    rows = tokens.shape[1]
    half_rows = rows // 2
    width = tokens.shape[2]
    part = width // shards
    local = w_attn.shape[2]
    heads = w_heads.shape[2]
    head_size = local // heads
    hidden_size = w_gate_up.shape[2]
    segs = seg_parents.shape[1]
    qk_scale = head_size ** (-0.5)

    def gathered(piece):
        return [piece] + [from_ring(piece, "shard", d) for d in range(1, shards)]

    gain_parts = gathered(norm_gain.astype(bf16))
    heads_w = gathered(w_heads.astype(bf16).reshape(part, 3 * heads))
    kv_w = gathered(w_attn[:, 1:3].astype(bf16).reshape(part, 2 * local))
    query_w = gathered(w_attn[:, 0].astype(bf16))
    gate_w = gathered(w_attn[:, 3].astype(bf16))
    out_w = gathered(w_out.astype(bf16))
    gateup_w = gathered(w_gate_up.astype(bf16).reshape(part, 2 * hidden_size))
    down_w = gathered(w_down.astype(bf16))

    def cut(values, d):
        return values[:, d * part : (d + 1) * part]

    def into(values, weights):
        total = mm(cut(values, 0), weights[0])
        for d in range(1, shards):
            total = total + mm(cut(values, d), weights[d])
        return total

    def out_of(values, weights):
        return jnp.concatenate([mm(values, w) for w in weights], axis=1)

    def back_out(values, weights):
        return jnp.concatenate([mm_nt(values, w) for w in weights], axis=1)

    def back_into(values, weights):
        total = mm_nt(cut(values, 0), weights[0])
        for d in range(1, shards):
            total = total + mm_nt(cut(values, d), weights[d])
        return total

    def tp_sum(partial_of):
        given = partner(partial_of(1), "tp", 1)
        total = (partial_of(0) + given).astype(bf16)
        bit = 2
        while bit < tps:
            other = partner(total, "tp", bit)
            total = total.astype(f32) + other.astype(f32)
            bit = bit * 2
            if bit < tps:
                total = total.astype(bf16)
        return total.astype(f32)

    def both_rows(own):
        return jnp.concatenate([own, partner(own, "tp", 1)], axis=0)

    gains = jnp.concatenate([g.astype(f32) for g in gain_parts], axis=1)
    inputs = turned(tokens[0], 1, shard, shards).astype(f32)
    grad_out = turned(turned(cotangent[0], 1, shard, shards), 0, core, 2)
    parents = seg_parents[0]
    offsets = seg_offsets[0]
    query_seg = tok_seg[0]
    row_start = ctx * rows
    query_pos = row_start + jnp.arange(rows, dtype=jnp.int32)
    seg_ids = jnp.arange(segs, dtype=jnp.int32)
    key_pos = jnp.concatenate([query_pos - d * rows for d in range(ctxs)])
    parent_mat = (parents[:, None] == seg_ids[None, :]).astype(bf16)
    ancestry = (
        jnp.eye(segs, dtype=f32) + parent_mat.astype(f32) + mm(parent_mat, parent_mat)
    )
    query_onehot = (query_seg[:, None] == seg_ids[None, :]).astype(bf16)
    query_anc = mm(query_onehot, ancestry.astype(bf16)).astype(bf16)
    query_parent = mm(query_onehot, parent_mat)
    key_onehot = (
        (key_pos[:, None] >= offsets[None, :segs]) & (key_pos[:, None] < offsets[None, 1:])
    ).astype(bf16)
    visible = (mm_nt(query_anc, key_onehot) > 0.5) & (key_pos[None, :] <= query_pos[:, None])
    visible_own = visible[:, :rows].astype(f32)
    is_start = jnp.sum((query_pos[:, None] == offsets[None, :segs]).astype(f32), axis=1) > 0.5
    end_select = (query_pos[None, :] == (offsets[1:] - 1)[:, None]).astype(f32)

    scale_one = rms_scale(inputs)
    first_in = (inputs * scale_one * gains[0]).astype(bf16)
    head_lin = into(first_in, heads_w)
    raw_kv = into(first_in, kv_w)
    forget_in = head_lin[:, :heads] + forget_bias
    log_forget = jax.nn.log_sigmoid(forget_in)
    alphas = jax.nn.sigmoid(head_lin[:, heads:])
    spread = (
        jnp.arange(2 * heads, dtype=jnp.int32)[:, None]
        == jnp.arange(2 * local, dtype=jnp.int32)[None, :] // head_size
    ).astype(f32)
    alpha_full = exact(alphas, spread)
    seg_sums = exact_tn(query_onehot.astype(f32), log_forget)
    side = 128
    table = jnp.concatenate([exact(end_select, raw_kv), raw_kv[-1:]], axis=0)
    message = jnp.concatenate(
        [table, jnp.pad(seg_sums, ((0, 1), (0, side - heads)))], axis=1
    )
    arrived = [along(message, "ctx", d) for d in range(1, ctxs)]
    earlier_all = sum(arrived[1:], arrived[0])
    seg_ends = table[:segs] + earlier_all[:segs, : 2 * local]
    before_first = arrived[0][segs:, : 2 * local]
    forget_sum = exact(visible_own, log_forget) + exact(
        query_anc.astype(f32), earlier_all[:segs, 2 * local : 2 * local + heads]
    )
    previous = jnp.concatenate([before_first, raw_kv[:-1]], axis=0)
    previous = jnp.where(is_start[:, None], exact(query_parent, seg_ends), previous)
    shift_delta = previous - raw_kv
    shifted = raw_kv + alpha_full * shift_delta
    raw_q = into(first_in, query_w)
    raw_g = into(first_in, gate_w)

    def head_scale(values):
        split = values.reshape(rows, heads, head_size)
        scale = rms_scale(split)
        return jnp.broadcast_to(scale, split.shape).reshape(rows, local)

    scale_q = head_scale(raw_q)
    key_shift = shifted[:, :local]
    scale_k = head_scale(key_shift)
    query_b = (raw_q * scale_q * qk_gain[0]).astype(bf16)
    key_b = (key_shift * scale_k * qk_gain[1]).astype(bf16)
    own_kv = jnp.concatenate([key_b, shifted[:, local:].astype(bf16)], axis=1)
    forget_keys = jnp.concatenate(
        [forget_sum] + [along(forget_sum, "ctx", d) for d in range(1, ctxs)], axis=0
    )
    all_kv = jnp.concatenate(
        [own_kv] + [along(own_kv, "ctx", d) for d in range(1, ctxs)], axis=0
    )
    keys = all_kv[:, :local].reshape(-1, heads, head_size)
    vals = all_kv[:, local:].reshape(-1, heads, head_size)
    query_heads = query_b.reshape(rows, heads, head_size)

    def attn_scores():
        products = (
            jnp.einsum("qhe,khe->hqk", query_heads, keys, preferred_element_type=f32) * qk_scale
        )
        scores = products + forget_sum.T[:, :, None] - forget_keys.T[:, None, :]
        return jnp.where(visible[None], scores, neg_large)

    scores = attn_scores()
    row_max = jnp.max(scores, axis=2, keepdims=True)
    log_total = row_max + jnp.log(jnp.sum(jnp.exp(scores - row_max), axis=2, keepdims=True))
    probs = jnp.exp(scores - log_total)
    probs_b = probs.astype(bf16)
    attended = jnp.einsum("hqk,khe->qhe", probs_b, vals, preferred_element_type=f32).reshape(
        rows, local
    )
    gate_sig = jax.nn.sigmoid(raw_g)
    gated = turned((attended * gate_sig).astype(bf16), 0, core, 2)

    def rows_of(values, which):
        return values[which * half_rows : (which + 1) * half_rows]

    attn_sum = tp_sum(lambda which: out_of(rows_of(gated, which), out_w))
    own_in = rows_of(turned(inputs, 0, core, 2), 0)
    middle = own_in + attn_sum
    scale_two = rms_scale(middle)
    second_in = both_rows((middle * scale_two * gains[1]).astype(bf16))
    gate_up = into(second_in, gateup_w)
    gate_lin = gate_up[:, :hidden_size]
    up_lin = gate_up[:, hidden_size:]
    silu_sig = jax.nn.sigmoid(gate_lin)
    silu = gate_lin * silu_sig
    hidden = (silu * up_lin).astype(bf16)
    d_hidden = back_into(grad_out, down_w)
    d_gate_up = jnp.concatenate(
        [
            (d_hidden * up_lin * silu_sig * (1.0 + gate_lin * (1.0 - silu_sig))).astype(bf16),
            (d_hidden * silu).astype(bf16),
        ],
        axis=1,
    )
    d_second = tp_sum(lambda which: back_out(rows_of(d_gate_up, which), gateup_w))
    grad_own = rows_of(grad_out, 0).astype(f32)
    d_middle_norm, d_gain_two = norm_grad(middle, scale_two, gains[1], d_second)
    d_middle = grad_own + d_middle_norm
    d_middle_b = both_rows(d_middle.astype(bf16))
    mlp_sum = tp_sum(lambda which: out_of(rows_of(hidden, which), down_w))
    output = both_rows((middle + mlp_sum).astype(bf16))

    def shard_sum(part_of):
        total = part_of(0)
        for d in range(1, shards):
            total = total + from_ring(part_of(d).astype(bf16), "shard", shards - d).astype(f32)
        return ctx_sum(total.astype(bf16)).astype(f32)

    d_down = shard_sum(lambda d: mm_tn(hidden, cut(grad_out, d)))
    d_gateup = shard_sum(lambda d: mm_tn(cut(second_in, d), d_gate_up))
    d_out = shard_sum(lambda d: mm_tn(gated, cut(d_middle_b, d)))

    d_gated = turned(back_into(d_middle_b, out_w), 0, core, 2)
    d_attended = (d_gated * gate_sig).astype(bf16)
    d_raw_g = d_gated * attended * gate_sig * (1.0 - gate_sig)
    d_att_heads = d_attended.reshape(rows, heads, head_size)
    d_probs = jnp.einsum("qhe,khe->hqk", d_att_heads, vals, preferred_element_type=f32)
    delta = jnp.sum(probs * d_probs, axis=2, keepdims=True)
    d_scores = (probs * (d_probs - delta)).astype(bf16)
    d_query = (
        jnp.einsum("hqk,khe->qhe", d_scores, keys, preferred_element_type=f32) * qk_scale
    ).reshape(rows, local)
    d_keys = (
        jnp.einsum("hqk,qhe->khe", d_scores, query_heads, preferred_element_type=f32) * qk_scale
    ).reshape(-1, local)
    d_vals = jnp.einsum("hqk,qhe->khe", probs_b, d_att_heads, preferred_element_type=f32).reshape(
        -1, local
    )
    d_scores_f = d_scores.astype(f32)
    d_forget_q = jnp.sum(d_scores_f, axis=2).T
    d_forget_k = -jnp.sum(d_scores_f, axis=1).T
    d_kv = jnp.concatenate([d_keys, d_vals], axis=1)

    def block(values, d):
        return values[d * rows : (d + 1) * rows]

    def to_owner(values, kind):
        total = block(values, ctxs - 1)
        for d in reversed(range(ctxs - 1)):
            total = block(values, d) + along(total.astype(kind), "ctx", -1).astype(f32)
        return total

    d_forget = d_forget_q + to_owner(d_forget_k, f32)
    d_shifted = to_owner(d_kv, bf16)

    d_raw_q, d_gain_q = head_grad(raw_q, scale_q, qk_gain[0], d_query, heads)
    d_key_shift, d_gain_k = head_grad(key_shift, scale_k, qk_gain[1], d_shifted[:, :local], heads)
    d_shift = jnp.concatenate([d_key_shift, d_shifted[:, local:]], axis=1)
    d_alphas = exact_nt(d_shift * shift_delta, spread) * alphas * (1.0 - alphas)
    d_prev = alpha_full * d_shift
    start_col = is_start[:, None]
    d_step = jnp.where(start_col, 0.0, d_prev)
    d_table = exact_tn(jnp.where(start_col, query_parent, 0.0), d_prev)
    seg_grads = exact_tn(query_onehot.astype(f32), d_forget)
    back_message = jnp.concatenate(
        [
            jnp.concatenate([d_table, d_step[:1]], axis=0),
            jnp.pad(seg_grads, ((0, 1), (0, side - heads))),
        ],
        axis=1,
    )
    returned = [along(back_message, "ctx", -d) for d in range(1, ctxs)]
    later_all = sum(returned[1:], returned[0])
    d_ends = exact_tn(end_select, d_table + later_all[:segs, : 2 * local])
    d_raw_kv = (
        d_shift
        - d_prev
        + jnp.concatenate([d_step[1:], returned[0][segs:, : 2 * local]], axis=0)
        + d_ends
    )
    later_grads = exact_tn(ancestry, later_all[:segs, 2 * local : 2 * local + heads])
    d_log_forget = exact_tn(visible_own, d_forget) + exact(query_onehot.astype(f32), later_grads)
    d_forget_in = d_log_forget * jax.nn.sigmoid(-forget_in)
    d_head_lin = jnp.concatenate([d_forget_in, d_alphas], axis=1).astype(bf16)
    d_raw_q = d_raw_q.astype(bf16)
    d_raw_kv = d_raw_kv.astype(bf16)
    d_raw_g = d_raw_g.astype(bf16)

    d_gate_wt = shard_sum(lambda d: mm_tn(cut(first_in, d), d_raw_g))
    d_query_wt = shard_sum(lambda d: mm_tn(cut(first_in, d), d_raw_q))
    d_kv_wt = shard_sum(lambda d: mm_tn(cut(first_in, d), d_raw_kv))
    d_heads_wt = shard_sum(lambda d: mm_tn(cut(first_in, d), d_head_lin))

    turned_q = turned(d_raw_q, 0, core, 2)
    turned_kv = turned(d_raw_kv, 0, core, 2)
    turned_g = turned(d_raw_g, 0, core, 2)
    turned_h = turned(d_head_lin, 0, core, 2)

    def first_part(which):
        return (
            back_out(rows_of(turned_q, which), query_w)
            + back_out(rows_of(turned_kv, which), kv_w)
            + back_out(rows_of(turned_g, which), gate_w)
            + back_out(rows_of(turned_h, which), heads_w)
        )

    d_first = tp_sum(first_part)
    own_scale = rms_scale(own_in)
    d_input_norm, d_gain_one = norm_grad(own_in, own_scale, gains[0], d_first)
    d_inputs = both_rows(d_middle + d_input_norm)
    d_inputs = turned(turned(d_inputs, 0, core, 2), 1, -shard, shards)
    output = turned(turned(output, 0, core, 2), 1, -shard, shards)

    d_gains = jnp.stack([d_gain_one, d_gain_two], axis=0)
    d_gains = d_gains + partner(d_gains, "tp", 1)
    small_width = max(part, local)

    def widened(values):
        return jnp.pad(values, ((0, 0), (0, small_width - values.shape[1])))

    shared = jnp.concatenate(
        [
            widened(jnp.stack([d_gain_q, d_gain_k], axis=0)),
            widened(jnp.sum(d_forget_in, axis=0)[None]),
        ],
        axis=0,
    )

    def small_for(d):
        return jnp.concatenate([widened(cut(d_gains, d)), shared], axis=0)

    small = small_for(0)
    for d in range(1, shards):
        small = small + from_ring(small_for(d), "shard", shards - d)
    small = ctx_sum(small)
    return (
        output[None],
        d_inputs[None],
        small[:2, :part],
        jnp.stack(
            [d_query_wt, d_kv_wt[:, :local], d_kv_wt[:, local:], d_gate_wt], axis=1
        ),
        d_heads_wt.reshape(part, 3, heads),
        small[4, :heads],
        small[2:4, :local],
        d_out,
        d_gateup.reshape(part, 2, hidden_size),
        d_down,
    )


def exact_nt(left, right):
    return lax.dot_general(left, right, (((1,), (1,)), ((), ())), precision=highest)


def head_grad(values, scale, gain_row, d_result, heads):
    rows, local = values.shape
    normed = values * scale
    d_normed = d_result * gain_row
    mean = jnp.mean((d_normed * normed).reshape(rows, heads, -1), axis=-1, keepdims=True)
    mean = jnp.broadcast_to(mean, (rows, heads, local // heads)).reshape(rows, local)
    return scale * (d_normed - normed * mean), jnp.sum(d_result * normed, axis=0)


def solution(mesh):
    in_specs = (
        P("shard", "ctx", None),
        P("shard", None),
        P("shard", None),
        P("shard", "ctx"),
        P(None, "shard"),
        P("shard", None, "tp"),
        P("shard", None, "tp"),
        P("tp"),
        P(None, "tp"),
        P("tp", "shard"),
        P("shard", None, "tp"),
        P("tp", "shard"),
        P("shard", "ctx", None),
    )
    out_specs = (
        P("shard", "ctx", None),
        P("shard", "ctx", None),
        P(None, "shard"),
        P("shard", None, "tp"),
        P("shard", None, "tp"),
        P("tp"),
        P(None, "tp"),
        P("tp", "shard"),
        P("shard", None, "tp"),
        P("tp", "shard"),
    )
    return jax.shard_map(body, mesh=mesh, in_specs=in_specs, out_specs=out_specs, check_vma=False)
```

```python
import jax
import jax.numpy as jnp
from jax import lax
from jax.experimental import pallas as pl
from jax.experimental.pallas import tpu as pltpu
from jax.sharding import PartitionSpec as P

epsilon = 1e-06
neg_large = -1e30
highest = lax.Precision.HIGHEST
f32 = jnp.float32
bf16 = jnp.bfloat16
segs_up = 16


def from_ring(values, axis, step):
    count = lax.axis_size(axis)
    return lax.ppermute(values, axis, [((i + step) % count, i) for i in range(count)])


def along(values, axis, step):
    count = lax.axis_size(axis)
    return lax.ppermute(
        values, axis, [(i, i + step) for i in range(count) if 0 <= i + step < count]
    )


def partner(values, axis, bit):
    count = lax.axis_size(axis)
    return lax.ppermute(values, axis, [(i, i ^ bit) for i in range(count)])


def dot_of(dims, precision=None):
    def product(left, right):
        return lax.dot_general(
            left, right, (dims, ((), ())), precision=precision, preferred_element_type=f32
        )

    return product


mm = dot_of(((1,), (0,)))
mm_nt = dot_of(((1,), (1,)))
mm_tn = dot_of(((0,), (0,)))
exact = dot_of(((1,), (0,)), highest)
exact_nt = dot_of(((1,), (1,)), highest)
exact_tn = dot_of(((0,), (0,)), highest)


def rms_scale(values):
    return lax.rsqrt(jnp.mean(values * values, axis=-1, keepdims=True) + epsilon)


def norm_grad(values, scale, gain_row, d_result):
    normed = values * scale
    d_normed = d_result * gain_row
    d_values = scale * (d_normed - normed * jnp.mean(d_normed * normed, axis=-1, keepdims=True))
    return d_values, jnp.sum(d_result * normed, axis=0, keepdims=True)


def iota(shape, axis):
    return lax.broadcasted_iota(jnp.int32, shape, axis)


def same_head(width, size):
    return jnp.where(iota((width, width), 0) // size == iota((width, width), 1) // size, 1.0, 0.0)


def head_mean(values, size):
    return exact(values, same_head(values.shape[1], size)) * (1.0 / size)


def head_scale(values, size):
    return lax.rsqrt(head_mean(values * values, size) + epsilon)


def head_grad(values, gain_row, d_result, size):
    scale = head_scale(values, size)
    normed = values * scale
    d_normed = d_result * gain_row
    d_values = scale * (d_normed - normed * head_mean(d_normed * normed, size))
    return d_values, jnp.sum(d_result * normed, axis=0, keepdims=True)


def spread_of(heads_up, width, size):
    return jnp.where(iota((heads_up, width), 0) == iota((heads_up, width), 1) // size, 1.0, 0.0)


def nbytes(leaf):
    return leaf.size * leaf.dtype.itemsize


def whole(kernel, outs, *args, extra=8):
    leaves, form = jax.tree.flatten(args)

    def flat(*refs):
        kernel(*jax.tree.unflatten(form, refs[: len(leaves)]), *refs[len(leaves) :])

    shapes = [jax.ShapeDtypeStruct(shape, kind) for shape, kind in outs]
    spaces = [
        pltpu.SMEM if leaf.ndim == 1 and leaf.dtype == jnp.int32 else pltpu.VMEM
        for leaf in leaves
    ]
    size = sum(nbytes(x) for x in leaves) + sum(nbytes(x) for x in shapes)
    found = pl.pallas_call(
        flat,
        out_shape=shapes,
        in_specs=[pl.BlockSpec(memory_space=s) for s in spaces],
        out_specs=[pl.BlockSpec(memory_space=pltpu.VMEM) for _ in shapes],
        compiler_params=pltpu.CompilerParams(
            vmem_limit_bytes=min(60 << 20, size + size // 4 + (extra << 20))
        ),
        cost_estimate=pl.CostEstimate(flops=1, transcendentals=1, bytes_accessed=1),
        name=kernel.__name__,
    )(*leaves)
    return found


def masks_kernel(place, low, high, high_col, parents_col, seg_col, bias, key_anc, onehot, parent, start, ends, anc, key_onehot):
    rows = seg_col.shape[0]
    ctx = place[2]
    lanes = iota((segs_up, segs_up), 1)
    parent_mat = jnp.where(parents_col[...] == lanes, 1.0, 0.0)
    eye = jnp.where(iota((segs_up, segs_up), 0) == lanes, 1.0, 0.0)
    ancestry = eye + parent_mat + exact(parent_mat, parent_mat)
    anc[...] = ancestry
    mine = jnp.where(seg_col[...] == iota((rows, segs_up), 1), 1.0, 0.0)
    onehot[...] = mine
    parent[...] = exact(mine, parent_mat)
    mine_anc = exact(mine, ancestry)
    query_pos = ctx * rows + iota((1, rows), 1)
    query_col = ctx * rows + iota((rows, 1), 0)
    ends[...] = jnp.where(query_pos == high_col[...] - 1, 1.0, 0.0)
    start[...] = jnp.sum(
        jnp.where(query_col == low[...], 1.0, 0.0), axis=1, keepdims=True
    )
    for d in range(bias.shape[0] // rows):
        span = slice(d * rows, (d + 1) * rows)
        key_pos = (ctx - d) * rows + iota((rows, 1), 0)
        keys = jnp.where((key_pos >= low[...]) & (key_pos < high[...]), 1.0, 0.0)
        key_anc[span, :] = exact(keys, ancestry)
        key_onehot[span, :] = keys
        linked = mm_nt(keys.astype(bf16), mine_anc.astype(bf16)) > 0.5
        bias[span, :] = jnp.where(linked & (key_pos <= query_pos), 0.0, neg_large)


def turned(values, first, count):
    width = values.shape[1] // count
    pieces = [
        lax.dynamic_slice_in_dim(values, lax.rem(first + i, count) * width, width, 1)
        for i in range(count)
    ]
    return jnp.concatenate(pieces, axis=1)


def part_at(ref, shard, d, shards, rows=slice(None)):
    part = ref.shape[1] // shards
    if part % 128:
        return ref[rows, d * part : (d + 1) * part]
    start = pl.multiple_of(lax.rem(shard + d, shards) * part, 128)
    return ref[rows, pl.ds(start, part)]


def enter_kernel(place, tokens, packs, first_in):
    shards = len(packs)
    part = packs[0].shape[1]
    pieces = [part_at(tokens, place[1], d, shards).astype(f32) for d in range(shards)]
    mean = sum(jnp.sum(x * x, axis=1, keepdims=True) for x in pieces) * (
        1.0 / tokens.shape[1]
    )
    scale = lax.rsqrt(mean + epsilon)
    for d in range(shards):
        gain = packs[d][24:25, :].astype(f32)
        first_in[:, d * part : (d + 1) * part] = (pieces[d] * scale * gain).astype(bf16)


def keys_in_kernel(first_in, kv_w, packs, forget_bias, bias, onehot, ends, raw_kv, lin, message):
    part = packs[0].shape[1]
    rows = first_in.shape[0]
    local = raw_kv.shape[2]
    heads_up = forget_bias.shape[0]
    cuts = [first_in[:, d * part : (d + 1) * part] for d in range(len(packs))]
    head_lin = sum(mm_nt(p[:24, :], x) for p, x in zip(packs, cuts))
    forget_in = head_lin[:heads_up] + forget_bias[...]
    lin[...] = head_lin
    lin[:heads_up, :] = forget_in
    log_forget = jnp.minimum(forget_in, 0.0) - jnp.log1p(jnp.exp(-jnp.abs(forget_in)))
    seen = jnp.where(bias[:rows, :] == 0.0, 1.0, 0.0)
    message[...] = jnp.zeros_like(message)
    for i in range(2):
        raw = sum(mm(x, w[i]) for w, x in zip(kv_w, cuts))
        raw_kv[i] = raw
        cols = slice(i * local, (i + 1) * local)
        message[:segs_up, cols] = exact(ends[...], raw)
        message[segs_up - 1 : segs_up, cols] = raw[rows - 1 :]
    message[segs_up : segs_up + heads_up, :rows] = exact(log_forget, seen)
    message[segs_up : segs_up + heads_up, local : local + segs_up] = exact(
        log_forget, onehot[...]
    )


def keys_shift_kernel(raw_kv, lin, blocks, parent, start, key_anc, gain, own_kv, delta, fq, fk, *, size):
    rows, local = raw_kv.shape[1:]
    heads_up = lin.shape[0] // 3
    spread = spread_of(heads_up, local, size)
    seg_ends = sum((b[:segs_up, :] for b in blocks[1:]), blocks[0][:segs_up, :])
    at_start = start[...] > 0.5
    at_top = iota((rows, 1), 0) == 0
    for i in range(2):
        cols = slice(i * local, (i + 1) * local)
        alpha_rows = jax.nn.sigmoid(lin[(i + 1) * heads_up : (i + 2) * heads_up, :])
        alpha = exact_tn(alpha_rows, spread)
        raw = raw_kv[i]
        previous = jnp.where(
            at_top, blocks[1][segs_up - 1 : segs_up, cols], pltpu.roll(raw, 1, 0)
        )
        previous = jnp.where(at_start, exact(parent[...], seg_ends[:, cols]), previous)
        step = previous - raw
        delta[i] = step
        shifted = raw + alpha * step
        if i == 0:
            shifted = shifted * head_scale(shifted, size) * gain[...]
        own_kv[i] = shifted.astype(bf16)
    table = slice(segs_up, segs_up + heads_up)
    for d in range(len(blocks)):
        sums = blocks[d][table, :rows]
        span = slice(d * rows, (d + 1) * rows)
        later = blocks[d + 1 :]
        if later:
            before = sum(
                (b[table, local : local + segs_up] for b in later[1:]),
                later[0][table, local : local + segs_up],
            )
            sums = sums + exact_nt(before, key_anc[span, :])
        for h in range(2 * fk.shape[0]):
            fk[h // 2, h % 2 : h % 2 + 1, span] = sums[h : h + 1]
            if d == 0:
                fq[h // 2, h % 2 : h % 2 + 1, :] = sums[h : h + 1]


def queries_kernel(first_in, query_w, gate_w, gain, raw_q, query, raw_g, *, size):
    part = query_w[0].shape[0]
    cuts = [first_in[:, d * part : (d + 1) * part] for d in range(len(query_w))]
    raw = sum(mm(x, w[...]) for w, x in zip(query_w, cuts))
    raw_q[...] = raw
    raw_g[...] = sum(mm(x, w[...]) for w, x in zip(gate_w, cuts))
    normed = (raw * head_scale(raw, size) * gain[...]).astype(bf16)
    query[...] = (normed.astype(f32) * (size**-0.5)).astype(bf16)


def share_kernel(values, weights, out, *, which):
    half = out.shape[0]
    part = out.shape[1] // len(weights)
    rows = slice(which * half, (which + 1) * half)
    for d, w in enumerate(weights):
        out[:, d * part : (d + 1) * part] = mm(values[rows, :], w[...])


def share_sum_kernel(values, weights, given, out):
    half = out.shape[0]
    part = out.shape[1] // len(weights)
    for d, w in enumerate(weights):
        cols = slice(d * part, (d + 1) * part)
        out[:, cols] = (mm(values[:half, :], w[...]) + given[:, cols]).astype(bf16)


def middle_kernel(place, tokens, packs, total, other, middle, second_in):
    shards = len(packs)
    part = packs[0].shape[1]
    half = total.shape[0]
    rows = pl.ds(pl.multiple_of(place[0] * half, 16), half)
    square = jnp.zeros((half, 1), f32)
    for d in range(shards):
        cols = slice(d * part, (d + 1) * part)
        value = part_at(tokens, place[1], d, shards, rows).astype(f32) + (
            total[:, cols].astype(f32) + other[:, cols].astype(f32)
        )
        middle[:, cols] = value
        square = square + jnp.sum(value * value, axis=1, keepdims=True)
    scale = lax.rsqrt(square * (1.0 / middle.shape[1]) + epsilon)
    for d in range(shards):
        cols = slice(d * part, (d + 1) * part)
        gain = packs[d][25:26, :].astype(f32)
        second_in[:, cols] = (middle[:, cols] * scale * gain).astype(bf16)


def grad_hidden_kernel(place, cotangent, down_w, grad_out, d_hidden):
    shards = len(down_w)
    part = down_w[0].shape[1]
    half = cotangent.shape[0] // 2
    for k in range(2):
        rows = pl.ds(pl.multiple_of(lax.rem(place[0] + k, 2) * half, 16), half)
        span = slice(k * half, (k + 1) * half)
        for d in range(shards):
            grad_out[span, d * part : (d + 1) * part] = part_at(
                cotangent, place[1], d, shards, rows
            )
    d_hidden[...] = sum(
        mm_nt(grad_out[:, d * part : (d + 1) * part], w[...]) for d, w in enumerate(down_w)
    )


def mlp_kernel(*refs):
    mine, theirs = refs[:2]
    weights = refs[2:-4]
    d_hidden, hidden, d_gate, d_up = refs[-4:]
    part = weights[0].shape[1]
    half = mine.shape[0]
    for k, second in enumerate((mine, theirs)):
        rows = slice(k * half, (k + 1) * half)
        lin = [
            sum(mm(second[:, d * part : (d + 1) * part], w[i]) for d, w in enumerate(weights))
            for i in range(2)
        ]
        sig = jax.nn.sigmoid(lin[0])
        silu = lin[0] * sig
        grad = d_hidden[rows, :]
        hidden[rows, :] = (silu * lin[1]).astype(bf16)
        d_gate[rows, :] = (grad * lin[1] * (sig * (1.0 + lin[0] * (1.0 - sig)))).astype(bf16)
        d_up[rows, :] = (grad * silu).astype(bf16)


def mlp(mine, theirs, weights, d_hidden):
    half, width = mine.shape
    rows, hidden_size = d_hidden.shape
    part = weights[0].shape[1]
    block = 256
    flat = pl.BlockSpec((half, width), lambda j: (0, 0))
    return pl.pallas_call(
        mlp_kernel,
        grid=(hidden_size // block,),
        in_specs=[flat, flat]
        + [pl.BlockSpec((2, part, block), lambda j: (0, 0, j)) for _ in weights]
        + [pl.BlockSpec((rows, block), lambda j: (0, j))],
        out_specs=[pl.BlockSpec((rows, block), lambda j: (0, j))] * 3,
        out_shape=[jax.ShapeDtypeStruct((rows, hidden_size), bf16)] * 3,
        compiler_params=pltpu.CompilerParams(vmem_limit_bytes=24 << 20),
        cost_estimate=pl.CostEstimate(flops=1, transcendentals=1, bytes_accessed=1),
        name="mlp",
    )(mine, theirs, *weights, d_hidden)


def back_share_kernel(d_gate, d_up, weights, out, *, which):
    half = out.shape[0]
    part = out.shape[1] // len(weights)
    rows = slice(which * half, (which + 1) * half)
    for d, w in enumerate(weights):
        out[:, d * part : (d + 1) * part] = mm_nt(d_gate[rows, :], w[0]) + mm_nt(d_up[rows, :], w[1])


def back_share_sum_kernel(d_gate, d_up, weights, given, out):
    half = out.shape[0]
    part = out.shape[1] // len(weights)
    for d, w in enumerate(weights):
        cols = slice(d * part, (d + 1) * part)
        out[:, cols] = (
            mm_nt(d_gate[:half, :], w[0])
            + mm_nt(d_up[:half, :], w[1])
            + given[:, cols]
        ).astype(bf16)


def gain_row(packs, row):
    return jnp.concatenate([p[row : row + 1, :].astype(f32) for p in packs], axis=1)


def middle_back_kernel(grad_out, packs, middle, total, other, d_middle, d_middle_b, d_gain):
    half = middle.shape[0]
    value = middle[...]
    d_second = total[...].astype(f32) + other[...].astype(f32)
    d_value, gain = norm_grad(value, rms_scale(value), gain_row(packs, 25), d_second)
    d_gain[...] = gain
    d_value = d_value + grad_out[:half, :].astype(f32)
    d_middle[...] = d_value
    d_middle_b[...] = d_value.astype(bf16)


def gate_back_kernel(place, mine, theirs, out_w, raw_g, attended, d_attended, d_raw_g):
    half = mine.shape[0]
    part = out_w[0].shape[1]
    for k, source in enumerate((mine, theirs)):
        rows = pl.ds(pl.multiple_of(lax.rem(place[0] + k, 2) * half, 16), half)
        d_gated = sum(
            mm_nt(source[:, d * part : (d + 1) * part], w[...]) for d, w in enumerate(out_w)
        )
        sig = jax.nn.sigmoid(raw_g[rows, :])
        d_attended[rows, :] = (d_gated * sig).astype(bf16)
        d_raw_g[rows, :] = (d_gated * attended[rows, :] * sig * (1.0 - sig)).astype(bf16)


def query_back_kernel(raw_q, d_query, gain, d_raw_g, d_gq, d_gain, *, size):
    local = raw_q.shape[1]
    d_raw, gain_grad = head_grad(raw_q[...], gain[...], d_query[...], size)
    d_gain[...] = gain_grad
    d_gq[:, :local] = d_raw_g[...]
    d_gq[:, local:] = d_raw.astype(bf16)


def chain_kernel(partial, got, out):
    out[...] = (partial[...].astype(f32) + got[...].astype(f32)).astype(out.dtype)


def shift_back_kernel(
    d_kv, got, raw_kv, delta, lin, gain, start, parent, dcq, dck, key_onehots,
    base, messages, d_alpha, d_gain, d_forget_own, *, size,
):
    rows, local = raw_kv.shape[1:]
    heads_up = lin.shape[0] // 3
    heads = 2 * dcq.shape[0]
    spread = spread_of(heads_up, local, size)
    not_start = 1.0 - start[...]
    start_parent = parent[...] * start[...]
    for m in messages:
        m[...] = jnp.zeros_like(m)
    for i in range(2):
        cols = slice(i * local, (i + 1) * local)
        alpha_rows = jax.nn.sigmoid(lin[(i + 1) * heads_up : (i + 2) * heads_up, :])
        alpha = exact_tn(alpha_rows, spread)
        d_shift = d_kv[i] + got[i].astype(f32)
        if i == 0:
            shifted = raw_kv[0] + alpha * delta[0]
            d_shift, gain_grad = head_grad(shifted, gain[...], d_shift, size)
            d_gain[...] = gain_grad
        d_alpha[i * heads_up : (i + 1) * heads_up, :] = (
            exact_nt(spread, d_shift * delta[i]) * alpha_rows * (1.0 - alpha_rows)
        )
        d_prev = alpha * d_shift
        d_step = d_prev * not_start
        base[i] = (
            d_shift
            - d_prev
            + jnp.where(iota((rows, 1), 0) == rows - 1, 0.0, pltpu.roll(d_step, rows - 1, 0))
        )
        table = exact_tn(start_parent, d_prev)
        for m in messages:
            m[:segs_up, cols] = table
            m[segs_up - 1 : segs_up, cols] = d_step[:1]
    later = jnp.zeros((heads_up, segs_up), f32)
    blank = jnp.zeros((heads_up - heads, rows), f32)
    for d in range(len(messages) + 1):
        span = slice(d * rows, (d + 1) * rows)
        grads = jnp.concatenate(
            [-dck[h // 2, h % 2 : h % 2 + 1, span] for h in range(heads)] + [blank], axis=0
        )
        if d == 0:
            grads = grads + jnp.concatenate(
                [dcq[h // 2, h % 2 : h % 2 + 1, :] for h in range(heads)] + [blank], axis=0
            )
            d_forget_own[...] = grads
        else:
            messages[d - 1][segs_up : segs_up + heads_up, :rows] = grads
            messages[d - 1][segs_up : segs_up + heads_up, local : local + segs_up] = later
        if d < len(messages):
            later = later + exact(grads, key_onehots[span, :])


def raw_back_kernel(
    base, table_own, returned, ends, bias, onehot, anc, lin, d_forget_own, d_alpha,
    d_raw_kv, d_lin, d_bias,
):
    rows, local = base.shape[1:]
    heads_up = lin.shape[0] // 3
    tail = slice(segs_up, segs_up + heads_up)
    for i in range(2):
        cols = slice(i * local, (i + 1) * local)
        table = table_own[:segs_up, cols]
        for r in returned:
            table = table + r[:segs_up, cols]
        edge = jnp.where(
            iota((rows, 1), 0) == rows - 1, returned[0][segs_up - 1 : segs_up, cols], 0.0
        )
        d_raw_kv[i] = (base[i] + edge + exact_tn(ends[...], table)).astype(bf16)
    own = d_forget_own[...]
    sums = jnp.zeros((heads_up, segs_up), f32)
    for r in returned:
        own = own + r[tail, :rows]
        sums = sums + r[tail, local : local + segs_up]
    seen = jnp.where(bias[:rows, :] == 0.0, 1.0, 0.0)
    d_log = exact_nt(own, seen) + exact_nt(exact(sums, anc[...]), onehot[...])
    d_forget = d_log * jax.nn.sigmoid(-lin[:heads_up, :])
    d_bias[...] = jnp.sum(d_forget, axis=1, keepdims=True)
    d_lin[:heads_up, :] = d_forget.astype(bf16)
    d_lin[heads_up:, :] = d_alpha[...].astype(bf16)


def first_gq_kernel(place, d_gq, gate_w, query_w, out):
    half = d_gq.shape[0] // 2
    part = gate_w[0].shape[0]
    local = d_gq.shape[1] // 2
    for k in range(2):
        rows = pl.ds(pl.multiple_of(lax.rem(place[0] + k, 2) * half, 16), half)
        for d in range(len(gate_w)):
            out[k * half : (k + 1) * half, d * part : (d + 1) * part] = mm_nt(
                d_gq[rows, :local], gate_w[d][...]
            ) + mm_nt(d_gq[rows, local:], query_w[d][...])


def first_share_kernel(place, d_kv, d_lin, kv_w, packs, partial, out, heads_part, *, which):
    half = out.shape[0]
    part = packs[0].shape[1]
    rows = pl.ds(pl.multiple_of(lax.rem(place[0] + which, 2) * half, 16), half)
    for d in range(len(packs)):
        cols = slice(d * part, (d + 1) * part)
        heads_part[...] = mm_tn(d_lin[...], packs[d][:24, :])
        out[:, cols] = (
            mm_nt(d_kv[0, rows, :], kv_w[d][0])
            + mm_nt(d_kv[1, rows, :], kv_w[d][1])
            + heads_part[rows, :]
            + partial[which * half : (which + 1) * half, cols]
        ).astype(out.dtype)


def first_sum_kernel(mine, given, out):
    out[...] = (mine[...] + given[...]).astype(bf16)


def enter_back_kernel(place, tokens, packs, d_middle, total, other, d_own, d_gain):
    shards = len(packs)
    half = total.shape[0]
    rows = pl.ds(pl.multiple_of(place[0] * half, 16), half)
    value = jnp.concatenate(
        [part_at(tokens, place[1], d, shards, rows).astype(f32) for d in range(shards)], axis=1
    )
    d_first = total[...].astype(f32) + other[...].astype(f32)
    d_value, gain = norm_grad(value, rms_scale(value), gain_row(packs, 24), d_first)
    d_gain[...] = gain
    d_own[...] = d_middle[...] + d_value


def settle_kernel(place, mine, theirs, out, *, shards):
    half = mine.shape[0]
    part = mine.shape[1] // shards
    for k, source in enumerate((mine, theirs)):
        rows = pl.ds(pl.multiple_of(lax.rem(place[0] + k, 2) * half, 16), half)
        for d in range(shards):
            cols = slice(d * part, (d + 1) * part)
            if part % 128:
                out[rows, cols] = source[:, cols]
            else:
                start = pl.multiple_of(lax.rem(place[1] + d, shards) * part, 128)
                out[rows, pl.ds(start, part)] = source[:, cols]


def leave_kernel(middle, total, other, out):
    out[...] = (
        middle[...] + (total[...].astype(f32) + other[...].astype(f32))
    ).astype(bf16)


def named(kernel, **fixed):
    def bound(*refs):
        kernel(*refs, **fixed)

    bound.__name__ = kernel.__name__
    return bound


class At:

    def __init__(self, array, rows=None, cols=None, lead=None):
        if cols and (cols[0] % 128 or cols[1] % 128):
            array, cols = array[..., cols[0] : cols[1]], None
        self.array, self.lead = array, lead
        self.rows = rows or (0, array.shape[-2])
        self.cols = cols or (0, array.shape[-1])

    def spec(self, block=None):
        start, stop = self.rows
        height = stop - start
        first, last = self.cols
        wide = block or last - first
        shape, row, col = (height, wide), start // height, first // wide

        def at(j):
            return (row, col + j if block else col)

        if self.lead is None:
            return pl.BlockSpec(shape, at)
        return pl.BlockSpec((None,) + shape, lambda j: (self.lead,) + at(j))


def weight_grad(order, pairs, got, block):
    count = len(pairs)
    rows = pairs[0][0].cols[1] - pairs[0][0].cols[0]
    width = pairs[0][1].cols[1] - pairs[0][1].cols[0]

    def weight_grad_kernel(*refs):
        total = mm_tn(refs[0][...], refs[1][...])
        for i in range(1, count):
            total = total + mm_tn(refs[2 * i][...], refs[2 * i + 1][...])
        for ref in refs[2 * count : -1]:
            total = total + ref[...].astype(f32)
        refs[-1][...] = total.astype(bf16)

    specs = [spec for a, b in pairs for spec in (a.spec(block), b.spec())]
    over = pl.BlockSpec((block, width), lambda j: (j, 0))
    call = pl.pallas_call(
        weight_grad_kernel,
        grid=(rows // block,),
        in_specs=specs + [over for _ in got],
        out_specs=over,
        out_shape=jax.ShapeDtypeStruct((rows, width), bf16),
        compiler_params=pltpu.CompilerParams(vmem_limit_bytes=20 << 20),
        cost_estimate=pl.CostEstimate(flops=1, transcendentals=1, bytes_accessed=1),
        name="weight_grad",
    )
    return order(call, *[x.array for pair in pairs for x in pair], *got)


def add_rows(left, right):
    rows, width = left.shape
    block = rows if rows % 64 else 64 if rows <= 256 else 128

    def add_kernel(left, right, out):
        out[...] = (left[...].astype(f32) + right[...].astype(f32)).astype(out.dtype)

    over = pl.BlockSpec((block, width), lambda j: (j, 0))
    return pl.pallas_call(
        add_kernel,
        grid=(rows // block,),
        in_specs=[over, over],
        out_specs=over,
        out_shape=jax.ShapeDtypeStruct((rows, width), left.dtype),
        compiler_params=pltpu.CompilerParams(vmem_limit_bytes=8 << 20),
        cost_estimate=pl.CostEstimate(flops=1, transcendentals=1, bytes_accessed=1),
        name="add",
    )(left, right)


def attend_kernel(*refs):
    place, query_ref, *kv_refs, bias_ref, cq_ref, ck_ref, gate_ref, out_ref, gated_ref, lse_ref = refs
    rows = query_ref.shape[0]
    half = rows // 2
    size = query_ref.shape[1] // 2
    key_cols = ck_ref[0].T
    outs = []
    for e in range(2):
        cols = slice(e * size, (e + 1) * size)
        query = query_ref[:, cols]
        forget_row = cq_ref[0, e : e + 1, :]
        total = jnp.zeros((1, rows), f32)
        mixed = jnp.zeros((size, rows), f32)
        for d in range(len(kv_refs) // 2):
            span = slice(d * rows, (d + 1) * rows)
            scores = mm_nt(kv_refs[2 * d][0, :, cols], query)
            scores = scores + (forget_row - key_cols[span, e : e + 1]) + bias_ref[span, :]
            weights = jnp.exp(scores)
            total = total + jnp.sum(weights, axis=0, keepdims=True)
            mixed = mixed + mm_tn(kv_refs[2 * d + 1][0, :, cols], weights.astype(bf16))
        outs.append((mixed / total).T)
        lse_ref[0, e : e + 1, :] = jnp.log(total)
    attended = jnp.concatenate(outs, axis=1)
    out_ref[...] = attended
    gated = (attended * jax.nn.sigmoid(gate_ref[...])).astype(bf16)
    for k in range(2):
        there = pl.ds(pl.multiple_of(lax.rem(place[0] + k, 2) * half, 16), half)
        gated_ref[there, :] = gated[k * half : (k + 1) * half]


def attend_back_kernel(*refs):
    count = (len(refs) - 10) // 3
    query_ref, d_out_ref = refs[:2]
    kv_refs = refs[2 : 2 + 2 * count]
    bias_ref, cq_ref, ck_ref, lse_ref = refs[2 + 2 * count : 6 + 2 * count]
    d_query_ref = refs[6 + 2 * count]
    d_kv_refs = refs[7 + 2 * count : 7 + 3 * count]
    dcq_ref, dck_ref, prob_ref, d_prob_ref = refs[7 + 3 * count :]
    rows = query_ref.shape[0]
    size = query_ref.shape[1] // 2
    key_cols = ck_ref[0].T
    ones = jnp.ones((8, rows), bf16)
    for e in range(2):
        cols = slice(e * size, (e + 1) * size)
        query = query_ref[:, cols]
        d_out = d_out_ref[:, cols]
        forget_row = cq_ref[0, e : e + 1, :] - lse_ref[0, e : e + 1, :]
        delta = jnp.zeros((1, rows), f32)
        for d in range(count):
            span = slice(d * rows, (d + 1) * rows)
            scores = mm_nt(kv_refs[2 * d][0, :, cols], query)
            scores = scores + (forget_row - key_cols[span, e : e + 1]) + bias_ref[span, :]
            probs = jnp.exp(scores)
            d_probs = mm_nt(kv_refs[2 * d + 1][0, :, cols], d_out)
            delta = delta + jnp.sum(probs * d_probs, axis=0, keepdims=True)
            prob_ref[span, :] = probs
            d_prob_ref[span, :] = d_probs
        d_query = jnp.zeros((size, rows), f32)
        d_row = jnp.zeros((1, rows), f32)
        for d in range(count):
            span = slice(d * rows, (d + 1) * rows)
            probs = prob_ref[span, :]
            d_scores = (probs * (d_prob_ref[span, :] - delta)).astype(bf16)
            d_kv_refs[d][0, :, cols] = mm(d_scores, query).astype(d_kv_refs[d].dtype)
            d_kv_refs[d][1, :, cols] = mm(probs.astype(bf16), d_out).astype(d_kv_refs[d].dtype)
            d_query = d_query + mm_tn(kv_refs[2 * d][0, :, cols], d_scores)
            d_row = d_row + jnp.sum(d_scores.astype(f32), axis=0, keepdims=True)
            dck_ref[0, e : e + 1, span] = mm_nt(ones, d_scores)[:1]
        d_query_ref[:, cols] = d_query.T * (size ** (-0.5))
        dcq_ref[0, e : e + 1, :] = d_row


def kv_specs(blocks, lanes):
    rows = blocks[0].shape[1]
    return [
        pl.BlockSpec((1, rows, lanes), lambda p, kind=kind: (kind, 0, p))
        for _ in blocks
        for kind in range(2)
    ]


def twice(blocks):
    return [b for b in blocks for _ in range(2)]


def attention(place, query, kv_blocks, bias, forget_q, forget_k, raw_g):
    rows, local = query.shape
    pairs = forget_q.shape[0]
    keys = bias.shape[0]
    lanes = local // pairs
    flat = pl.BlockSpec((rows, lanes), lambda p: (0, p))
    row_spec = pl.BlockSpec((1, 8, rows), lambda p: (p, 0, 0))
    return pl.pallas_call(
        attend_kernel,
        grid=(pairs,),
        in_specs=[pl.BlockSpec(memory_space=pltpu.SMEM), flat]
        + kv_specs(kv_blocks, lanes)
        + [
            pl.BlockSpec((keys, rows), lambda p: (0, 0)),
            row_spec,
            pl.BlockSpec((1, 8, keys), lambda p: (p, 0, 0)),
            flat,
        ],
        out_specs=[flat, flat, row_spec],
        out_shape=[
            jax.ShapeDtypeStruct((rows, local), f32),
            jax.ShapeDtypeStruct((rows, local), bf16),
            jax.ShapeDtypeStruct((pairs, 8, rows), f32),
        ],
        compiler_params=pltpu.CompilerParams(vmem_limit_bytes=32 << 20),
        cost_estimate=pl.CostEstimate(flops=1, transcendentals=1, bytes_accessed=1),
        name="attend",
    )(place, query, *twice(kv_blocks), bias, forget_q, forget_k, raw_g)


def attention_back(query, d_out, kv_blocks, bias, forget_q, forget_k, lse):
    rows, local = query.shape
    pairs = forget_q.shape[0]
    keys = bias.shape[0]
    lanes = local // pairs
    count = len(kv_blocks)
    flat = pl.BlockSpec((rows, lanes), lambda p: (0, p))
    row_spec = pl.BlockSpec((1, 8, rows), lambda p: (p, 0, 0))
    key_spec = pl.BlockSpec((1, 8, keys), lambda p: (p, 0, 0))
    return pl.pallas_call(
        attend_back_kernel,
        grid=(pairs,),
        in_specs=[flat, flat]
        + kv_specs(kv_blocks, lanes)
        + [pl.BlockSpec((keys, rows), lambda p: (0, 0)), row_spec, key_spec, row_spec],
        out_specs=[flat]
        + [pl.BlockSpec((2, rows, lanes), lambda p: (0, 0, p))] * count
        + [row_spec, key_spec],
        out_shape=[jax.ShapeDtypeStruct((rows, local), f32)]
        + [
            jax.ShapeDtypeStruct((2, rows, local), bf16 if d == count - 1 else f32)
            for d in range(count)
        ]
        + [
            jax.ShapeDtypeStruct((pairs, 8, rows), f32),
            jax.ShapeDtypeStruct((pairs, 8, keys), f32),
        ],
        scratch_shapes=[pltpu.VMEM((keys, rows), f32), pltpu.VMEM((keys, rows), f32)],
        compiler_params=pltpu.CompilerParams(vmem_limit_bytes=40 << 20),
        cost_estimate=pl.CostEstimate(flops=1, transcendentals=1, bytes_accessed=1),
        name="attend_back",
    )(query, d_out, *twice(kv_blocks), bias, forget_q, forget_k, lse)


def small_kernel(d_lin, first_in, gains, other, gain_q, gain_k, d_bias, *outs):
    part = first_in.shape[1] // len(outs)
    local = gain_q.shape[1]
    for d, out in enumerate(outs):
        cols = slice(d * part, (d + 1) * part)
        out[...] = jnp.zeros_like(out)
        out[:24, :part] = mm(d_lin[...], first_in[:, cols])
        out[24:26, :part] = gains[:, cols] + other[:, cols]
        out[26:27, :local] = gain_q[...]
        out[27:28, :local] = gain_k[...]
        out[32:40, :1] = d_bias[...]


class Order:

    def __init__(self):
        self.last = None

    def __call__(self, work, *args):
        if self.last is not None:
            args, _ = lax.optimization_barrier((args, self.last))
        found = work(*args)
        self.last = min(jax.tree.leaves(found), key=nbytes)
        return found


class LineSum:

    def __init__(self, order, values):
        self.order, self.total = order, values
        self.count = lax.axis_size("ctx")
        self.half = self.count // 2
        self.hop, self.coming = 0, None
        self.send()

    def send(self):
        k, count, half = self.hop, self.count, self.half
        if k < half - 1:
            pairs = [(k, k + 1), (count - 1 - k, count - 2 - k)]
        elif k == half - 1:
            pairs = [(half - 1, half), (half, half - 1)]
        elif k < 2 * half - 1:
            j = 2 * half - 2 - k
            pairs = [(j + 1, j), (count - 2 - j, count - 1 - j)]
        else:
            return
        self.coming = lax.ppermute(self.total, "ctx", pairs)

    def step(self):
        k, half = self.hop, self.half
        self.hop += 1
        if k < half:
            self.total = self.order(add_rows, self.total, self.coming)
        else:
            j = 2 * half - 2 - k
            index = lax.axis_index("ctx")
            ends = (index == j) | (index == self.count - 1 - j)
            self.total = self.order(
                lambda a, b: jnp.where(ends, b, a), self.total, self.coming
            )
        self.send()

    def finish(self):
        while self.hop < 2 * self.half - 1:
            self.step()
        return self.total


def body(
    tokens,
    seg_parents,
    seg_offsets,
    tok_seg,
    norm_gain,
    w_attn,
    w_heads,
    forget_bias,
    qk_gain,
    w_out,
    w_gate_up,
    w_down,
    cotangent,
):
    shards = lax.axis_size("shard")
    ctxs = lax.axis_size("ctx")
    ctx = lax.axis_index("ctx")
    tps = lax.axis_size("tp")
    rows, width = tokens.shape[1:]
    half = rows // 2
    part = width // shards
    local = w_attn.shape[2]
    heads = w_heads.shape[2]
    heads_up = 8
    size = local // heads
    hidden_size = w_gate_up.shape[2]
    segs = seg_parents.shape[1]
    order = Order()
    place = jnp.stack(
        [lax.axis_index("tp") % 2, lax.axis_index("shard"), ctx]
    ).astype(jnp.int32)

    def gathered(piece):
        return [piece] + [from_ring(piece, "shard", d) for d in range(1, shards)]

    def crossed(total):
        bit = 2
        other = partner(total, "tp", bit)
        while bit * 2 < tps:
            total = (total.astype(f32) + other.astype(f32)).astype(bf16)
            bit = bit * 2
            other = partner(total, "tp", bit)
        return total, other

    def pack_small(w, gain):
        table = jnp.pad(
            jnp.transpose(w, (1, 2, 0)), ((0, 0), (0, heads_up - heads), (0, 0))
        ).reshape(3 * heads_up, part)
        return jnp.concatenate([table, jnp.pad(gain, ((0, 6), (0, 0)))], axis=0).astype(bf16)

    packs = gathered(order(pack_small, w_heads, norm_gain))
    attn_b = order(lambda w: jnp.transpose(w, (1, 0, 2)).astype(bf16), w_attn)
    kv_w = gathered(order(lambda w: w[1:3], attn_b))
    padded = jnp.full((segs_up - segs,), -1, jnp.int32)
    low = jnp.concatenate([seg_offsets[0, :segs], padded])
    high = jnp.concatenate([seg_offsets[0, 1:], padded])
    parents = jnp.concatenate([seg_parents[0], padded])
    bias, key_anc, onehot, parent, start, ends, anc, key_onehot = order(
        lambda *a: whole(
            masks_kernel,
            [
                ((rows * ctxs, rows), f32),
                ((rows * ctxs, segs_up), f32),
                ((rows, segs_up), f32),
                ((rows, segs_up), f32),
                ((rows, 1), f32),
                ((segs_up, rows), f32),
                ((segs_up, segs_up), f32),
                ((rows * ctxs, segs_up), f32),
            ],
            *a,
        ),
        place,
        low[None],
        high[None],
        high[:, None],
        parents[:, None],
        tok_seg[0][:, None],
    )
    tree, cotangent = tokens[0], cotangent[0]
    if part % 128:
        tree = turned(tree, place[1], shards)
        cotangent = turned(cotangent, place[1], shards)

    def settled(values):
        return turned(values, shards - place[1], shards) if part % 128 else values

    (first_in,) = order(
        lambda *a: whole(enter_kernel, [((rows, width), bf16)], *a), place, tree, packs
    )
    query_w = gathered(order(lambda w: w[0], attn_b))
    gate_w = gathered(order(lambda w: w[3], attn_b))
    out_w = gathered(order(lambda w: w.astype(bf16), w_out))
    down_w = gathered(order(lambda w: w.astype(bf16), w_down))
    gateup_w = gathered(order(lambda w: jnp.transpose(w, (1, 0, 2)).astype(bf16), w_gate_up))

    forget_col = jnp.pad(forget_bias, (0, heads_up - heads))[:, None]
    raw_kv, lin, message = order(
        lambda *a: whole(
            keys_in_kernel,
            [
                ((2, rows, local), f32),
                ((3 * heads_up, rows), f32),
                ((segs_up + heads_up, 2 * local), f32),
            ],
            *a,
        ),
        first_in,
        kv_w,
        packs,
        forget_col,
        bias,
        onehot,
        ends,
    )
    blocks = [message] + [along(message, "ctx", d) for d in range(1, ctxs)]
    gain_q, gain_k = qk_gain[:1], qk_gain[1:]
    own_kv, delta, forget_q, forget_k = order(
        lambda *a: whole(
            named(keys_shift_kernel, size=size),
            [
                ((2, rows, local), bf16),
                ((2, rows, local), f32),
                ((heads // 2, 8, rows), f32),
                ((heads // 2, 8, rows * ctxs), f32),
            ],
            *a,
        ),
        raw_kv,
        lin,
        blocks,
        parent,
        start,
        key_anc,
        gain_k,
    )
    kv_blocks = [own_kv] + [along(own_kv, "ctx", d) for d in range(1, ctxs)]
    raw_q, query, raw_g = order(
        lambda *a: whole(
            named(queries_kernel, size=size),
            [((rows, local), f32), ((rows, local), bf16), ((rows, local), f32)],
            *a,
        ),
        first_in,
        query_w,
        gate_w,
        gain_q,
    )
    attended, gated, lse = order(
        attention, place, query, kv_blocks, bias, forget_q, forget_k, raw_g
    )

    (share,) = order(
        lambda *a: whole(named(share_kernel, which=1), [((half, width), f32)], *a), gated, out_w
    )
    given = partner(share, "tp", 1)
    (total,) = order(
        lambda *a: whole(share_sum_kernel, [((half, width), bf16)], *a), gated, out_w, given
    )
    total, other = crossed(total)
    grad_out, d_hidden = order(
        lambda *a: whole(
            grad_hidden_kernel, [((rows, width), bf16), ((rows, hidden_size), f32)], *a
        ),
        place,
        cotangent,
        down_w,
    )
    middle, second = order(
        lambda *a: whole(
            middle_kernel, [((half, width), f32), ((half, width), bf16)], *a
        ),
        place,
        tree,
        packs,
        total,
        other,
    )
    second_too = partner(second, "tp", 1)
    hidden, d_gate, d_up = order(mlp, second, second_too, gateup_w, d_hidden)
    (share,) = order(
        lambda *a: whole(named(back_share_kernel, which=1), [((half, width), f32)], *a),
        d_gate,
        d_up,
        gateup_w,
    )
    given = partner(share, "tp", 1)
    (total,) = order(
        lambda *a: whole(back_share_sum_kernel, [((half, width), bf16)], *a),
        d_gate,
        d_up,
        gateup_w,
        given,
    )
    second_total = crossed(total)

    def columns(d):
        return (d * part, (d + 1) * part)

    def sent(make):
        return [from_ring(make(d), "shard", shards - d) for d in range(1, shards)]

    def rows_at(k):
        return (k * half, (k + 1) * half)

    def down_part(d, got=()):
        return weight_grad(order, [(At(hidden), At(grad_out, cols=columns(d)))], got, 256)

    def gateup_part(d_lin, d, got=()):
        return weight_grad(
            order,
            [
                (At(x, cols=columns(d)), At(d_lin, rows=rows_at(k)))
                for k, x in enumerate((second, second_too))
            ],
            got,
            min(256, part),
        )

    down_got = sent(down_part)
    gate_got = sent(lambda d: gateup_part(d_gate, d))
    (share,) = order(
        lambda *a: whole(named(share_kernel, which=1), [((half, width), f32)], *a),
        hidden,
        down_w,
    )
    given = partner(share, "tp", 1)
    up_got = sent(lambda d: gateup_part(d_up, d))
    d_middle, d_middle_b, d_gain_two = order(
        lambda *a: whole(
            middle_back_kernel,
            [((half, width), f32), ((half, width), bf16), ((1, width), f32)],
            *a,
        ),
        grad_out,
        packs,
        middle,
        *second_total,
    )
    d_middle_too = partner(d_middle_b, "tp", 1)
    (total,) = order(
        lambda *a: whole(share_sum_kernel, [((half, width), bf16)], *a), hidden, down_w, given
    )
    mlp_total = crossed(total)
    d_attended, d_raw_g = order(
        lambda *a: whole(
            gate_back_kernel, [((rows, local), bf16), ((rows, local), bf16)], *a
        ),
        place,
        d_middle_b,
        d_middle_too,
        out_w,
        raw_g,
        attended,
    )
    backs = order(attention_back, query, d_attended, kv_blocks, bias, forget_q, forget_k, lse)
    d_query, d_kv = backs[0], backs[1 : 1 + ctxs]
    dcq, dck = backs[1 + ctxs :]

    def left(values, d):
        return lax.ppermute(values, "ctx", [(i, i - 1) for i in range(d, ctxs)])

    def chained(partial, got):
        return whole(chain_kernel, [(partial.shape, bf16)], partial, got)[0]

    def out_part(d, got=()):
        return weight_grad(
            order,
            [
                (At(gated, rows=rows_at(k)), At(x, cols=columns(d)))
                for k, x in enumerate((d_middle_b, d_middle_too))
            ],
            got,
            min(128, local),
        )

    coming = left(d_kv[ctxs - 1], ctxs - 1)
    d_gq, d_gain_q = order(
        lambda *a: whole(
            named(query_back_kernel, size=size),
            [((rows, 2 * local), bf16), ((1, local), f32)],
            *a,
        ),
        raw_q,
        d_query,
        gain_q,
        d_raw_g,
    )
    out_got = sent(out_part)
    gq_all = gathered(d_gq)
    first_parts = [first_in] + [
        from_ring(first_in[:, part * (shards - d) : part * (shards - d + 1)], "shard", d)
        for d in range(1, shards)
    ]
    for d in range(ctxs - 2, 0, -1):
        coming = left(order(chained, d_kv[d], coming), d)
        if d == ctxs - 2:
            down_sum = LineSum(order, down_part(0, down_got))
            (first_gq,) = order(
                lambda *a: whole(first_gq_kernel, [((rows, width), f32)], *a),
                place,
                d_gq,
                gate_w,
                query_w,
            )
    gate_sum = LineSum(order, gateup_part(d_gate, 0, gate_got))
    (output,) = order(
        lambda *a: whole(leave_kernel, [((half, width), bf16)], *a), middle, *mlp_total
    )
    output_too = partner(output, "tp", 1)
    base, messages, d_alpha, d_gain_k, d_forget_own = order(
        lambda *a: shift_back(a, rows, local, heads_up, ctxs, size),
        d_kv[0],
        coming,
        raw_kv,
        delta,
        lin,
        gain_k,
        start,
        parent,
        dcq,
        dck,
        key_onehot,
    )
    returned = [along(m, "ctx", -d - 1) for d, m in enumerate(messages)]
    down_sum.step()
    (output,) = order(
        lambda *a: whole(named(settle_kernel, shards=shards), [((rows, width), bf16)], *a),
        place,
        output,
        output_too,
    )
    d_raw_kv, d_lin, d_bias = order(
        lambda *a: whole(
            raw_back_kernel,
            [((2, rows, local), bf16), ((3 * heads_up, rows), bf16), ((heads_up, 1), f32)],
            *a,
        ),
        base,
        messages[0],
        returned,
        ends,
        bias,
        onehot,
        anc,
        lin,
        d_forget_own,
        d_alpha,
    )
    kv_all = gathered(d_raw_kv)

    def first_share(which, kind):
        return lambda *a: whole(
            named(first_share_kernel_of(part, rows), which=which), [((half, width), kind)], *a
        )[0]

    share = order(first_share(1, f32), place, d_raw_kv, d_lin, kv_w, packs, first_gq)
    given = partner(share, "tp", 1)
    mine = order(first_share(0, f32), place, d_raw_kv, d_lin, kv_w, packs, first_gq)
    (total,) = order(
        lambda *a: whole(first_sum_kernel, [((half, width), bf16)], *a), mine, given
    )
    first_total = crossed(total)
    gate_sum.step()
    up_sum = LineSum(order, gateup_part(d_up, 0, up_got))
    kv_sums = []
    for i in range(2):
        pairs = [
            (At(f, cols=(0, part)), At(g, lead=i)) for f, g in zip(first_parts, kv_all)
        ]
        kv_sums.append(LineSum(order, weight_grad(order, pairs, (), min(256, part))))
    d_own, d_gain_one = order(
        lambda *a: whole(
            enter_back_kernel, [((half, width), f32), ((1, width), f32)], *a
        ),
        place,
        tree,
        packs,
        d_middle,
        *first_total,
    )
    d_own_too = partner(d_own, "tp", 1)
    d_gains = jnp.concatenate([d_gain_one, d_gain_two], axis=0)
    d_gains_too = partner(d_gains, "tp", 1)
    down_sum.step()
    gate_sum.step()
    up_sum.step()
    (d_tokens,) = order(
        lambda *a: whole(named(settle_kernel, shards=shards), [((rows, width), f32)], *a),
        place,
        d_own,
        d_own_too,
    )
    smalls = order(
        lambda *a: whole(
            small_kernel, [((40, max(part, local)), f32) for _ in range(shards)], *a
        ),
        d_lin,
        first_in,
        d_gains,
        d_gains_too,
        d_gain_q,
        d_gain_k,
        d_bias,
    )
    small_got = [
        from_ring(smalls[d], "shard", shards - d) for d in range(1, shards)
    ]
    for k in kv_sums:
        k.step()
    small = smalls[0]
    for got in small_got:
        small = order(add_rows, small, got)
    small_sum = LineSum(order, small)
    pairs = [(At(f, cols=(0, part)), At(g)) for f, g in zip(first_parts, gq_all)]
    gq_sum = LineSum(order, weight_grad(order, pairs, (), min(256, part)))
    out_sum = LineSum(order, out_part(0, out_got))
    sums = [down_sum, gate_sum, up_sum] + kv_sums + [small_sum, gq_sum, out_sum]
    for hop in range(2 * (ctxs // 2) - 1):
        for s in sums:
            if s.hop == hop:
                s.step()
    small = small_sum.total
    d_gq_w = gq_sum.total.astype(f32)
    return (
        settled(output)[None],
        settled(d_tokens)[None],
        small[24:26, :part],
        jnp.stack(
            [
                d_gq_w[:, local:],
                kv_sums[0].total.astype(f32),
                kv_sums[1].total.astype(f32),
                d_gq_w[:, :local],
            ],
            axis=1,
        ),
        jnp.transpose(
            small[: 3 * heads_up, :part].reshape(3, heads_up, part)[:, :heads], (2, 0, 1)
        ),
        small[32 : 32 + heads, 0],
        small[26:28, :local],
        out_sum.total.astype(f32),
        jnp.stack([gate_sum.total.astype(f32), up_sum.total.astype(f32)], axis=1),
        down_sum.total.astype(f32),
    )


def shift_back(args, rows, local, heads_up, ctxs, size):
    edge = (segs_up + heads_up, 2 * local)
    count = ctxs - 1

    def shift_back_all_kernel(*refs):
        ins, outs = refs[:11], refs[11:]
        shift_back_kernel(
            *ins, outs[0], outs[1 : 1 + count], *outs[1 + count :], size=size
        )

    outs = whole(
        shift_back_all_kernel,
        [((2, rows, local), f32)]
        + [(edge, f32)] * count
        + [((2 * heads_up, rows), f32), ((1, local), f32), ((heads_up, rows), f32)],
        *args,
    )
    return outs[0], list(outs[1 : 1 + count]), *outs[1 + count :]


def first_share_kernel_of(part, rows):
    def first_share_scoped_kernel(*refs, which):
        pl.run_scoped(
            lambda scratch: first_share_kernel(*refs, scratch, which=which),
            pltpu.VMEM((rows, part), f32),
        )

    return first_share_scoped_kernel


def solution(mesh):
    in_specs = (
        P("shard", "ctx", None),
        P("shard", None),
        P("shard", None),
        P("shard", "ctx"),
        P(None, "shard"),
        P("shard", None, "tp"),
        P("shard", None, "tp"),
        P("tp"),
        P(None, "tp"),
        P("tp", "shard"),
        P("shard", None, "tp"),
        P("tp", "shard"),
        P("shard", "ctx", None),
    )
    out_specs = (
        P("shard", "ctx", None),
        P("shard", "ctx", None),
        P(None, "shard"),
        P("shard", None, "tp"),
        P("shard", None, "tp"),
        P("tp"),
        P(None, "tp"),
        P("tp", "shard"),
        P("shard", None, "tp"),
        P("tp", "shard"),
    )
    return jax.shard_map(body, mesh=mesh, in_specs=in_specs, out_specs=out_specs, check_vma=False)
```

```python
import functools

import jax
import jax.numpy as jnp
from jax import lax
from jax.experimental import pallas as pl
from jax.experimental.pallas import tpu as pltpu
from jax.sharding import PartitionSpec as P

epsilon = 1e-06
neg_large = -1e30
highest = lax.Precision.HIGHEST
f32 = jnp.float32
bf16 = jnp.bfloat16
segs_up = 16


def from_ring(values, axis, step):
    count = lax.axis_size(axis)
    return lax.ppermute(values, axis, [((i + step) % count, i) for i in range(count)])


def along(values, axis, step):
    count = lax.axis_size(axis)
    return lax.ppermute(
        values, axis, [(i, i + step) for i in range(count) if 0 <= i + step < count]
    )


def partner(values, axis, bit):
    count = lax.axis_size(axis)
    return lax.ppermute(values, axis, [(i, i ^ bit) for i in range(count)])


def dot_of(dims, precision=None):
    def product(left, right):
        return lax.dot_general(
            left, right, (dims, ((), ())), precision=precision, preferred_element_type=f32
        )

    return product


mm = dot_of(((1,), (0,)))
mm_nt = dot_of(((1,), (1,)))
mm_tn = dot_of(((0,), (0,)))
exact = dot_of(((1,), (0,)), highest)
exact_nt = dot_of(((1,), (1,)), highest)
exact_tn = dot_of(((0,), (0,)), highest)


def rms_scale(values):
    return lax.rsqrt(jnp.mean(values * values, axis=-1, keepdims=True) + epsilon)


def norm_grad(values, scale, gain_row, d_result):
    normed = values * scale
    d_normed = d_result * gain_row
    d_values = scale * (d_normed - normed * jnp.mean(d_normed * normed, axis=-1, keepdims=True))
    return d_values, jnp.sum(d_result * normed, axis=0, keepdims=True)


def iota(shape, axis):
    return lax.broadcasted_iota(jnp.int32, shape, axis)


def same_head(width, size):
    return jnp.where(iota((width, width), 0) // size == iota((width, width), 1) // size, 1.0, 0.0)


def head_mean(values, size):
    return exact(values, same_head(values.shape[1], size)) * (1.0 / size)


def head_scale(values, size):
    return lax.rsqrt(head_mean(values * values, size) + epsilon)


def head_grad(values, gain_row, d_result, size):
    scale = head_scale(values, size)
    normed = values * scale
    d_normed = d_result * gain_row
    d_values = scale * (d_normed - normed * head_mean(d_normed * normed, size))
    return d_values, jnp.sum(d_result * normed, axis=0, keepdims=True)


def spread_of(heads_up, width, size):
    return jnp.where(iota((heads_up, width), 0) == iota((heads_up, width), 1) // size, 1.0, 0.0)


def nbytes(leaf):
    return leaf.size * leaf.dtype.itemsize


def whole(kernel, outs, *args, extra=8):
    leaves, form = jax.tree.flatten(args)

    def flat(*refs):
        kernel(*jax.tree.unflatten(form, refs[: len(leaves)]), *refs[len(leaves) :])

    shapes = [jax.ShapeDtypeStruct(shape, kind) for shape, kind in outs]
    spaces = [
        pltpu.SMEM if leaf.ndim == 1 and leaf.dtype == jnp.int32 else pltpu.VMEM
        for leaf in leaves
    ]
    size = sum(nbytes(x) for x in leaves) + sum(nbytes(x) for x in shapes)
    found = pl.pallas_call(
        flat,
        out_shape=shapes,
        in_specs=[pl.BlockSpec(memory_space=s) for s in spaces],
        out_specs=[pl.BlockSpec(memory_space=pltpu.VMEM) for _ in shapes],
        compiler_params=pltpu.CompilerParams(
            vmem_limit_bytes=min(60 << 20, size + size // 4 + (extra << 20))
        ),
        cost_estimate=pl.CostEstimate(flops=1, transcendentals=1, bytes_accessed=1),
        name=kernel.__name__,
    )(*leaves)
    return found


def masks_kernel(place, low, high, high_col, parents_col, seg_col, bias, seen, key_anc, onehot, parent, start, ends, anc, key_onehot):
    rows = seg_col.shape[0]
    ctx = place[2]
    lanes = iota((segs_up, segs_up), 1)
    parent_mat = jnp.where(parents_col[...] == lanes, 1.0, 0.0)
    eye = jnp.where(iota((segs_up, segs_up), 0) == lanes, 1.0, 0.0)
    ancestry = eye + parent_mat + exact(parent_mat, parent_mat)
    anc[...] = ancestry
    mine = jnp.where(seg_col[...] == iota((rows, segs_up), 1), 1.0, 0.0)
    onehot[...] = mine
    parent[...] = exact(mine, parent_mat)
    mine_anc = exact(mine, ancestry)
    query_pos = ctx * rows + iota((1, rows), 1)
    query_col = ctx * rows + iota((rows, 1), 0)
    ends[...] = jnp.where(query_pos == high_col[...] - 1, 1.0, 0.0)
    start[...] = jnp.sum(
        jnp.where(query_col == low[...], 1.0, 0.0), axis=1, keepdims=True
    )
    for d in range(bias.shape[0] // rows):
        span = slice(d * rows, (d + 1) * rows)
        key_pos = (ctx - d) * rows + iota((rows, 1), 0)
        keys = jnp.where((key_pos >= low[...]) & (key_pos < high[...]), 1.0, 0.0)
        key_anc[span, :] = exact(keys, ancestry)
        key_onehot[span, :] = keys
        linked = mm_nt(keys.astype(bf16), mine_anc.astype(bf16)) > 0.5
        visible = linked & (key_pos <= query_pos)
        bias[span, :] = jnp.where(visible, 0.0, neg_large)
        if d == 0:
            seen[...] = jnp.where(visible, 1.0, 0.0)


def turned(values, first, count):
    width = values.shape[1] // count
    pieces = [
        lax.dynamic_slice_in_dim(values, lax.rem(first + i, count) * width, width, 1)
        for i in range(count)
    ]
    return jnp.concatenate(pieces, axis=1)


def part_at(ref, shard, d, shards, rows=slice(None)):
    part = ref.shape[1] // shards
    if part % 128:
        return ref[rows, d * part : (d + 1) * part]
    start = pl.multiple_of(lax.rem(shard + d, shards) * part, 128)
    return ref[rows, pl.ds(start, part)]


def enter_kernel(place, tokens, packs, first_in):
    shards = len(packs)
    part = packs[0].shape[1]
    pieces = [part_at(tokens, place[1], d, shards).astype(f32) for d in range(shards)]
    mean = sum(jnp.sum(x * x, axis=1, keepdims=True) for x in pieces) * (
        1.0 / tokens.shape[1]
    )
    scale = lax.rsqrt(mean + epsilon)
    for d in range(shards):
        gain = packs[d][24:25, :].astype(f32)
        first_in[:, d * part : (d + 1) * part] = (pieces[d] * scale * gain).astype(bf16)


def keys_in_kernel(first_in, kv_w, packs, forget_bias, seen, onehot, ends, raw_kv, lin, message):
    part = packs[0].shape[1]
    rows = first_in.shape[0]
    local = raw_kv.shape[2]
    heads_up = forget_bias.shape[0]
    cuts = [first_in[:, d * part : (d + 1) * part] for d in range(len(packs))]
    head_lin = sum(mm_nt(p[:24, :], x) for p, x in zip(packs, cuts))
    forget_in = head_lin[:heads_up] + forget_bias[...]
    lin[...] = head_lin
    lin[:heads_up, :] = forget_in
    log_forget = jnp.minimum(forget_in, 0.0) - jnp.log1p(jnp.exp(-jnp.abs(forget_in)))
    message[...] = jnp.zeros_like(message)
    for i in range(2):
        raw = sum(mm(x, w[i]) for w, x in zip(kv_w, cuts))
        raw_kv[i] = raw
        cols = slice(i * local, (i + 1) * local)
        message[:segs_up, cols] = exact(ends[...], raw)
        message[segs_up - 1 : segs_up, cols] = raw[rows - 1 :]
    message[segs_up : segs_up + heads_up, :rows] = exact(log_forget, seen[...])
    message[segs_up : segs_up + heads_up, local : local + segs_up] = exact(
        log_forget, onehot[...]
    )


def keys_shift_kernel(raw_kv, lin, blocks, parent, start, key_anc, gain, own_kv, delta, fq, fk, *, size):
    rows, local = raw_kv.shape[1:]
    heads_up = lin.shape[0] // 3
    spread = spread_of(heads_up, local, size)
    seg_ends = sum((b[:segs_up, :] for b in blocks[1:]), blocks[0][:segs_up, :])
    at_start = start[...] > 0.5
    at_top = iota((rows, 1), 0) == 0
    for i in range(2):
        cols = slice(i * local, (i + 1) * local)
        alpha_rows = jax.nn.sigmoid(lin[(i + 1) * heads_up : (i + 2) * heads_up, :])
        alpha = exact_tn(alpha_rows, spread)
        raw = raw_kv[i]
        previous = jnp.where(
            at_top, blocks[1][segs_up - 1 : segs_up, cols], pltpu.roll(raw, 1, 0)
        )
        previous = jnp.where(at_start, exact(parent[...], seg_ends[:, cols]), previous)
        step = previous - raw
        delta[i] = step
        shifted = raw + alpha * step
        if i == 0:
            shifted = shifted * head_scale(shifted, size) * gain[...]
        own_kv[i] = shifted.astype(bf16)
    table = slice(segs_up, segs_up + heads_up)
    for d in range(len(blocks)):
        sums = blocks[d][table, :rows]
        span = slice(d * rows, (d + 1) * rows)
        later = blocks[d + 1 :]
        if later:
            before = sum(
                (b[table, local : local + segs_up] for b in later[1:]),
                later[0][table, local : local + segs_up],
            )
            sums = sums + exact_nt(before, key_anc[span, :])
        for h in range(2 * fk.shape[0]):
            fk[h // 2, h % 2 : h % 2 + 1, span] = sums[h : h + 1]
            if d == 0:
                fq[h // 2, h % 2 : h % 2 + 1, :] = sums[h : h + 1]


def queries_kernel(first_in, bundles, gain, raw_q, query, raw_g, *, size):
    part = bundles[0].shape[1]
    cuts = [first_in[:, d * part : (d + 1) * part] for d in range(len(bundles))]
    raw = sum(mm(x, w[0]) for w, x in zip(bundles, cuts))
    raw_q[...] = raw
    raw_g[...] = sum(mm(x, w[1]) for w, x in zip(bundles, cuts))
    normed = (raw * head_scale(raw, size) * gain[...]).astype(bf16)
    query[...] = (normed.astype(f32) * (size**-0.5)).astype(bf16)


def attn_share_kernel(values, bundles, out):
    half = out.shape[0]
    part = bundles[0].shape[1]
    for d, w in enumerate(bundles):
        out[:, d * part : (d + 1) * part] = mm_nt(values[half:, :], w[2])


def attn_share_sum_kernel(values, bundles, given, out):
    half = out.shape[0]
    part = bundles[0].shape[1]
    for d, w in enumerate(bundles):
        cols = slice(d * part, (d + 1) * part)
        out[:, cols] = (mm_nt(values[:half, :], w[2]) + given[:, cols]).astype(bf16)


def share_kernel(values, weights, out, *, which):
    half = out.shape[0]
    part = out.shape[1] // len(weights)
    rows = slice(which * half, (which + 1) * half)
    for d, w in enumerate(weights):
        out[:, d * part : (d + 1) * part] = mm(values[rows, :], w[...])


def share_sum_kernel(values, weights, given, out):
    half = out.shape[0]
    part = out.shape[1] // len(weights)
    for d, w in enumerate(weights):
        cols = slice(d * part, (d + 1) * part)
        out[:, cols] = (mm(values[:half, :], w[...]) + given[:, cols]).astype(bf16)


def middle_kernel(place, tokens, packs, total, other, middle, second_in):
    shards = len(packs)
    part = packs[0].shape[1]
    half = total.shape[0]
    rows = pl.ds(pl.multiple_of(place[0] * half, 16), half)
    square = jnp.zeros((half, 1), f32)
    for d in range(shards):
        cols = slice(d * part, (d + 1) * part)
        value = part_at(tokens, place[1], d, shards, rows).astype(f32) + (
            total[:, cols].astype(f32) + other[:, cols].astype(f32)
        )
        middle[:, cols] = value
        square = square + jnp.sum(value * value, axis=1, keepdims=True)
    scale = lax.rsqrt(square * (1.0 / middle.shape[1]) + epsilon)
    for d in range(shards):
        cols = slice(d * part, (d + 1) * part)
        gain = packs[d][25:26, :].astype(f32)
        second_in[:, cols] = (middle[:, cols] * scale * gain).astype(bf16)


def grad_hidden_kernel(place, cotangent, down_w, grad_out, d_hidden):
    shards = len(down_w)
    part = down_w[0].shape[1]
    half = cotangent.shape[0] // 2
    for k in range(2):
        rows = pl.ds(pl.multiple_of(lax.rem(place[0] + k, 2) * half, 16), half)
        span = slice(k * half, (k + 1) * half)
        for d in range(shards):
            grad_out[span, d * part : (d + 1) * part] = part_at(
                cotangent, place[1], d, shards, rows
            )
    d_hidden[...] = sum(
        mm_nt(grad_out[:, d * part : (d + 1) * part], w[...]) for d, w in enumerate(down_w)
    )


def mlp_kernel(*refs):
    mine, theirs = refs[:2]
    weights = refs[2:-3]
    d_hidden, hidden, d_lin = refs[-3:]
    part = weights[0].shape[1]
    half = mine.shape[0]
    for k, second in enumerate((mine, theirs)):
        rows = slice(k * half, (k + 1) * half)
        lin = [
            sum(mm(second[:, d * part : (d + 1) * part], w[i]) for d, w in enumerate(weights))
            for i in range(2)
        ]
        sig = jax.nn.sigmoid(lin[0])
        silu = lin[0] * sig
        grad = d_hidden[rows, :]
        hidden[rows, :] = (silu * lin[1]).astype(bf16)
        d_lin[0, rows, :] = (grad * lin[1] * (sig * (1.0 + lin[0] * (1.0 - sig)))).astype(bf16)
        d_lin[1, rows, :] = (grad * silu).astype(bf16)


def mlp(mine, theirs, weights, d_hidden):
    half, width = mine.shape
    rows, hidden_size = d_hidden.shape
    part = weights[0].shape[1]
    block = 256
    flat = pl.BlockSpec((half, width), lambda j: (0, 0))
    return pl.pallas_call(
        mlp_kernel,
        grid=(hidden_size // block,),
        in_specs=[flat, flat]
        + [pl.BlockSpec((2, part, block), lambda j: (0, 0, j)) for _ in weights]
        + [pl.BlockSpec((rows, block), lambda j: (0, j))],
        out_specs=[
            pl.BlockSpec((rows, block), lambda j: (0, j)),
            pl.BlockSpec((2, rows, block), lambda j: (0, 0, j)),
        ],
        out_shape=[
            jax.ShapeDtypeStruct((rows, hidden_size), bf16),
            jax.ShapeDtypeStruct((2, rows, hidden_size), bf16),
        ],
        compiler_params=pltpu.CompilerParams(vmem_limit_bytes=24 << 20),
        cost_estimate=pl.CostEstimate(flops=1, transcendentals=1, bytes_accessed=1),
        name="mlp",
    )(mine, theirs, *weights, d_hidden)


def back_share_kernel(*refs):
    count = refs[-1].shape[0]
    d_lin, weights, given, out = refs[0], refs[1 : 1 + count], refs[1 + count : -1], refs[-1]
    for d, w in enumerate(weights):
        share = mm_nt(d_lin[0], w[0]) + mm_nt(d_lin[1], w[1])
        if given:
            share = share + given[0][d]
        out[d] = share.astype(out.dtype)


def back_share(d_lin, weights, which, given=None):
    rows, hidden_size = d_lin.shape[1:]
    half = rows // 2
    shards = len(weights)
    part = weights[0].shape[1]
    block = 256 if part % 256 == 0 else part
    over = pl.BlockSpec((shards, half, block), lambda j: (0, 0, j))
    extra = [] if given is None else [given]
    return pl.pallas_call(
        back_share_kernel,
        grid=(part // block,),
        in_specs=[pl.BlockSpec((2, half, hidden_size), lambda j: (0, which, 0))]
        + [pl.BlockSpec((2, block, hidden_size), lambda j: (0, j, 0)) for _ in weights]
        + [over for _ in extra],
        out_specs=over,
        out_shape=jax.ShapeDtypeStruct((shards, half, part), bf16 if extra else f32),
        compiler_params=pltpu.CompilerParams(vmem_limit_bytes=24 << 20),
        cost_estimate=pl.CostEstimate(flops=1, transcendentals=1, bytes_accessed=1),
        name="back_share",
    )(d_lin, *weights, *extra)


def gain_row(packs, row):
    return jnp.concatenate([p[row : row + 1, :].astype(f32) for p in packs], axis=1)


def middle_back_kernel(grad_out, packs, middle, total, other, d_middle, d_middle_b, d_gain):
    half = middle.shape[0]
    value = middle[...]
    d_second = jnp.concatenate(
        [total[d].astype(f32) + other[d].astype(f32) for d in range(total.shape[0])], axis=1
    )
    d_value, gain = norm_grad(value, rms_scale(value), gain_row(packs, 25), d_second)
    d_gain[...] = gain
    d_value = d_value + grad_out[:half, :].astype(f32)
    d_middle[...] = d_value
    d_middle_b[...] = d_value.astype(bf16)


def gate_back_kernel(place, mine, theirs, bundles, raw_g, attended, d_attended, d_raw_g):
    half = mine.shape[0]
    part = bundles[0].shape[1]
    for k, source in enumerate((mine, theirs)):
        rows = pl.ds(pl.multiple_of(lax.rem(place[0] + k, 2) * half, 16), half)
        d_gated = sum(
            mm(source[:, d * part : (d + 1) * part], w[2]) for d, w in enumerate(bundles)
        )
        sig = jax.nn.sigmoid(raw_g[rows, :])
        d_attended[rows, :] = (d_gated * sig).astype(bf16)
        d_raw_g[rows, :] = (d_gated * attended[rows, :] * sig * (1.0 - sig)).astype(bf16)


def query_back_kernel(raw_q, d_query, gain, d_raw_g, d_gq, d_gain, *, size):
    local = raw_q.shape[1]
    d_raw, gain_grad = head_grad(raw_q[...], gain[...], d_query[...], size)
    d_gain[...] = gain_grad
    d_gq[:, :local] = d_raw_g[...]
    d_gq[:, local:] = d_raw.astype(bf16)


def chain_kernel(partial, got, out):
    out[...] = (partial[...].astype(f32) + got[...].astype(f32)).astype(out.dtype)


def shift_back_kernel(
    d_kv, got, raw_kv, delta, lin, gain, start, parent, dcq, dck, key_onehots,
    base, messages, d_alpha, d_gain, d_forget_own, *, size,
):
    rows, local = raw_kv.shape[1:]
    heads_up = lin.shape[0] // 3
    heads = 2 * dcq.shape[0]
    spread = spread_of(heads_up, local, size)
    not_start = 1.0 - start[...]
    start_parent = parent[...] * start[...]
    for m in messages:
        m[...] = jnp.zeros_like(m)
    for i in range(2):
        cols = slice(i * local, (i + 1) * local)
        alpha_rows = jax.nn.sigmoid(lin[(i + 1) * heads_up : (i + 2) * heads_up, :])
        alpha = exact_tn(alpha_rows, spread)
        d_shift = d_kv[i] + got[i].astype(f32)
        if i == 0:
            shifted = raw_kv[0] + alpha * delta[0]
            d_shift, gain_grad = head_grad(shifted, gain[...], d_shift, size)
            d_gain[...] = gain_grad
        d_alpha[i * heads_up : (i + 1) * heads_up, :] = (
            exact_nt(spread, d_shift * delta[i]) * alpha_rows * (1.0 - alpha_rows)
        )
        d_prev = alpha * d_shift
        d_step = d_prev * not_start
        base[i] = (
            d_shift
            - d_prev
            + jnp.where(iota((rows, 1), 0) == rows - 1, 0.0, pltpu.roll(d_step, rows - 1, 0))
        )
        table = exact_tn(start_parent, d_prev)
        for m in messages:
            m[:segs_up, cols] = table
            m[segs_up - 1 : segs_up, cols] = d_step[:1]
    later = jnp.zeros((heads_up, segs_up), f32)
    blank = jnp.zeros((heads_up - heads, rows), f32)
    for d in range(len(messages) + 1):
        span = slice(d * rows, (d + 1) * rows)
        grads = jnp.concatenate(
            [-dck[h // 2, h % 2 : h % 2 + 1, span] for h in range(heads)] + [blank], axis=0
        )
        if d == 0:
            grads = grads + jnp.concatenate(
                [dcq[h // 2, h % 2 : h % 2 + 1, :] for h in range(heads)] + [blank], axis=0
            )
            d_forget_own[...] = grads
        else:
            messages[d - 1][segs_up : segs_up + heads_up, :rows] = grads
            messages[d - 1][segs_up : segs_up + heads_up, local : local + segs_up] = later
        if d < len(messages):
            later = later + exact(grads, key_onehots[span, :])


def raw_back_kernel(
    base, table_own, returned, ends, seen, onehot, anc, lin, d_forget_own, d_alpha,
    d_raw_kv, d_lin, d_bias,
):
    rows, local = base.shape[1:]
    heads_up = lin.shape[0] // 3
    tail = slice(segs_up, segs_up + heads_up)
    for i in range(2):
        cols = slice(i * local, (i + 1) * local)
        table = table_own[:segs_up, cols]
        for r in returned:
            table = table + r[:segs_up, cols]
        edge = jnp.where(
            iota((rows, 1), 0) == rows - 1, returned[0][segs_up - 1 : segs_up, cols], 0.0
        )
        d_raw_kv[i] = (base[i] + edge + exact_tn(ends[...], table)).astype(bf16)
    own = d_forget_own[...]
    sums = jnp.zeros((heads_up, segs_up), f32)
    for r in returned:
        own = own + r[tail, :rows]
        sums = sums + r[tail, local : local + segs_up]
    d_log = exact_nt(own, seen[...]) + exact_nt(exact(sums, anc[...]), onehot[...])
    d_forget = d_log * jax.nn.sigmoid(-lin[:heads_up, :])
    d_bias[...] = jnp.sum(d_forget, axis=1, keepdims=True)
    d_lin[:heads_up, :] = d_forget.astype(bf16)
    d_lin[heads_up:, :] = d_alpha[...].astype(bf16)


def first_gq_kernel(place, d_gq, bundles, out):
    half = d_gq.shape[0] // 2
    part = bundles[0].shape[1]
    local = d_gq.shape[1] // 2
    for k in range(2):
        rows = pl.ds(pl.multiple_of(lax.rem(place[0] + k, 2) * half, 16), half)
        for d, w in enumerate(bundles):
            out[k * half : (k + 1) * half, d * part : (d + 1) * part] = mm_nt(
                d_gq[rows, :local], w[1]
            ) + mm_nt(d_gq[rows, local:], w[0])


def first_share_kernel(place, d_kv, d_lin, kv_w, packs, partial, out, heads_part, *, which):
    half = out.shape[0]
    part = packs[0].shape[1]
    rows = pl.ds(pl.multiple_of(lax.rem(place[0] + which, 2) * half, 16), half)
    for d in range(len(packs)):
        cols = slice(d * part, (d + 1) * part)
        heads_part[...] = mm_tn(d_lin[...], packs[d][:24, :])
        out[:, cols] = (
            mm_nt(d_kv[0, rows, :], kv_w[d][0])
            + mm_nt(d_kv[1, rows, :], kv_w[d][1])
            + heads_part[rows, :]
            + partial[which * half : (which + 1) * half, cols]
        ).astype(out.dtype)


def first_sum_kernel(mine, given, out):
    out[...] = (mine[...] + given[...]).astype(bf16)


def enter_back_kernel(place, tokens, packs, d_middle, total, other, d_own, d_gain):
    shards = len(packs)
    half = total.shape[0]
    rows = pl.ds(pl.multiple_of(place[0] * half, 16), half)
    value = jnp.concatenate(
        [part_at(tokens, place[1], d, shards, rows).astype(f32) for d in range(shards)], axis=1
    )
    d_first = total[...].astype(f32) + other[...].astype(f32)
    d_value, gain = norm_grad(value, rms_scale(value), gain_row(packs, 24), d_first)
    d_gain[...] = gain
    d_own[...] = d_middle[...] + d_value


def settle_kernel(place, mine, theirs, out, *, shards):
    half = mine.shape[0]
    part = mine.shape[1] // shards
    for k, source in enumerate((mine, theirs)):
        rows = pl.ds(pl.multiple_of(lax.rem(place[0] + k, 2) * half, 16), half)
        for d in range(shards):
            cols = slice(d * part, (d + 1) * part)
            if part % 128:
                out[rows, cols] = source[:, cols]
            else:
                start = pl.multiple_of(lax.rem(place[1] + d, shards) * part, 128)
                out[rows, pl.ds(start, part)] = source[:, cols]


def leave_kernel(middle, total, other, out):
    out[...] = (
        middle[...] + (total[...].astype(f32) + other[...].astype(f32))
    ).astype(bf16)


def named(kernel, **fixed):
    def bound(*refs):
        kernel(*refs, **fixed)

    bound.__name__ = kernel.__name__
    return bound


class At:

    def __init__(self, array, rows=None, cols=None, lead=None):
        if cols and (cols[0] % 128 or cols[1] % 128):
            array, cols = array[..., cols[0] : cols[1]], None
        self.array, self.lead = array, lead
        self.rows = rows or (0, array.shape[-2])
        self.cols = cols or (0, array.shape[-1])

    def spec(self, block=None):
        start, stop = self.rows
        height = stop - start
        first, last = self.cols
        wide = block or last - first
        shape, row, col = (height, wide), start // height, first // wide

        def at(j):
            return (row, col + j if block else col)

        if self.lead is None:
            return pl.BlockSpec(shape, at)
        return pl.BlockSpec((None,) + shape, lambda j: (self.lead,) + at(j))


def weight_grad(order, pairs, got, block):
    count = len(pairs)
    rows = pairs[0][0].cols[1] - pairs[0][0].cols[0]
    width = pairs[0][1].cols[1] - pairs[0][1].cols[0]

    def weight_grad_kernel(*refs):
        total = mm_tn(refs[0][...], refs[1][...])
        for i in range(1, count):
            total = total + mm_tn(refs[2 * i][...], refs[2 * i + 1][...])
        for ref in refs[2 * count : -1]:
            total = total + ref[...].astype(f32)
        refs[-1][...] = total.astype(bf16)

    specs = [spec for a, b in pairs for spec in (a.spec(block), b.spec())]
    over = pl.BlockSpec((block, width), lambda j: (j, 0))
    call = pl.pallas_call(
        weight_grad_kernel,
        grid=(rows // block,),
        in_specs=specs + [over for _ in got],
        out_specs=over,
        out_shape=jax.ShapeDtypeStruct((rows, width), bf16),
        compiler_params=pltpu.CompilerParams(vmem_limit_bytes=20 << 20),
        cost_estimate=pl.CostEstimate(flops=1, transcendentals=1, bytes_accessed=1),
        name="weight_grad",
    )
    return order(call, *[x.array for pair in pairs for x in pair], *got)


def add_rows(left, right):
    rows, width = left.shape
    block = rows if rows % 64 else 64 if rows <= 256 else 128

    def add_kernel(left, right, out):
        out[...] = (left[...].astype(f32) + right[...].astype(f32)).astype(out.dtype)

    over = pl.BlockSpec((block, width), lambda j: (j, 0))
    return pl.pallas_call(
        add_kernel,
        grid=(rows // block,),
        in_specs=[over, over],
        out_specs=over,
        out_shape=jax.ShapeDtypeStruct((rows, width), left.dtype),
        compiler_params=pltpu.CompilerParams(vmem_limit_bytes=8 << 20),
        cost_estimate=pl.CostEstimate(flops=1, transcendentals=1, bytes_accessed=1),
        name="add",
    )(left, right)


def attend_kernel(*refs):
    place, query_ref, *kv_refs, bias_ref, cq_ref, ck_ref, gate_ref, out_ref, gated_ref, lse_ref = refs
    rows = query_ref.shape[0]
    half = rows // 2
    size = query_ref.shape[1] // 2
    key_cols = ck_ref[0].T
    outs = []
    for e in range(2):
        cols = slice(e * size, (e + 1) * size)
        query = query_ref[:, cols]
        forget_row = cq_ref[0, e : e + 1, :]
        total = jnp.zeros((1, rows), f32)
        mixed = jnp.zeros((size, rows), f32)
        for d in range(len(kv_refs) // 2):
            span = slice(d * rows, (d + 1) * rows)
            scores = mm_nt(kv_refs[2 * d][0, :, cols], query)
            scores = scores + (forget_row - key_cols[span, e : e + 1]) + bias_ref[span, :]
            weights = jnp.exp(scores)
            total = total + jnp.sum(weights, axis=0, keepdims=True)
            mixed = mixed + mm_tn(kv_refs[2 * d + 1][0, :, cols], weights.astype(bf16))
        outs.append((mixed / total).T)
        lse_ref[0, e : e + 1, :] = jnp.log(total)
    attended = jnp.concatenate(outs, axis=1)
    out_ref[...] = attended
    gated = (attended * jax.nn.sigmoid(gate_ref[...])).astype(bf16)
    for k in range(2):
        there = pl.ds(pl.multiple_of(lax.rem(place[0] + k, 2) * half, 16), half)
        gated_ref[there, :] = gated[k * half : (k + 1) * half]


def attend_back_kernel(*refs):
    count = (len(refs) - 10) // 3
    query_ref, d_out_ref = refs[:2]
    kv_refs = refs[2 : 2 + 2 * count]
    bias_ref, cq_ref, ck_ref, lse_ref = refs[2 + 2 * count : 6 + 2 * count]
    d_query_ref = refs[6 + 2 * count]
    d_kv_refs = refs[7 + 2 * count : 7 + 3 * count]
    dcq_ref, dck_ref, prob_ref, d_prob_ref = refs[7 + 3 * count :]
    rows = query_ref.shape[0]
    size = query_ref.shape[1] // 2
    key_cols = ck_ref[0].T
    ones = jnp.ones((8, rows), bf16)
    for e in range(2):
        cols = slice(e * size, (e + 1) * size)
        query = query_ref[:, cols]
        d_out = d_out_ref[:, cols]
        forget_row = cq_ref[0, e : e + 1, :] - lse_ref[0, e : e + 1, :]
        delta = jnp.zeros((1, rows), f32)
        for d in range(count):
            span = slice(d * rows, (d + 1) * rows)
            scores = mm_nt(kv_refs[2 * d][0, :, cols], query)
            scores = scores + (forget_row - key_cols[span, e : e + 1]) + bias_ref[span, :]
            probs = jnp.exp(scores)
            d_probs = mm_nt(kv_refs[2 * d + 1][0, :, cols], d_out)
            delta = delta + jnp.sum(probs * d_probs, axis=0, keepdims=True)
            prob_ref[span, :] = probs
            d_prob_ref[span, :] = d_probs
        d_query = jnp.zeros((size, rows), f32)
        d_row = jnp.zeros((1, rows), f32)
        for d in range(count):
            span = slice(d * rows, (d + 1) * rows)
            probs = prob_ref[span, :]
            d_scores = (probs * (d_prob_ref[span, :] - delta)).astype(bf16)
            d_kv_refs[d][0, :, cols] = mm(d_scores, query).astype(d_kv_refs[d].dtype)
            d_kv_refs[d][1, :, cols] = mm(probs.astype(bf16), d_out).astype(d_kv_refs[d].dtype)
            d_query = d_query + mm_tn(kv_refs[2 * d][0, :, cols], d_scores)
            d_row = d_row + jnp.sum(d_scores.astype(f32), axis=0, keepdims=True)
            dck_ref[0, e : e + 1, span] = mm_nt(ones, d_scores)[:1]
        d_query_ref[:, cols] = d_query.T * (size ** (-0.5))
        dcq_ref[0, e : e + 1, :] = d_row


def kv_specs(blocks, lanes):
    rows = blocks[0].shape[1]
    return [
        pl.BlockSpec((1, rows, lanes), lambda p, kind=kind: (kind, 0, p))
        for _ in blocks
        for kind in range(2)
    ]


def twice(blocks):
    return [b for b in blocks for _ in range(2)]


def attention(place, query, kv_blocks, bias, forget_q, forget_k, raw_g):
    rows, local = query.shape
    pairs = forget_q.shape[0]
    keys = bias.shape[0]
    lanes = local // pairs
    flat = pl.BlockSpec((rows, lanes), lambda p: (0, p))
    row_spec = pl.BlockSpec((1, 8, rows), lambda p: (p, 0, 0))
    return pl.pallas_call(
        attend_kernel,
        grid=(pairs,),
        in_specs=[pl.BlockSpec(memory_space=pltpu.SMEM), flat]
        + kv_specs(kv_blocks, lanes)
        + [
            pl.BlockSpec((keys, rows), lambda p: (0, 0)),
            row_spec,
            pl.BlockSpec((1, 8, keys), lambda p: (p, 0, 0)),
            flat,
        ],
        out_specs=[flat, flat, row_spec],
        out_shape=[
            jax.ShapeDtypeStruct((rows, local), f32),
            jax.ShapeDtypeStruct((rows, local), bf16),
            jax.ShapeDtypeStruct((pairs, 8, rows), f32),
        ],
        compiler_params=pltpu.CompilerParams(vmem_limit_bytes=32 << 20),
        cost_estimate=pl.CostEstimate(flops=1, transcendentals=1, bytes_accessed=1),
        name="attend",
    )(place, query, *twice(kv_blocks), bias, forget_q, forget_k, raw_g)


def attention_back(query, d_out, kv_blocks, bias, forget_q, forget_k, lse):
    rows, local = query.shape
    pairs = forget_q.shape[0]
    keys = bias.shape[0]
    lanes = local // pairs
    count = len(kv_blocks)
    flat = pl.BlockSpec((rows, lanes), lambda p: (0, p))
    row_spec = pl.BlockSpec((1, 8, rows), lambda p: (p, 0, 0))
    key_spec = pl.BlockSpec((1, 8, keys), lambda p: (p, 0, 0))
    return pl.pallas_call(
        attend_back_kernel,
        grid=(pairs,),
        in_specs=[flat, flat]
        + kv_specs(kv_blocks, lanes)
        + [pl.BlockSpec((keys, rows), lambda p: (0, 0)), row_spec, key_spec, row_spec],
        out_specs=[flat]
        + [pl.BlockSpec((2, rows, lanes), lambda p: (0, 0, p))] * count
        + [row_spec, key_spec],
        out_shape=[jax.ShapeDtypeStruct((rows, local), f32)]
        + [
            jax.ShapeDtypeStruct((2, rows, local), bf16 if d == count - 1 else f32)
            for d in range(count)
        ]
        + [
            jax.ShapeDtypeStruct((pairs, 8, rows), f32),
            jax.ShapeDtypeStruct((pairs, 8, keys), f32),
        ],
        scratch_shapes=[pltpu.VMEM((keys, rows), f32), pltpu.VMEM((keys, rows), f32)],
        compiler_params=pltpu.CompilerParams(vmem_limit_bytes=40 << 20),
        cost_estimate=pl.CostEstimate(flops=1, transcendentals=1, bytes_accessed=1),
        name="attend_back",
    )(query, d_out, *twice(kv_blocks), bias, forget_q, forget_k, lse)


def small_kernel(d_lin, first_in, gains, other, gain_q, gain_k, d_bias, *outs):
    part = first_in.shape[1] // len(outs)
    local = gain_q.shape[1]
    for d, out in enumerate(outs):
        cols = slice(d * part, (d + 1) * part)
        out[...] = jnp.zeros_like(out)
        out[:24, :part] = mm(d_lin[...], first_in[:, cols])
        out[24:26, :part] = gains[:, cols] + other[:, cols]
        out[26:27, :local] = gain_q[...]
        out[27:28, :local] = gain_k[...]
        out[32:40, :1] = d_bias[...]


def pieces_kernel(place, *refs):
    rest, out = refs[-2:]
    count = len(refs) - 2
    rows = refs[0].shape[0]
    for k, piece in enumerate(refs[:count]):
        start = pl.multiple_of(lax.rem(place[2] + k, count) * rows, 16)
        out[pl.ds(start, rows), :] = piece[...]
    out[count * rows :, :] = rest[...]


class Order:

    def __init__(self):
        self.last, self.held = None, []

    def tied(self, *args):
        if self.last is not None:
            args, _, _ = lax.optimization_barrier((args, self.last, self.held))
        self.held = []
        return args

    def hold(self, values):
        self.held.append(values)

    def __call__(self, work, *args):
        found = work(*self.tied(*args))
        self.last = min(jax.tree.leaves(found), key=nbytes)
        return found


class LineSum:

    def __init__(self, order, values):
        self.order, self.total = order, values
        self.count = lax.axis_size("ctx")
        self.half = self.count // 2
        self.hop, self.coming = 0, None
        self.send()

    def send(self):
        k, count, half = self.hop, self.count, self.half
        if k < half - 1:
            pairs = [(k, k + 1), (count - 1 - k, count - 2 - k)]
        elif k == half - 1:
            pairs = [(half - 1, half), (half, half - 1)]
        elif k < 2 * half - 1:
            j = 2 * half - 2 - k
            pairs = [(j + 1, j), (count - 2 - j, count - 1 - j)]
        else:
            return
        self.coming = lax.ppermute(self.total, "ctx", pairs)

    def step(self):
        k, half = self.hop, self.half
        self.hop += 1
        if k < half:
            self.total = self.order(add_rows, self.total, self.coming)
            self.coming = None
        elif k < 2 * half - 2:
            j = 2 * half - 2 - k
            index = lax.axis_index("ctx")
            at_ends = (index == j) | (index == self.count - 1 - j)
            self.total = self.order(
                lambda a, b: jnp.where(at_ends, b, a), self.total, self.coming
            )
            self.coming = None
        else:
            self.order.hold(self.coming)
            return
        self.send()

    def finish(self):
        while self.hop < 2 * self.half - 1:
            self.step()
        return self.total, self.coming


def spread_out(order, place, planes):
    sums = [s.finish() for plane in planes for s in plane]
    arrays = [x for pair in sums for x in pair if x is not None]
    each = len(arrays) // len(sums)
    height, width = planes[0][0].total.shape
    chunks = len(planes[0])
    block = 128 if height % 128 == 0 else height
    steps = height // block
    count = lax.axis_size("ctx")

    def spread_out_kernel(place, *refs):
        out = refs[-1]
        at_ends = (place[2] == 0) | (place[2] == count - 1)
        for c in range(chunks):

            @pl.when(pl.program_id(0) // steps == c)
            def _():
                for i in range(len(planes)):
                    first = (i * chunks + c) * each
                    value = refs[first][...].astype(f32)
                    if each > 1:
                        value = jnp.where(at_ends, refs[first + 1][...].astype(f32), value)
                    if len(planes) > 1:
                        out[:, i, :] = value
                    else:
                        out[...] = value

    def spec(c):
        return pl.BlockSpec(
            (block, width), lambda j: (jnp.clip(j - c * steps, 0, steps - 1), 0)
        )

    specs = [spec(c) for _ in planes for c in range(chunks) for _ in range(each)]
    middle = (len(planes),) if len(planes) > 1 else ()
    call = pl.pallas_call(
        spread_out_kernel,
        grid=(chunks * steps,),
        in_specs=[pl.BlockSpec(memory_space=pltpu.SMEM)] + specs,
        out_specs=pl.BlockSpec((block, *middle, width), lambda j: (j, *(0 for _ in middle), 0)),
        out_shape=jax.ShapeDtypeStruct((chunks * height, *middle, width), f32),
        compiler_params=pltpu.CompilerParams(vmem_limit_bytes=24 << 20),
        cost_estimate=pl.CostEstimate(flops=1, transcendentals=1, bytes_accessed=1),
        name="spread_out",
    )
    return order(call, place, *arrays)


schedule = (
    "bs1", "U00", "D00", "bs2", "G00", "mb", "U01", "gb", "ab", "c1", "O0", "G01", "U02", "ms1",
    "qb", "G10", "D10", "fgq", "c2", "O1", "U10", "D01", "G02", "U03", "Qq1", "c3", "ms2", "O2",
    "G03", "D02", "G11", "U0h", "sb", "O3", "U11", "Qq2", "rb", "G0h", "D11", "lv", "fs1", "G12",
    "Qg1", "D03", "fs2", "Oh", "K1", "Qq3", "U12", "V1", "D0h", "fsum", "G13", "D12", "Qqh", "U13",
    "K2", "Qg2", "so", "G1h", "D13", "U1h", "V2", "K3", "eb", "of", "sm", "Qg3", "sm1", "gu",
    "D1h", "V3", "Kh", "sm2", "Qgh", "st", "sm3", "df", "Vh", "at", "smf",
)


def body(
    tokens,
    seg_parents,
    seg_offsets,
    tok_seg,
    norm_gain,
    w_attn,
    w_heads,
    forget_bias,
    qk_gain,
    w_out,
    w_gate_up,
    w_down,
    cotangent,
):
    shards = lax.axis_size("shard")
    ctxs = lax.axis_size("ctx")
    ctx = lax.axis_index("ctx")
    tps = lax.axis_size("tp")
    rows, width = tokens.shape[1:]
    half = rows // 2
    part = width // shards
    local = w_attn.shape[2]
    heads = w_heads.shape[2]
    heads_up = 8
    size = local // heads
    hidden_size = w_gate_up.shape[2]
    segs = seg_parents.shape[1]
    order = Order()
    place = jnp.stack(
        [lax.axis_index("tp") % 2, lax.axis_index("shard"), ctx]
    ).astype(jnp.int32)

    def gathered(piece):
        return [piece] + [from_ring(piece, "shard", d) for d in range(1, shards)]

    def owned(piece):
        return [piece[:, :part]] + [
            from_ring(piece[:, part * (shards - d) : part * (shards - d + 1)], "shard", d)
            for d in range(1, shards)
        ]

    def crossed(total):
        bit = 2
        other = partner(total, "tp", bit)
        while bit * 2 < tps:
            total = (total.astype(f32) + other.astype(f32)).astype(bf16)
            bit = bit * 2
            other = partner(total, "tp", bit)
        return total, other

    def pack_small(w, gain):
        table = jnp.pad(
            jnp.transpose(w, (1, 2, 0)), ((0, 0), (0, heads_up - heads), (0, 0))
        ).reshape(3 * heads_up, part)
        return jnp.concatenate([table, jnp.pad(gain, ((0, 6), (0, 0)))], axis=0).astype(bf16)

    packs = gathered(order(pack_small, w_heads, norm_gain))
    attn_b = order(lambda w: jnp.transpose(w, (1, 0, 2)).astype(bf16), w_attn)
    piece_rows = hidden_size // (2 * ctxs)
    piece = order(
        lambda w: lax.dynamic_slice_in_dim(w, ctx * piece_rows, piece_rows, 0).astype(bf16), w_down
    )
    pieces = [from_ring(piece, "shard", d) for d in range(1, shards)]
    kv_w = gathered(order(lambda w: w[1:3], attn_b))
    padded = jnp.full((segs_up - segs,), -1, jnp.int32)
    low = jnp.concatenate([seg_offsets[0, :segs], padded])
    high = jnp.concatenate([seg_offsets[0, 1:], padded])
    parents = jnp.concatenate([seg_parents[0], padded])
    bias, seen, key_anc, onehot, parent, start, ends, anc, key_onehot = order(
        lambda *a: whole(
            masks_kernel,
            [
                ((rows * ctxs, rows), f32),
                ((rows, rows), f32),
                ((rows * ctxs, segs_up), f32),
                ((rows, segs_up), f32),
                ((rows, segs_up), f32),
                ((rows, 1), f32),
                ((segs_up, rows), f32),
                ((segs_up, segs_up), f32),
                ((rows * ctxs, segs_up), f32),
            ],
            *a,
        ),
        place,
        low[None],
        high[None],
        high[:, None],
        parents[:, None],
        tok_seg[0][:, None],
    )
    tree, cotangent = tokens[0], cotangent[0]
    if part % 128:
        tree = turned(tree, place[1], shards)
        cotangent = turned(cotangent, place[1], shards)

    def settled(values):
        return turned(values, shards - place[1], shards) if part % 128 else values

    for p in pieces:
        order.hold(p)
    (first_in,) = order(
        lambda *a: whole(enter_kernel, [((rows, width), bf16)], *a), place, tree, packs
    )
    pieces = order.tied(*pieces)
    piece_sets = [[p] + [from_ring(p, "ctx", k) for k in range(1, ctxs)] for p in pieces]
    bundles = gathered(
        order(lambda a, w: jnp.stack([a[0], a[3], w.T.astype(bf16)]), attn_b, w_out)
    )
    gateup_w = gathered(
        order(lambda w: jnp.transpose(w, (1, 0, 2)).astype(bf16), w_gate_up)
    )

    own_down = order(lambda w: w.astype(bf16), w_down)
    down_rest = [
        from_ring(own_down[hidden_size // 2 :], "shard", d) for d in range(1, shards)
    ]
    order.hold(piece_sets)

    forget_col = jnp.pad(forget_bias, (0, heads_up - heads))[:, None]
    raw_kv, lin, message = order(
        lambda *a: whole(
            keys_in_kernel,
            [
                ((2, rows, local), f32),
                ((3 * heads_up, rows), f32),
                ((segs_up + heads_up, 2 * local), f32),
            ],
            *a,
        ),
        first_in,
        kv_w,
        packs,
        forget_col,
        seen,
        onehot,
        ends,
    )
    blocks = [message] + [along(message, "ctx", d) for d in range(1, ctxs)]
    gain_q, gain_k = qk_gain[:1], qk_gain[1:]
    own_kv, delta, forget_q, forget_k = order(
        lambda *a: whole(
            named(keys_shift_kernel, size=size),
            [
                ((2, rows, local), bf16),
                ((2, rows, local), f32),
                ((heads // 2, 8, rows), f32),
                ((heads // 2, 8, rows * ctxs), f32),
            ],
            *a,
        ),
        raw_kv,
        lin,
        blocks,
        parent,
        start,
        key_anc,
        gain_k,
    )
    kv_blocks = [own_kv] + [along(own_kv, "ctx", d) for d in range(1, ctxs)]
    raw_q, query, raw_g = order(
        lambda *a: whole(
            named(queries_kernel, size=size),
            [((rows, local), f32), ((rows, local), bf16), ((rows, local), f32)],
            *a,
        ),
        first_in,
        bundles,
        gain_q,
    )
    attended, gated, lse = order(
        attention, place, query, kv_blocks, bias, forget_q, forget_k, raw_g
    )

    (share,) = order(
        lambda *a: whole(attn_share_kernel, [((half, width), f32)], *a), gated, bundles
    )
    given = partner(share, "tp", 1)
    (total,) = order(
        lambda *a: whole(attn_share_sum_kernel, [((half, width), bf16)], *a),
        gated,
        bundles,
        given,
    )
    total, other = crossed(total)
    middle, second = order(
        lambda *a: whole(
            middle_kernel, [((half, width), f32), ((half, width), bf16)], *a
        ),
        place,
        tree,
        packs,
        total,
        other,
    )
    second_too = partner(second, "tp", 1)
    down_w = [own_down] + [
        order(
            lambda *a: whole(pieces_kernel, [((hidden_size, part), bf16)], *a)[0], place, *p, r
        )
        for p, r in zip(piece_sets, down_rest)
    ]
    grad_out, d_hidden = order(
        lambda *a: whole(
            grad_hidden_kernel, [((rows, width), bf16), ((rows, hidden_size), f32)], *a
        ),
        place,
        cotangent,
        down_w,
    )
    hidden, d_lin = order(mlp, second, second_too, gateup_w, d_hidden)
    first_parts = owned(order.tied(first_in)[0])

    at = {}
    hidden_half, part_half = hidden_size // 2, part // 2

    def core_sum(name, kernel, out, *args):
        def run(given):
            (at[name],) = order(
                lambda *a: whole(kernel, [((half, width), out)], *a), *args, *given
            )

        return run

    def shared(kernel, *args):
        (share,) = order(lambda *a: whole(kernel, [((half, width), f32)], *a), *args)
        return partner(share, "tp", 1)

    def total_of(kernel, *args):
        (total,) = order(lambda *a: whole(kernel, [((half, width), bf16)], *a), *args)
        return crossed(total)

    def left(values, d):
        return lax.ppermute(values, "ctx", [(i, i - 1) for i in range(d, ctxs)])

    def chained(partial, got):
        return whole(chain_kernel, [(partial.shape, bf16)], partial, got)[0]

    def rows_at(k):
        return (k * half, (k + 1) * half)

    def out_part(d, got=()):
        return weight_grad(
            order,
            [
                (At(gated, rows=rows_at(k)), At(x, cols=(d * part, (d + 1) * part)))
                for k, x in enumerate((at["mb"], at["mb_too"]))
            ],
            got,
            min(128, local),
        )

    def summed(left_ones, right_ones, block, cols=None, lead=None, right_cols=None):
        return LineSum(
            order,
            weight_grad(
                order,
                [
                    (At(a, cols=cols), At(b, lead=lead, cols=right_cols))
                    for a, b in zip(left_ones, right_ones)
                ],
                (),
                block,
            ),
        )

    def run_bs1():
        at["bs1"] = partner(order(lambda d, *w: back_share(d, w, 1), d_lin, *gateup_w), "tp", 1)

    def run_bs2():
        at["bs2"] = crossed(
            order(lambda g, d, *w: back_share(d, w, 0, g), at["bs1"], d_lin, *gateup_w)
        )

    def column_part(d, start, stop):
        return (d * part + start, d * part + stop)

    def down_part(i, d, got=()):
        return weight_grad(
            order,
            [
                (
                    At(hidden, cols=(i * hidden_half, (i + 1) * hidden_half)),
                    At(grad_out, cols=column_part(d, 0, part)),
                )
            ],
            got,
            256,
        )

    def lin_part(lead, i, d, got=()):
        return weight_grad(
            order,
            [
                (
                    At(x, cols=column_part(d, i * part_half, (i + 1) * part_half)),
                    At(d_lin, rows=rows_at(k), lead=lead),
                )
                for k, x in enumerate((second, second_too))
            ],
            got,
            min(128, part_half),
        )

    def run_ms1():
        at["ms1"] = shared(named(share_kernel, which=1), hidden, down_w)

    def run_ms2():
        at["ms2"] = total_of(share_sum_kernel, hidden, down_w, at["ms1"])

    def run_mb():
        at["d_middle"], at["mb"], at["gain_two"] = order(
            lambda *a: whole(
                middle_back_kernel,
                [((half, width), f32), ((half, width), bf16), ((1, width), f32)],
                *a,
            ),
            grad_out,
            packs,
            middle,
            *at["bs2"],
        )
        at["mb_too"] = partner(at["mb"], "tp", 1)

    def run_gb():
        at["d_attended"], at["d_raw_g"] = order(
            lambda *a: whole(
                gate_back_kernel, [((rows, local), bf16), ((rows, local), bf16)], *a
            ),
            place,
            at["mb"],
            at["mb_too"],
            bundles,
            raw_g,
            attended,
        )

    def run_ab():
        order.hold(first_parts[1:])
        backs = order(
            attention_back, query, at["d_attended"], kv_blocks, bias, forget_q, forget_k, lse
        )
        at["d_query"], at["d_kv"] = backs[0], backs[1 : 1 + ctxs]
        at["dcq"], at["dck"] = backs[1 + ctxs :]

    def run_c(d):
        if d == ctxs - 1:
            at["coming"] = left(order.tied(at["d_kv"][d])[0], d)
        else:
            at["coming"] = left(order(chained, at["d_kv"][d], at["coming"]), d)

    def run_qb():
        at["d_gq"], at["gain_q"] = order(
            lambda *a: whole(
                named(query_back_kernel, size=size),
                [((rows, 2 * local), bf16), ((1, local), f32)],
                *a,
            ),
            raw_q,
            at["d_query"],
            gain_q,
            at["d_raw_g"],
        )
        at["gq"] = gathered(at["d_gq"])

    def run_fgq():
        (at["fgq"],) = order(
            lambda *a: whole(first_gq_kernel, [((rows, width), f32)], *a),
            place,
            at["d_gq"],
            bundles,
        )

    def run_sb():
        at["base"], at["messages"], at["d_alpha"], at["gain_k"], at["d_forget"] = order(
            lambda *a: shift_back(a, rows, local, heads_up, ctxs, size),
            at["d_kv"][0],
            at["coming"],
            raw_kv,
            delta,
            lin,
            gain_k,
            start,
            parent,
            at["dcq"],
            at["dck"],
            key_onehot,
        )
        at["returned"] = [along(m, "ctx", -d - 1) for d, m in enumerate(at["messages"])]

    def run_rb():
        at["d_raw_kv"], at["d_head"], at["d_bias"] = order(
            lambda *a: whole(
                raw_back_kernel,
                [((2, rows, local), bf16), ((3 * heads_up, rows), bf16), ((heads_up, 1), f32)],
                *a,
            ),
            at["base"],
            at["messages"][0],
            at["returned"],
            ends,
            seen,
            onehot,
            anc,
            lin,
            at["d_forget"],
            at["d_alpha"],
        )
        at["kv"] = gathered(at["d_raw_kv"])

    def first_share(which):
        return order(
            lambda *a: whole(
                named(first_share_kernel_of(part, rows), which=which), [((half, width), f32)], *a
            )[0],
            place,
            at["d_raw_kv"],
            at["d_head"],
            kv_w,
            packs,
            at["fgq"],
        )

    def run_fs1():
        at["fs1"] = partner(first_share(1), "tp", 1)

    def run_fs2():
        at["fs2"] = first_share(0)

    def run_fsum():
        at["fsum"] = total_of(first_sum_kernel, at["fs2"], at["fs1"])

    def run_eb():
        at["eb"], gain_one = order(
            lambda *a: whole(
                enter_back_kernel, [((half, width), f32), ((1, width), f32)], *a
            ),
            place,
            tree,
            packs,
            at["d_middle"],
            *at["fsum"],
        )
        at["eb_too"] = partner(at["eb"], "tp", 1)
        at["gains"] = jnp.concatenate([gain_one, at["gain_two"]], axis=0)
        at["gains_too"] = partner(at["gains"], "tp", 1)

    def settle(name, kind):
        (at[name],) = order(
            lambda *a: whole(named(settle_kernel, shards=shards), [((rows, width), kind)], *a),
            place,
            at[name],
            at[name + "_too"],
        )

    def run_lv():
        (at["lv"],) = order(
            lambda *a: whole(leave_kernel, [((half, width), bf16)], *a), middle, *at["ms2"]
        )
        at["lv_too"] = partner(at["lv"], "tp", 1)

    def run_sm():
        at["sm"] = order(
            lambda *a: whole(
                small_kernel, [((40, max(part, local)), f32) for _ in range(shards)], *a
            ),
            at["d_head"],
            first_in,
            at["gains"],
            at["gains_too"],
            at["gain_q"],
            at["gain_k"],
            at["d_bias"],
        )
        at["sm_got"] = [from_ring(at["sm"][d], "shard", shards - d) for d in range(1, shards)]

    def run_sm1():
        small = at["sm"][0]
        for got in at["sm_got"]:
            small = order(add_rows, small, got)
        at["small"] = LineSum(order, small)

    def run_out(name, *planes):
        at[name] = spread_out(order, place, [[at[n] for n in plane] for plane in planes])

    block = min(128, part)
    work = {
        "bs1": run_bs1, "bs2": run_bs2,
        "ms1": run_ms1, "ms2": run_ms2, "mb": run_mb, "gb": run_gb,
        "ab": run_ab, "c1": lambda: run_c(ctxs - 1), "c2": lambda: run_c(ctxs - 2),
        "c3": lambda: [run_c(d) for d in range(ctxs - 3, 0, -1)], "qb": run_qb, "fgq": run_fgq,
        "sb": run_sb, "rb": run_rb, "fs1": run_fs1, "fs2": run_fs2, "fsum": run_fsum,
        "eb": run_eb, "st": lambda: settle("eb", f32), "lv": run_lv,
        "so": lambda: settle("lv", bf16), "sm": run_sm, "sm1": run_sm1,
        "gu": lambda: run_out("gu", ("G0", "G1"), ("U0", "U1")),
        "df": lambda: run_out("df", ("D0", "D1")), "of": lambda: run_out("of", ("O",)),
        "at": lambda: run_out("at", ("Qq",), ("K",), ("V",), ("Qg",)),
    }
    starts = {
        "Qg1": lambda: summed(first_parts, at["gq"], block, right_cols=(0, local)),
        "Qq1": lambda: summed(first_parts, at["gq"], block, right_cols=(local, 2 * local)),
        "K1": lambda: summed(first_parts, at["kv"], block, lead=0),
        "V1": lambda: summed(first_parts, at["kv"], block, lead=1),
    }
    makes = {"O": out_part}
    for i in range(2):
        makes[f"D{i}"] = functools.partial(down_part, i)
        for lead, name in enumerate("GU"):
            makes[f"{name}{i}"] = functools.partial(lin_part, lead, i)
    for name, make in makes.items():

        def give(name=name, make=make):
            at[name + "0"] = [
                from_ring(make(d), "shard", shards - d) for d in range(1, shards)
            ]

        work[name + "0"] = give
        starts[name + "1"] = lambda name=name, make=make: LineSum(
            order, make(0, at[name + "0"])
        )
    for name in schedule:
        if name in work:
            work[name]()
        elif name in starts:
            at[name[:-1]] = starts[name]()
        else:
            at["small" if name[:2] == "sm" else name[:-1]].step()
    small, ends_small = at["small"].finish()
    if ends_small is not None:
        small = jnp.where((ctx == 0) | (ctx == ctxs - 1), ends_small, small)
    return (
        settled(at["lv"])[None],
        settled(at["eb"])[None],
        small[24:26, :part],
        at["at"],
        jnp.transpose(
            small[: 3 * heads_up, :part].reshape(3, heads_up, part)[:, :heads], (2, 0, 1)
        ),
        small[32 : 32 + heads, 0],
        small[26:28, :local],
        at["of"],
        at["gu"],
        at["df"],
    )


def shift_back(args, rows, local, heads_up, ctxs, size):
    edge = (segs_up + heads_up, 2 * local)
    count = ctxs - 1

    def shift_back_all_kernel(*refs):
        ins, outs = refs[:11], refs[11:]
        shift_back_kernel(
            *ins, outs[0], outs[1 : 1 + count], *outs[1 + count :], size=size
        )

    outs = whole(
        shift_back_all_kernel,
        [((2, rows, local), f32)]
        + [(edge, f32)] * count
        + [((2 * heads_up, rows), f32), ((1, local), f32), ((heads_up, rows), f32)],
        *args,
    )
    return outs[0], list(outs[1 : 1 + count]), *outs[1 + count :]


def first_share_kernel_of(part, rows):
    def first_share_scoped_kernel(*refs, which):
        pl.run_scoped(
            lambda scratch: first_share_kernel(*refs, scratch, which=which),
            pltpu.VMEM((rows, part), f32),
        )

    return first_share_scoped_kernel


def solution(mesh):
    in_specs = (
        P("shard", "ctx", None),
        P("shard", None),
        P("shard", None),
        P("shard", "ctx"),
        P(None, "shard"),
        P("shard", None, "tp"),
        P("shard", None, "tp"),
        P("tp"),
        P(None, "tp"),
        P("tp", "shard"),
        P("shard", None, "tp"),
        P("tp", "shard"),
        P("shard", "ctx", None),
    )
    out_specs = (
        P("shard", "ctx", None),
        P("shard", "ctx", None),
        P(None, "shard"),
        P("shard", None, "tp"),
        P("shard", None, "tp"),
        P("tp"),
        P(None, "tp"),
        P("tp", "shard"),
        P("shard", None, "tp"),
        P("tp", "shard"),
    )
    return jax.shard_map(body, mesh=mesh, in_specs=in_specs, out_specs=out_specs, check_vma=False)
```

```python
import functools

import jax
import jax.numpy as jnp
from jax import lax
from jax.experimental import pallas as pl
from jax.experimental.pallas import tpu as pltpu
from jax.sharding import PartitionSpec as P

epsilon = 1e-06
neg_large = -1e30
f32 = jnp.float32
bf16 = jnp.bfloat16
segs_up = 16


def from_ring(values, axis, step):
    count = lax.axis_size(axis)
    return lax.ppermute(values, axis, [((i + step) % count, i) for i in range(count)])


def along(values, axis, step):
    count = lax.axis_size(axis)
    return lax.ppermute(
        values, axis, [(i, i + step) for i in range(count) if 0 <= i + step < count]
    )


def partner(values, axis, bit):
    count = lax.axis_size(axis)
    return lax.ppermute(values, axis, [(i, i ^ bit) for i in range(count)])


def dot_of(dims, precision=None):
    def product(left, right):
        return lax.dot_general(
            left, right, (dims, ((), ())), precision=precision, preferred_element_type=f32
        )

    return product


mm = dot_of(((1,), (0,)))
mm_nt = dot_of(((1,), (1,)))
mm_tn = dot_of(((0,), (0,)))


def bf16_pieces(values, count):
    pieces = []
    for _ in range(count - 1):
        pieces.append(values.astype(bf16))
        values = values - pieces[-1].astype(f32)
    return pieces + [values.astype(bf16)]


def exact_by(product, side):
    def exactly(left, right, count=3):
        if side == 0:
            right = right.astype(bf16)
            return sum(product(p, right) for p in bf16_pieces(left, count))
        left = left.astype(bf16)
        return sum(product(left, p) for p in bf16_pieces(right, count))

    return exactly


left_exact, left_exact_nt, left_exact_tn = (exact_by(p, 0) for p in (mm, mm_nt, mm_tn))
right_exact, right_exact_nt, right_exact_tn = (exact_by(p, 1) for p in (mm, mm_nt, mm_tn))


def rms_scale(values):
    return lax.rsqrt(jnp.mean(values * values, axis=-1, keepdims=True) + epsilon)


def norm_grad(values, scale, gain_row, d_result):
    normed = values * scale
    d_normed = d_result * gain_row
    d_values = scale * (d_normed - normed * jnp.mean(d_normed * normed, axis=-1, keepdims=True))
    return d_values, jnp.sum(d_result * normed, axis=0, keepdims=True)


def iota(shape, axis):
    return lax.broadcasted_iota(jnp.int32, shape, axis)


def same_head(width, size):
    return jnp.where(iota((width, width), 0) // size == iota((width, width), 1) // size, 1.0, 0.0)


def head_mean(values, size):
    return left_exact(values, same_head(values.shape[1], size), 2) * (1.0 / size)


def head_scale(values, size):
    return lax.rsqrt(head_mean(values * values, size) + epsilon)


def head_grad(values, gain_row, d_result, size):
    scale = head_scale(values, size)
    normed = values * scale
    d_normed = d_result * gain_row
    d_values = scale * (d_normed - normed * head_mean(d_normed * normed, size))
    return d_values, jnp.sum(d_result * normed, axis=0, keepdims=True)


def spread_of(heads_up, width, size):
    return jnp.where(iota((heads_up, width), 0) == iota((heads_up, width), 1) // size, 1.0, 0.0)


def nbytes(leaf):
    return leaf.size * leaf.dtype.itemsize


def whole(kernel, outs, *args, extra=8):
    leaves, form = jax.tree.flatten(args)

    def flat(*refs):
        kernel(*jax.tree.unflatten(form, refs[: len(leaves)]), *refs[len(leaves) :])

    shapes = [jax.ShapeDtypeStruct(shape, kind) for shape, kind in outs]
    spaces = [
        pltpu.SMEM if leaf.ndim == 1 and leaf.dtype == jnp.int32 else pltpu.VMEM
        for leaf in leaves
    ]
    size = sum(nbytes(x) for x in leaves) + sum(nbytes(x) for x in shapes)
    found = pl.pallas_call(
        flat,
        out_shape=shapes,
        in_specs=[pl.BlockSpec(memory_space=s) for s in spaces],
        out_specs=[pl.BlockSpec(memory_space=pltpu.VMEM) for _ in shapes],
        compiler_params=pltpu.CompilerParams(
            vmem_limit_bytes=min(60 << 20, size + size // 4 + (extra << 20))
        ),
        cost_estimate=pl.CostEstimate(flops=1, transcendentals=1, bytes_accessed=1),
        name=kernel.__name__,
    )(*leaves)
    return found


def masks_kernel(place, low, high, high_col, parents_col, seg_col, bias, later, seen, key_anc, onehot, parent, start, ends, anc, key_onehot):
    rows = seg_col.shape[0]
    ctx = place[2]
    lanes = iota((segs_up, segs_up), 1)
    parent_mat = jnp.where(parents_col[...] == lanes, 1.0, 0.0)
    eye = jnp.where(iota((segs_up, segs_up), 0) == lanes, 1.0, 0.0)
    ancestry = eye + parent_mat + right_exact(parent_mat, parent_mat, 1)
    anc[...] = ancestry
    mine = jnp.where(seg_col[...] == iota((rows, segs_up), 1), 1.0, 0.0)
    onehot[...] = mine
    parent[...] = right_exact(mine, parent_mat, 1)
    mine_anc = right_exact(mine, ancestry, 1)
    query_pos = ctx * rows + iota((1, rows), 1)
    query_col = ctx * rows + iota((rows, 1), 0)
    ends[...] = jnp.where(query_pos == high_col[...] - 1, 1.0, 0.0)
    start[...] = jnp.sum(
        jnp.where(query_col == low[...], 1.0, 0.0), axis=1, keepdims=True
    )
    for d in range(bias.shape[0] // rows):
        span = slice(d * rows, (d + 1) * rows)
        key_pos = (ctx - d) * rows + iota((rows, 1), 0)
        keys = jnp.where((key_pos >= low[...]) & (key_pos < high[...]), 1.0, 0.0)
        key_anc[span, :] = right_exact(keys, ancestry, 1)
        key_onehot[span, :] = keys
        linked = mm_nt(keys.astype(bf16), mine_anc.astype(bf16)) > 0.5
        visible = linked & (key_pos <= query_pos)
        bias[span, :] = jnp.where(visible, 0.0, neg_large)
        if d == 0:
            seen[...] = jnp.where(visible, 1.0, 0.0)
            own_keys = keys.astype(bf16)
    for d in range(1, bias.shape[0] // rows):
        span = slice((d - 1) * rows, d * rows)
        query_at = (ctx + d) * rows + iota((rows, 1), 0)
        theirs = jnp.where((query_at >= low[...]) & (query_at < high[...]), 1.0, 0.0)
        theirs = right_exact(theirs, ancestry, 1).astype(bf16)
        later[span, :] = jnp.where(mm_nt(own_keys, theirs) > 0.5, 0.0, neg_large)


def turned(values, first, count):
    width = values.shape[1] // count
    pieces = [
        lax.dynamic_slice_in_dim(values, lax.rem(first + i, count) * width, width, 1)
        for i in range(count)
    ]
    return jnp.concatenate(pieces, axis=1)


def part_at(ref, shard, d, shards, rows=slice(None)):
    part = ref.shape[1] // shards
    if part % 128:
        return ref[rows, d * part : (d + 1) * part]
    start = pl.multiple_of(lax.rem(shard + d, shards) * part, 128)
    return ref[rows, pl.ds(start, part)]


def enter_kernel(place, tokens, packs, first_in):
    shards = len(packs)
    part = packs[0].shape[1]
    pieces = [part_at(tokens, place[1], d, shards).astype(f32) for d in range(shards)]
    mean = sum(jnp.sum(x * x, axis=1, keepdims=True) for x in pieces) * (
        1.0 / tokens.shape[1]
    )
    scale = lax.rsqrt(mean + epsilon)
    for d in range(shards):
        gain = packs[d][24:25, :].astype(f32)
        first_in[:, d * part : (d + 1) * part] = (pieces[d] * scale * gain).astype(bf16)


def keys_in_kernel(first_in, kv_w, packs, forget_bias, seen, onehot, ends, raw_kv, lin, message):
    part = packs[0].shape[1]
    rows = first_in.shape[0]
    local = raw_kv.shape[2]
    heads_up = forget_bias.shape[0]
    cuts = [first_in[:, d * part : (d + 1) * part] for d in range(len(packs))]
    head_lin = sum(mm_nt(p[:24, :], x) for p, x in zip(packs, cuts))
    forget_in = head_lin[:heads_up] + forget_bias[...]
    lin[...] = head_lin
    lin[:heads_up, :] = forget_in
    log_forget = jnp.minimum(forget_in, 0.0) - jnp.log1p(jnp.exp(-jnp.abs(forget_in)))
    message[...] = jnp.zeros_like(message)
    for i in range(2):
        raw = sum(mm(x, w[i]) for w, x in zip(kv_w, cuts))
        raw_kv[i] = raw
        cols = slice(i * local, (i + 1) * local)
        message[:segs_up, cols] = right_exact(ends[...], raw)
        message[segs_up - 1 : segs_up, cols] = raw[rows - 1 :]
    message[segs_up : segs_up + heads_up, :rows] = left_exact(log_forget, seen[...])
    message[segs_up : segs_up + heads_up, local : local + segs_up] = left_exact(
        log_forget, onehot[...]
    )


def keys_shift_kernel(raw_kv, lin, blocks, parent, start, key_anc, gain, own_kv, delta, fq, fk, *, size):
    rows, local = raw_kv.shape[1:]
    heads_up = lin.shape[0] // 3
    spread = spread_of(heads_up, local, size)
    seg_ends = sum((b[:segs_up, :] for b in blocks[1:]), blocks[0][:segs_up, :])
    at_start = start[...] > 0.5
    at_top = iota((rows, 1), 0) == 0
    for i in range(2):
        cols = slice(i * local, (i + 1) * local)
        alpha_rows = jax.nn.sigmoid(lin[(i + 1) * heads_up : (i + 2) * heads_up, :])
        alpha = left_exact_tn(alpha_rows, spread)
        raw = raw_kv[i]
        previous = jnp.where(
            at_top, blocks[1][segs_up - 1 : segs_up, cols], pltpu.roll(raw, 1, 0)
        )
        previous = jnp.where(at_start, right_exact(parent[...], seg_ends[:, cols]), previous)
        step = previous - raw
        delta[i] = step
        shifted = raw + alpha * step
        if i == 0:
            shifted = shifted * head_scale(shifted, size) * gain[...]
        own_kv[i] = shifted.astype(bf16)
    table = slice(segs_up, segs_up + heads_up)
    for d in range(len(blocks)):
        sums = blocks[d][table, :rows]
        span = slice(d * rows, (d + 1) * rows)
        later = blocks[d + 1 :]
        if later:
            before = sum(
                (b[table, local : local + segs_up] for b in later[1:]),
                later[0][table, local : local + segs_up],
            )
            sums = sums + left_exact_nt(before, key_anc[span, :])
        for h in range(2 * fk.shape[0]):
            fk[h // 2, h % 2 : h % 2 + 1, span] = sums[h : h + 1]
            if d == 0:
                fq[h // 2, h % 2 : h % 2 + 1, :] = sums[h : h + 1]


def queries_kernel(first_in, bundles, gain, raw_q, query, raw_g, *, size):
    part = bundles[0].shape[1]
    cuts = [first_in[:, d * part : (d + 1) * part] for d in range(len(bundles))]
    raw = sum(mm(x, w[0]) for w, x in zip(bundles, cuts))
    raw_q[...] = raw
    raw_g[...] = sum(mm(x, w[1]) for w, x in zip(bundles, cuts))
    normed = (raw * head_scale(raw, size) * gain[...]).astype(bf16)
    query[...] = (normed.astype(f32) * (size**-0.5)).astype(bf16)


def attn_share_kernel(values, bundles, out):
    half = out.shape[0]
    part = bundles[0].shape[1]
    for d, w in enumerate(bundles):
        out[:, d * part : (d + 1) * part] = mm_nt(values[half:, :], w[2])


def attn_share_sum_kernel(values, bundles, given, out):
    half = out.shape[0]
    part = bundles[0].shape[1]
    for d, w in enumerate(bundles):
        cols = slice(d * part, (d + 1) * part)
        out[:, cols] = (mm_nt(values[:half, :], w[2]) + given[:, cols]).astype(bf16)


def share_kernel(values, weights, out, *, which):
    half = out.shape[0]
    part = out.shape[1] // len(weights)
    rows = slice(which * half, (which + 1) * half)
    for d, w in enumerate(weights):
        out[:, d * part : (d + 1) * part] = mm(values[rows, :], w[...])


def share_sum_kernel(values, weights, given, out):
    half = out.shape[0]
    part = out.shape[1] // len(weights)
    for d, w in enumerate(weights):
        cols = slice(d * part, (d + 1) * part)
        out[:, cols] = (mm(values[:half, :], w[...]) + given[:, cols]).astype(bf16)


def middle_kernel(place, tokens, packs, total, other, middle, second_in):
    shards = len(packs)
    part = packs[0].shape[1]
    half = total.shape[0]
    rows = pl.ds(pl.multiple_of(place[0] * half, 16), half)
    square = jnp.zeros((half, 1), f32)
    for d in range(shards):
        cols = slice(d * part, (d + 1) * part)
        value = part_at(tokens, place[1], d, shards, rows).astype(f32) + (
            total[:, cols].astype(f32) + other[:, cols].astype(f32)
        )
        middle[:, cols] = value
        square = square + jnp.sum(value * value, axis=1, keepdims=True)
    scale = lax.rsqrt(square * (1.0 / middle.shape[1]) + epsilon)
    for d in range(shards):
        cols = slice(d * part, (d + 1) * part)
        gain = packs[d][25:26, :].astype(f32)
        second_in[:, cols] = (middle[:, cols] * scale * gain).astype(bf16)


def grad_hidden_kernel(place, cotangent, down_w, grad_out, d_hidden):
    shards = len(down_w)
    part = down_w[0].shape[1]
    half = cotangent.shape[0] // 2
    for k in range(2):
        rows = pl.ds(pl.multiple_of(lax.rem(place[0] + k, 2) * half, 16), half)
        span = slice(k * half, (k + 1) * half)
        for d in range(shards):
            grad_out[span, d * part : (d + 1) * part] = part_at(
                cotangent, place[1], d, shards, rows
            )
    d_hidden[...] = sum(
        mm_nt(grad_out[:, d * part : (d + 1) * part], w[...]) for d, w in enumerate(down_w)
    )


def mlp_kernel(*refs):
    mine, theirs = refs[:2]
    d_hidden, hidden, d_lin, keep, give, second = refs[-6:]
    weights = refs[2:-6]
    part = weights[0].shape[1]
    half = mine.shape[0]

    @pl.when(pl.program_id(0) == 0)
    def _():
        second[:half, :] = mine[...]
        second[half:, :] = theirs[...]

    lin = [
        sum(mm(second[:, d * part : (d + 1) * part], w[i]) for d, w in enumerate(weights))
        for i in range(2)
    ]
    sig = jax.nn.sigmoid(lin[0])
    silu = lin[0] * sig
    grad = d_hidden[...]
    hidden[...] = (silu * lin[1]).astype(bf16)
    d_gate = (grad * lin[1] * (sig * (1.0 + lin[0] * (1.0 - sig)))).astype(bf16)
    d_up = (grad * silu).astype(bf16)
    d_lin[0] = d_gate
    d_lin[1] = d_up
    for d, w in enumerate(weights):
        value = mm_nt(d_gate, w[0]) + mm_nt(d_up, w[1])
        for share, rows in ((keep, slice(0, half)), (give, slice(half, 2 * half))):

            @pl.when(pl.program_id(0) == 0)
            def _():
                share[d] = value[rows]

            @pl.when(pl.program_id(0) > 0)
            def _():
                share[d] = share[d] + value[rows]


def mlp(mine, theirs, weights, d_hidden):
    half, width = mine.shape
    rows, hidden_size = d_hidden.shape
    shards = len(weights)
    part = weights[0].shape[1]
    block = 512
    flat = pl.BlockSpec((half, width), lambda j: (0, 0))
    share = pl.BlockSpec((shards, half, part), lambda j: (0, 0, 0))
    return pl.pallas_call(
        mlp_kernel,
        grid=(hidden_size // block,),
        in_specs=[flat, flat]
        + [pl.BlockSpec((2, part, block), lambda j: (0, 0, j)) for _ in weights]
        + [pl.BlockSpec((rows, block), lambda j: (0, j))],
        out_specs=[
            pl.BlockSpec((rows, block), lambda j: (0, j)),
            pl.BlockSpec((2, rows, block), lambda j: (0, 0, j)),
            share,
            share,
        ],
        out_shape=[
            jax.ShapeDtypeStruct((rows, hidden_size), bf16),
            jax.ShapeDtypeStruct((2, rows, hidden_size), bf16),
            jax.ShapeDtypeStruct((shards, half, part), f32),
            jax.ShapeDtypeStruct((shards, half, part), f32),
        ],
        scratch_shapes=[pltpu.VMEM((rows, width), bf16)],
        compiler_params=pltpu.CompilerParams(vmem_limit_bytes=26 << 20),
        cost_estimate=pl.CostEstimate(flops=1, transcendentals=1, bytes_accessed=1),
        name="mlp",
    )(mine, theirs, *weights, d_hidden)


def gain_row(packs, row):
    return jnp.concatenate([p[row : row + 1, :].astype(f32) for p in packs], axis=1)


def middle_back_kernel(grad_out, packs, middle, total, other, d_middle, d_middle_b, d_gain):
    half = middle.shape[0]
    value = middle[...]
    d_second = jnp.concatenate(
        [total[d].astype(f32) + other[d].astype(f32) for d in range(total.shape[0])], axis=1
    )
    d_value, gain = norm_grad(value, rms_scale(value), gain_row(packs, 25), d_second)
    d_gain[...] = gain
    d_value = d_value + grad_out[:half, :].astype(f32)
    d_middle[...] = d_value
    d_middle_b[...] = d_value.astype(bf16)


row_room = 48


def row_pieces(values):
    return jnp.concatenate([p.astype(f32) for p in bf16_pieces(values, 3)], axis=0)


def rows_back(block, start):
    pieces = block[...].astype(f32)[start : start + 24]
    return pieces[:8] + pieces[8:16] + pieces[16:]


def head_row(rows8, head):
    return jnp.sum(jnp.where(iota(rows8.shape, 0) == head, rows8, 0.0), axis=0, keepdims=True)


def gate_back_kernel(
    place, mine, theirs, bundles, raw_g, attended, forget_q, lse, message, d_raw_g, *, size
):
    half = mine.shape[0]
    rows, local = raw_g.shape
    part = bundles[0].shape[1]
    for k, source in enumerate((mine, theirs)):
        at = pl.ds(pl.multiple_of(lax.rem(place[0] + k, 2) * half, 16), half)
        d_gated = sum(
            mm(source[:, d * part : (d + 1) * part], w[2]) for d, w in enumerate(bundles)
        )
        sig = jax.nn.sigmoid(raw_g[at, :])
        message[at, :] = (d_gated * sig).astype(bf16)
        d_raw_g[at, :] = (d_gated * attended[at, :] * sig * (1.0 - sig)).astype(bf16)
    products = message[:rows, :].astype(f32) * attended[...]
    delta = right_exact_nt(spread_of(8, local, size), products)
    heads = 2 * forget_q.shape[0]
    forget = [
        forget_q[h // 2, h % 2 : h % 2 + 1, :] - lse[h // 2, h % 2 : h % 2 + 1, :]
        for h in range(heads)
    ]
    forget = jnp.concatenate(forget + [jnp.zeros((8 - heads, rows), f32)], axis=0)
    message[rows:, :] = jnp.concatenate(
        [row_pieces(forget), row_pieces(delta)], axis=0
    ).astype(bf16)


def query_back_kernel(raw_q, d_query, gain, d_raw_g, d_gq, d_gain, *, size):
    local = raw_q.shape[1]
    d_raw, gain_grad = head_grad(raw_q[...], gain[...], d_query[...], size)
    d_gain[...] = gain_grad
    d_gq[:, :local] = d_raw_g[...]
    d_gq[:, local:] = d_raw.astype(bf16)


def shift_back_kernel(
    d_kv, raw_kv, delta, lin, gain, start, parent, dcq, dck, onehot,
    base, message, d_alpha, d_gain, d_forget, *, size,
):
    rows, local = raw_kv.shape[1:]
    heads_up = lin.shape[0] // 3
    heads = 2 * dcq.shape[0]
    spread = spread_of(heads_up, local, size)
    not_start = 1.0 - start[...]
    start_parent = parent[...] * start[...]
    message[...] = jnp.zeros_like(message)
    for i in range(2):
        cols = slice(i * local, (i + 1) * local)
        alpha_rows = jax.nn.sigmoid(lin[(i + 1) * heads_up : (i + 2) * heads_up, :])
        alpha = left_exact_tn(alpha_rows, spread)
        d_shift = d_kv[i]
        if i == 0:
            shifted = raw_kv[0] + alpha * delta[0]
            d_shift, gain_grad = head_grad(shifted, gain[...], d_shift, size)
            d_gain[...] = gain_grad
        d_alpha[i * heads_up : (i + 1) * heads_up, :] = (
            right_exact_nt(spread, d_shift * delta[i], 2) * alpha_rows * (1.0 - alpha_rows)
        )
        d_prev = alpha * d_shift
        d_step = d_prev * not_start
        base[i] = (
            d_shift
            - d_prev
            + jnp.where(iota((rows, 1), 0) == rows - 1, 0.0, pltpu.roll(d_step, rows - 1, 0))
        )
        message[:segs_up, cols] = right_exact_tn(start_parent, d_prev, 2)
        message[segs_up - 1 : segs_up, cols] = d_step[:1]
    grads = [
        dcq[h // 2, h % 2 : h % 2 + 1, :] - dck[h // 2, h % 2 : h % 2 + 1, :]
        for h in range(heads)
    ]
    grads = jnp.concatenate(grads + [jnp.zeros((heads_up - heads, rows), f32)], axis=0)
    d_forget[...] = grads
    message[segs_up : segs_up + heads_up, local : local + segs_up] = left_exact(
        grads, onehot[...]
    )


def raw_back_kernel(
    base, table_own, returned, ends, seen, onehot, anc, lin, d_forget_own, d_alpha,
    d_raw_kv, d_lin, d_bias,
):
    rows, local = base.shape[1:]
    heads_up = lin.shape[0] // 3
    tail = slice(segs_up, segs_up + heads_up)
    for i in range(2):
        cols = slice(i * local, (i + 1) * local)
        table = table_own[:segs_up, cols]
        for r in returned:
            table = table + r[:segs_up, cols]
        edge = jnp.where(
            iota((rows, 1), 0) == rows - 1, returned[0][segs_up - 1 : segs_up, cols], 0.0
        )
        d_raw_kv[i] = (base[i] + edge + right_exact_tn(ends[...], table, 2)).astype(bf16)
    own = d_forget_own[...]
    sums = jnp.zeros((heads_up, segs_up), f32)
    for r in returned:
        sums = sums + r[tail, local : local + segs_up]
    d_log = left_exact_nt(own, seen[...]) + left_exact_nt(
        left_exact(sums, anc[...]), onehot[...]
    )
    d_forget = d_log * jax.nn.sigmoid(-lin[:heads_up, :])
    d_bias[...] = jnp.sum(d_forget, axis=1, keepdims=True)
    d_lin[:heads_up, :] = d_forget.astype(bf16)
    d_lin[heads_up:, :] = d_alpha[...].astype(bf16)


def first_gq_kernel(place, d_gq, bundles, out):
    half = d_gq.shape[0] // 2
    part = bundles[0].shape[1]
    local = d_gq.shape[1] // 2
    for k in range(2):
        rows = pl.ds(pl.multiple_of(lax.rem(place[0] + k, 2) * half, 16), half)
        for d, w in enumerate(bundles):
            out[k * half : (k + 1) * half, d * part : (d + 1) * part] = mm_nt(
                d_gq[rows, :local], w[1]
            ) + mm_nt(d_gq[rows, local:], w[0])


def first_share_kernel(place, d_kv, d_lin, kv_w, packs, partial, out, heads_part, *, which):
    half = out.shape[0]
    part = packs[0].shape[1]
    rows = pl.ds(pl.multiple_of(lax.rem(place[0] + which, 2) * half, 16), half)
    for d in range(len(packs)):
        cols = slice(d * part, (d + 1) * part)
        heads_part[...] = mm_tn(d_lin[...], packs[d][:24, :])
        out[:, cols] = (
            mm_nt(d_kv[0, rows, :], kv_w[d][0])
            + mm_nt(d_kv[1, rows, :], kv_w[d][1])
            + heads_part[rows, :]
            + partial[which * half : (which + 1) * half, cols]
        ).astype(out.dtype)


def first_sum_kernel(mine, given, out):
    out[...] = (mine[...] + given[...]).astype(bf16)


def enter_back_kernel(place, tokens, packs, d_middle, total, other, d_own, d_gain):
    shards = len(packs)
    half = total.shape[0]
    rows = pl.ds(pl.multiple_of(place[0] * half, 16), half)
    value = jnp.concatenate(
        [part_at(tokens, place[1], d, shards, rows).astype(f32) for d in range(shards)], axis=1
    )
    d_first = total[...].astype(f32) + other[...].astype(f32)
    d_value, gain = norm_grad(value, rms_scale(value), gain_row(packs, 24), d_first)
    d_gain[...] = gain
    d_own[...] = d_middle[...] + d_value


def settle_kernel(place, mine, theirs, out, *, shards):
    half = mine.shape[0]
    part = mine.shape[1] // shards
    for k, source in enumerate((mine, theirs)):
        rows = pl.ds(pl.multiple_of(lax.rem(place[0] + k, 2) * half, 16), half)
        for d in range(shards):
            cols = slice(d * part, (d + 1) * part)
            if part % 128:
                out[rows, cols] = source[:, cols]
            else:
                start = pl.multiple_of(lax.rem(place[1] + d, shards) * part, 128)
                out[rows, pl.ds(start, part)] = source[:, cols]


def leave_kernel(middle, total, other, out):
    out[...] = (
        middle[...] + (total[...].astype(f32) + other[...].astype(f32))
    ).astype(bf16)


def named(kernel, **fixed):
    def bound(*refs):
        kernel(*refs, **fixed)

    bound.__name__ = kernel.__name__
    return bound


def planes_of(weights):
    rows, count, width = weights.shape
    block = 128 if rows % 128 == 0 else rows

    def planes_kernel(source, out):
        for i in range(count):
            out[i] = source[:, i, :].astype(bf16)

    return pl.pallas_call(
        planes_kernel,
        grid=(rows // block,),
        in_specs=[pl.BlockSpec((block, count, width), lambda j: (j, 0, 0))],
        out_specs=pl.BlockSpec((count, block, width), lambda j: (0, j, 0)),
        out_shape=jax.ShapeDtypeStruct((count, rows, width), bf16),
        compiler_params=pltpu.CompilerParams(vmem_limit_bytes=12 << 20),
        cost_estimate=pl.CostEstimate(flops=1, transcendentals=1, bytes_accessed=1),
        name="planes",
    )(weights)


class At:

    def __init__(self, array, rows=None, cols=None, lead=None):
        if cols and (cols[0] % 128 or cols[1] % 128):
            array, cols = array[..., cols[0] : cols[1]], None
        self.array, self.lead = array, lead
        self.rows = rows or (0, array.shape[-2])
        self.cols = cols or (0, array.shape[-1])

    def spec(self, block=None):
        start, stop = self.rows
        height = stop - start
        first, last = self.cols
        wide = block or last - first
        shape, row, col = (height, wide), start // height, first // wide

        def at(j):
            return (row, col + j if block else col)

        if self.lead is None:
            return pl.BlockSpec(shape, at)
        return pl.BlockSpec((None,) + shape, lambda j: (self.lead,) + at(j))


def weight_grad(order, pairs, got, block):
    count = len(pairs)
    rows = pairs[0][0].cols[1] - pairs[0][0].cols[0]
    width = pairs[0][1].cols[1] - pairs[0][1].cols[0]

    def weight_grad_kernel(*refs):
        total = mm_tn(refs[0][...], refs[1][...])
        for i in range(1, count):
            total = total + mm_tn(refs[2 * i][...], refs[2 * i + 1][...])
        for ref in refs[2 * count : -1]:
            total = total + ref[...].astype(f32)
        refs[-1][...] = total.astype(bf16)

    specs = [spec for a, b in pairs for spec in (a.spec(block), b.spec())]
    over = pl.BlockSpec((block, width), lambda j: (j, 0))
    call = pl.pallas_call(
        weight_grad_kernel,
        grid=(rows // block,),
        in_specs=specs + [over for _ in got],
        out_specs=over,
        out_shape=jax.ShapeDtypeStruct((rows, width), bf16),
        compiler_params=pltpu.CompilerParams(vmem_limit_bytes=20 << 20),
        cost_estimate=pl.CostEstimate(flops=1, transcendentals=1, bytes_accessed=1),
        name="weight_grad",
    )
    return order(call, *[x.array for pair in pairs for x in pair], *got)


def add_rows(left, right):
    rows, width = left.shape
    block = rows if rows % 64 else 64 if rows <= 256 else 128

    def add_kernel(left, right, out):
        out[...] = (left[...].astype(f32) + right[...].astype(f32)).astype(out.dtype)

    over = pl.BlockSpec((block, width), lambda j: (j, 0))
    return pl.pallas_call(
        add_kernel,
        grid=(rows // block,),
        in_specs=[over, over],
        out_specs=over,
        out_shape=jax.ShapeDtypeStruct((rows, width), left.dtype),
        compiler_params=pltpu.CompilerParams(vmem_limit_bytes=8 << 20),
        cost_estimate=pl.CostEstimate(flops=1, transcendentals=1, bytes_accessed=1),
        name="add",
    )(left, right)


def attend_kernel(*refs):
    place, query_ref, *kv_refs, bias_ref, cq_ref, ck_ref, gate_ref, out_ref, gated_ref, lse_ref = refs
    rows = query_ref.shape[0]
    half = rows // 2
    size = query_ref.shape[1] // 2
    key_cols = ck_ref[0].T
    outs = []
    for e in range(2):
        cols = slice(e * size, (e + 1) * size)
        query = query_ref[:, cols]
        forget_row = cq_ref[0, e : e + 1, :]
        total = jnp.zeros((1, rows), f32)
        mixed = jnp.zeros((size, rows), f32)
        for d in range(len(kv_refs) // 2):
            span = slice(d * rows, (d + 1) * rows)
            scores = mm_nt(kv_refs[2 * d][0, :, cols], query)
            scores = scores + (forget_row - key_cols[span, e : e + 1]) + bias_ref[span, :]
            weights = jnp.exp(scores)
            total = total + jnp.sum(weights, axis=0, keepdims=True)
            mixed = mixed + mm_tn(kv_refs[2 * d + 1][0, :, cols], weights.astype(bf16))
        outs.append((mixed / total).T)
        lse_ref[0, e : e + 1, :] = jnp.log(total)
    attended = jnp.concatenate(outs, axis=1)
    out_ref[...] = attended
    gated = (attended * jax.nn.sigmoid(gate_ref[...])).astype(bf16)
    for k in range(2):
        there = pl.ds(pl.multiple_of(lax.rem(place[0] + k, 2) * half, 16), half)
        gated_ref[there, :] = gated[k * half : (k + 1) * half]


def score_grads(key, value, query, d_out, forget_row, delta_row, key_col, bias):
    scores = mm_nt(key, query) + (forget_row - key_col) + bias
    probs = jnp.exp(scores)
    d_scores = probs * (mm_nt(value, d_out) - delta_row)
    return probs.astype(bf16), d_scores.astype(bf16)


def first_col(rows, size):
    return jnp.where(iota((rows, size), 1) == 0, 1.0, 0.0).astype(bf16)


def as_rows(columns):
    pad = jnp.zeros((columns[0].shape[0], 8 - len(columns)), f32)
    return jnp.concatenate(columns + [pad], axis=1).T


def query_grads_kernel(*refs):
    query_ref, d_out_ref, row_values = refs[:3]
    kv_refs = refs[3:-6]
    bias_ref, ck_ref, d_query_ref, d_kv_ref, dcq_ref, dck_ref = refs[-6:]
    rows = query_ref.shape[0]
    size = query_ref.shape[1] // 2
    key_cols = ck_ref[0].T
    forget8, delta8 = rows_back(row_values, 0), rows_back(row_values, 24)
    sums = []
    for e in range(2):
        cols = slice(e * size, (e + 1) * size)
        head = 2 * pl.program_id(0) + e
        query = query_ref[:, cols]
        d_out = d_out_ref[:, cols]
        forget_row, delta_row = head_row(forget8, head), head_row(delta8, head)
        d_query = jnp.zeros((rows, size), f32)
        d_row = jnp.zeros((1, rows), f32)
        for d in range(len(kv_refs) // 2):
            span = slice(d * rows, (d + 1) * rows)
            key = kv_refs[2 * d][0, :, cols]
            probs, d_scores = score_grads(
                key,
                kv_refs[2 * d + 1][0, :, cols],
                query,
                d_out,
                forget_row,
                delta_row,
                key_cols[span, e : e + 1],
                bias_ref[span, :],
            )
            d_query = d_query + mm_tn(d_scores, key)
            d_row = d_row + jnp.sum(d_scores.astype(f32), axis=0, keepdims=True)
            if d == 0:
                found = mm(d_scores, jnp.concatenate([query, first_col(rows, size)], axis=1))
                sums.append(found[:, size : size + 1])
                d_kv_ref[0, :, cols] = found[:, :size]
                d_kv_ref[1, :, cols] = mm(probs, d_out)
        d_query_ref[:, cols] = d_query * (size ** (-0.5))
        dcq_ref[0, e : e + 1, :] = d_row
    dck_ref[0] = as_rows(sums)


def key_grads_kernel(*refs):
    key_ref, value_ref, bias_ref, ck_ref, own_ref, own_dck_ref = refs[:6]
    sets = refs[6:-2]
    d_kv_ref, dck_ref = refs[-2:]
    count = len(sets) // 3
    rows = key_ref.shape[1]
    size = key_ref.shape[2] // 2
    key_cols = ck_ref[0].T
    forget8 = [rows_back(sets[3 * d + 2], 0) for d in range(count)]
    delta8 = [rows_back(sets[3 * d + 2], 24) for d in range(count)]
    sums = []
    for e in range(2):
        cols = slice(e * size, (e + 1) * size)
        head = 2 * pl.program_id(0) + e
        key, value = key_ref[0, :, cols], value_ref[0, :, cols]
        d_key = jnp.zeros((rows, 2 * size), f32)
        d_value = jnp.zeros((rows, size), f32)
        for d in range(count):
            query, d_out = sets[3 * d][:, cols], sets[3 * d + 1][:, cols]
            probs, d_scores = score_grads(
                key,
                value,
                query,
                d_out,
                head_row(forget8[d], head),
                head_row(delta8[d], head),
                key_cols[:, e : e + 1],
                bias_ref[d * rows : (d + 1) * rows, :],
            )
            d_key = d_key + mm(
                d_scores, jnp.concatenate([query, first_col(rows, size)], axis=1)
            )
            d_value = d_value + mm(probs, d_out)
        sums.append(d_key[:, size : size + 1])
        d_kv_ref[0, :, cols] = own_ref[0, :, cols] + d_key[:, :size]
        d_kv_ref[1, :, cols] = own_ref[1, :, cols] + d_value
    dck_ref[0] = own_dck_ref[0] + as_rows(sums)


def kv_specs(blocks, lanes):
    rows = blocks[0].shape[1]
    return [
        pl.BlockSpec((1, rows, lanes), lambda p, kind=kind: (kind, 0, p))
        for _ in blocks
        for kind in range(2)
    ]


def twice(blocks):
    return [b for b in blocks for _ in range(2)]


def attention(place, query, kv_blocks, bias, forget_q, forget_k, raw_g):
    rows, local = query.shape
    pairs = forget_q.shape[0]
    keys = bias.shape[0]
    lanes = local // pairs
    flat = pl.BlockSpec((rows, lanes), lambda p: (0, p))
    row_spec = pl.BlockSpec((1, 8, rows), lambda p: (p, 0, 0))
    return pl.pallas_call(
        attend_kernel,
        grid=(pairs,),
        in_specs=[pl.BlockSpec(memory_space=pltpu.SMEM), flat]
        + kv_specs(kv_blocks, lanes)
        + [
            pl.BlockSpec((keys, rows), lambda p: (0, 0)),
            row_spec,
            pl.BlockSpec((1, 8, keys), lambda p: (p, 0, 0)),
            flat,
        ],
        out_specs=[flat, flat, row_spec],
        out_shape=[
            jax.ShapeDtypeStruct((rows, local), f32),
            jax.ShapeDtypeStruct((rows, local), bf16),
            jax.ShapeDtypeStruct((pairs, 8, rows), f32),
        ],
        compiler_params=pltpu.CompilerParams(vmem_limit_bytes=20 << 20),
        cost_estimate=pl.CostEstimate(flops=1, transcendentals=1, bytes_accessed=1),
        name="attend",
    )(place, query, *twice(kv_blocks), bias, forget_q, forget_k, raw_g)


def message_specs(rows, lanes, width):
    return [
        pl.BlockSpec((rows, lanes), lambda p: (0, p)),
        pl.BlockSpec((row_room, width), lambda p: (rows // row_room, 0)),
    ]


def back_params():
    return {
        "compiler_params": pltpu.CompilerParams(vmem_limit_bytes=20 << 20),
        "cost_estimate": pl.CostEstimate(flops=1, transcendentals=1, bytes_accessed=1),
    }


def query_grads(own_query, own_out, kv_blocks, bias, forget_k):
    keys, rows = bias.shape
    local = own_query.shape[1]
    pairs = forget_k.shape[0]
    lanes = local // pairs
    flat, row_block = message_specs(rows, lanes, local)
    row_spec = pl.BlockSpec((1, 8, rows), lambda p: (p, 0, 0))
    return pl.pallas_call(
        query_grads_kernel,
        grid=(pairs,),
        in_specs=[flat, flat, row_block]
        + kv_specs(kv_blocks, lanes)
        + [
            pl.BlockSpec((keys, rows), lambda p: (0, 0)),
            pl.BlockSpec((1, 8, keys), lambda p: (p, 0, 0)),
        ],
        out_specs=[
            flat,
            pl.BlockSpec((2, rows, lanes), lambda p: (0, 0, p)),
            row_spec,
            row_spec,
        ],
        out_shape=[
            jax.ShapeDtypeStruct((rows, local), f32),
            jax.ShapeDtypeStruct((2, rows, local), f32),
            jax.ShapeDtypeStruct((pairs, 8, rows), f32),
            jax.ShapeDtypeStruct((pairs, 8, rows), f32),
        ],
        name="query_grads",
        **back_params(),
    )(own_query, own_out, own_out, *twice(kv_blocks), bias, forget_k)


def key_grads(own_kv, later, forget_k, own_grads, own_dck, queries, outs):
    rows, local = own_kv.shape[1:]
    pairs = forget_k.shape[0]
    lanes = local // pairs
    flat, row_block = message_specs(rows, lanes, local)
    row_spec = pl.BlockSpec((1, 8, rows), lambda p: (p, 0, 0))
    pair_spec = pl.BlockSpec((2, rows, lanes), lambda p: (0, 0, p))
    return pl.pallas_call(
        key_grads_kernel,
        grid=(pairs,),
        in_specs=kv_specs([own_kv], lanes)
        + [pl.BlockSpec(later.shape, lambda p: (0, 0)), row_spec, pair_spec, row_spec]
        + [flat, flat, row_block] * len(queries),
        out_specs=[pair_spec, row_spec],
        out_shape=[
            jax.ShapeDtypeStruct((2, rows, local), f32),
            jax.ShapeDtypeStruct((pairs, 8, rows), f32),
        ],
        name="key_grads",
        **back_params(),
    )(
        own_kv,
        own_kv,
        later,
        forget_k,
        own_grads,
        own_dck,
        *[x for q, o in zip(queries, outs) for x in (q, o, o)],
    )


def small_kernel(d_lin, first_in, gains, other, gain_q, gain_k, d_bias, *outs):
    part = first_in.shape[1] // len(outs)
    local = gain_q.shape[1]
    for d, out in enumerate(outs):
        cols = slice(d * part, (d + 1) * part)
        out[...] = jnp.zeros_like(out)
        out[:24, :part] = mm(d_lin[...], first_in[:, cols])
        out[24:26, :part] = gains[:, cols] + other[:, cols]
        out[26:27, :local] = gain_q[...]
        out[27:28, :local] = gain_k[...]
        out[32:40, :1] = d_bias[...]


def pieces_kernel(place, *refs):
    out = refs[-1]
    count = len(refs) - 1
    rows = refs[0].shape[0]
    for k, piece in enumerate(refs[:count]):
        start = pl.multiple_of(lax.rem(place[2] + k, count) * rows, 16)
        out[pl.ds(start, rows), :] = piece[...]


class Order:

    def __init__(self):
        self.last, self.held = None, []

    def tied(self, *args):
        if self.last is not None:
            args, _, _ = lax.optimization_barrier((args, self.last, self.held))
        self.held = []
        return args

    def hold(self, values):
        self.held.append(values)

    def __call__(self, work, *args):
        found = work(*self.tied(*args))
        self.last = min(jax.tree.leaves(found), key=nbytes)
        return found


class LineSum:

    def __init__(self, order, values):
        self.order, self.total = order, values
        self.count = lax.axis_size("ctx")
        self.half = self.count // 2
        self.hop, self.coming = 0, None
        self.send()

    def send(self):
        k, count, half = self.hop, self.count, self.half
        if k < half - 1:
            pairs = [(k, k + 1), (count - 1 - k, count - 2 - k)]
        elif k == half - 1:
            pairs = [(half - 1, half), (half, half - 1)]
        elif k < 2 * half - 1:
            j = 2 * half - 2 - k
            pairs = [(j + 1, j), (count - 2 - j, count - 1 - j)]
        else:
            return
        self.coming = lax.ppermute(self.total, "ctx", pairs)

    def step(self):
        k, half = self.hop, self.half
        self.hop += 1
        if k < half:
            self.total = self.order(add_rows, self.total, self.coming)
            self.coming = None
        elif k < 2 * half - 2:
            j = 2 * half - 2 - k
            index = lax.axis_index("ctx")
            at_ends = (index == j) | (index == self.count - 1 - j)
            self.total = self.order(
                lambda a, b: jnp.where(at_ends, b, a), self.total, self.coming
            )
            self.coming = None
        else:
            self.order.hold(self.coming)
            return
        self.send()

    def finish(self):
        while self.hop < 2 * self.half - 1:
            self.step()
        return self.total, self.coming


def spread_out(order, place, planes):
    sums = [s.finish() for plane in planes for s in plane]
    arrays = [x for pair in sums for x in pair if x is not None]
    each = len(arrays) // len(sums)
    height, width = planes[0][0].total.shape
    chunks = len(planes[0])
    block = 128 if height % 128 == 0 else height
    steps = height // block
    count = lax.axis_size("ctx")

    def spread_out_kernel(place, *refs):
        out = refs[-1]
        at_ends = (place[2] == 0) | (place[2] == count - 1)
        for c in range(chunks):

            @pl.when(pl.program_id(0) // steps == c)
            def _():
                for i in range(len(planes)):
                    first = (i * chunks + c) * each
                    value = refs[first][...].astype(f32)
                    if each > 1:
                        value = jnp.where(at_ends, refs[first + 1][...].astype(f32), value)
                    if len(planes) > 1:
                        out[:, i, :] = value
                    else:
                        out[...] = value

    def spec(c):
        return pl.BlockSpec(
            (block, width), lambda j: (jnp.clip(j - c * steps, 0, steps - 1), 0)
        )

    specs = [spec(c) for _ in planes for c in range(chunks) for _ in range(each)]
    middle = (len(planes),) if len(planes) > 1 else ()
    call = pl.pallas_call(
        spread_out_kernel,
        grid=(chunks * steps,),
        in_specs=[pl.BlockSpec(memory_space=pltpu.SMEM)] + specs,
        out_specs=pl.BlockSpec((block, *middle, width), lambda j: (j, *(0 for _ in middle), 0)),
        out_shape=jax.ShapeDtypeStruct((chunks * height, *middle, width), f32),
        compiler_params=pltpu.CompilerParams(vmem_limit_bytes=24 << 20),
        cost_estimate=pl.CostEstimate(flops=1, transcendentals=1, bytes_accessed=1),
        name="spread_out",
    )
    return order(call, place, *arrays)


schedule = (
    "bs1", "G10", "ms1", "bs2", "ms2", "G00", "q1", "D10", "mb", "G11", "q2", "U10", "D00", "lv",
    "O0", "gb", "aq", "U00", "G12", "qb", "q3", "D01", "ak", "sb", "U11", "D02", "G01", "G13",
    "so", "rb", "fgq", "Qg1", "O1", "U12", "D03", "G1h", "D11", "G02", "K1", "U13", "V1", "Qg2",
    "D0h", "O2", "G03", "fs2", "U01", "U1h", "Qg3", "fs1", "K2", "G0h", "O3", "D12", "Qq1", "Qgh",
    "fsum", "K3", "Oh", "U02", "D13", "eb", "Kh", "Qq2", "U03", "D1h", "V2", "sm", "Qq3", "df",
    "st", "U0h", "sm1", "V3", "of", "Qqh", "sm2", "gu", "sm3", "Vh", "at", "smf",
)


def body(
    tokens,
    seg_parents,
    seg_offsets,
    tok_seg,
    norm_gain,
    w_attn,
    w_heads,
    forget_bias,
    qk_gain,
    w_out,
    w_gate_up,
    w_down,
    cotangent,
):
    shards = lax.axis_size("shard")
    ctxs = lax.axis_size("ctx")
    ctx = lax.axis_index("ctx")
    tps = lax.axis_size("tp")
    rows, width = tokens.shape[1:]
    half = rows // 2
    part = width // shards
    local = w_attn.shape[2]
    heads = w_heads.shape[2]
    heads_up = 8
    size = local // heads
    hidden_size = w_gate_up.shape[2]
    segs = seg_parents.shape[1]
    order = Order()
    place = jnp.stack(
        [lax.axis_index("tp") % 2, lax.axis_index("shard"), ctx]
    ).astype(jnp.int32)

    def gathered(piece):
        return [piece] + [from_ring(piece, "shard", d) for d in range(1, shards)]

    def owned(piece):
        return [piece[:, :part]] + [
            from_ring(piece[:, part * (shards - d) : part * (shards - d + 1)], "shard", d)
            for d in range(1, shards)
        ]

    def crossed(total):
        bit = 2
        other = partner(total, "tp", bit)
        while bit * 2 < tps:
            total = (total.astype(f32) + other.astype(f32)).astype(bf16)
            bit = bit * 2
            other = partner(total, "tp", bit)
        return total, other

    def pack_small(w, gain):
        table = jnp.pad(
            jnp.transpose(w, (1, 2, 0)), ((0, 0), (0, heads_up - heads), (0, 0))
        ).reshape(3 * heads_up, part)
        return jnp.concatenate([table, jnp.pad(gain, ((0, 6), (0, 0)))], axis=0).astype(bf16)

    packs = gathered(order(pack_small, w_heads, norm_gain))
    attn_b = order(lambda w: jnp.transpose(w, (1, 0, 2)).astype(bf16), w_attn)
    piece_rows = hidden_size // ctxs
    piece = order(
        lambda w: lax.dynamic_slice_in_dim(w, ctx * piece_rows, piece_rows, 0).astype(bf16), w_down
    )
    pieces = [from_ring(piece, "shard", d) for d in range(1, shards)]
    kv_w = gathered(order(lambda w: w[1:3], attn_b))
    padded = jnp.full((segs_up - segs,), -1, jnp.int32)
    low = jnp.concatenate([seg_offsets[0, :segs], padded])
    high = jnp.concatenate([seg_offsets[0, 1:], padded])
    parents = jnp.concatenate([seg_parents[0], padded])
    bias, later, seen, key_anc, onehot, parent, start, ends, anc, _ = order(
        lambda *a: whole(
            masks_kernel,
            [
                ((rows * ctxs, rows), f32),
                ((rows * (ctxs - 1), rows), f32),
                ((rows, rows), f32),
                ((rows * ctxs, segs_up), f32),
                ((rows, segs_up), f32),
                ((rows, segs_up), f32),
                ((rows, 1), f32),
                ((segs_up, rows), f32),
                ((segs_up, segs_up), f32),
                ((rows * ctxs, segs_up), f32),
            ],
            *a,
        ),
        place,
        low[None],
        high[None],
        high[:, None],
        parents[:, None],
        tok_seg[0][:, None],
    )
    tree, cotangent = tokens[0], cotangent[0]
    if part % 128:
        tree = turned(tree, place[1], shards)
        cotangent = turned(cotangent, place[1], shards)

    def settled(values):
        return turned(values, shards - place[1], shards) if part % 128 else values

    for p in pieces:
        order.hold(p)
    (first_in,) = order(
        lambda *a: whole(enter_kernel, [((rows, width), bf16)], *a), place, tree, packs
    )
    pieces = order.tied(*pieces)
    piece_sets = [[p] + [from_ring(p, "ctx", k) for k in range(1, ctxs)] for p in pieces]
    bundles = gathered(
        order(lambda a, w: jnp.stack([a[0], a[3], w.T.astype(bf16)]), attn_b, w_out)
    )
    gateup_w = gathered(
        order(planes_of, w_gate_up)
    )

    own_down = order(lambda w: w.astype(bf16), w_down)

    forget_col = jnp.pad(forget_bias, (0, heads_up - heads))[:, None]
    raw_kv, lin, message = order(
        lambda *a: whole(
            keys_in_kernel,
            [
                ((2, rows, local), f32),
                ((3 * heads_up, rows), f32),
                ((segs_up + heads_up, 2 * local), f32),
            ],
            *a,
        ),
        first_in,
        kv_w,
        packs,
        forget_col,
        seen,
        onehot,
        ends,
    )
    order.hold(piece_sets)
    blocks = [message] + [along(message, "ctx", d) for d in range(1, ctxs)]
    gain_q, gain_k = qk_gain[:1], qk_gain[1:]
    own_kv, delta, forget_q, forget_k = order(
        lambda *a: whole(
            named(keys_shift_kernel, size=size),
            [
                ((2, rows, local), bf16),
                ((2, rows, local), f32),
                ((heads // 2, 8, rows), f32),
                ((heads // 2, 8, rows * ctxs), f32),
            ],
            *a,
        ),
        raw_kv,
        lin,
        blocks,
        parent,
        start,
        key_anc,
        gain_k,
    )
    kv_blocks = [own_kv] + [along(own_kv, "ctx", d) for d in range(1, ctxs)]
    down_w = [own_down] + [
        order(
            lambda *a: whole(pieces_kernel, [((hidden_size, part), bf16)], *a)[0], place, *p
        )
        for p in piece_sets
    ]
    grad_out, d_hidden = order(
        lambda *a: whole(
            grad_hidden_kernel, [((rows, width), bf16), ((rows, hidden_size), f32)], *a
        ),
        place,
        cotangent,
        down_w,
    )
    raw_q, query, raw_g = order(
        lambda *a: whole(
            named(queries_kernel, size=size),
            [((rows, local), f32), ((rows, local), bf16), ((rows, local), f32)],
            *a,
        ),
        first_in,
        bundles,
        gain_q,
    )
    attended, gated, lse = order(
        attention, place, query, kv_blocks, bias, forget_q, forget_k, raw_g
    )

    (share,) = order(
        lambda *a: whole(attn_share_kernel, [((half, width), f32)], *a), gated, bundles
    )
    given = partner(share, "tp", 1)
    (total,) = order(
        lambda *a: whole(attn_share_sum_kernel, [((half, width), bf16)], *a),
        gated,
        bundles,
        given,
    )
    total, other = crossed(total)
    middle, second = order(
        lambda *a: whole(
            middle_kernel, [((half, width), f32), ((half, width), bf16)], *a
        ),
        place,
        tree,
        packs,
        total,
        other,
    )
    second_too = partner(second, "tp", 1)
    hidden, d_lin, keep, give = order(mlp, second, second_too, gateup_w, d_hidden)
    first_parts = owned(order.tied(first_in)[0])

    at = {}
    hidden_half, part_half = hidden_size // 2, part // 2

    def core_sum(name, kernel, out, *args):
        def run(given):
            (at[name],) = order(
                lambda *a: whole(kernel, [((half, width), out)], *a), *args, *given
            )

        return run

    def shared(kernel, *args):
        (share,) = order(lambda *a: whole(kernel, [((half, width), f32)], *a), *args)
        return partner(share, "tp", 1)

    def total_of(kernel, *args):
        (total,) = order(lambda *a: whole(kernel, [((half, width), bf16)], *a), *args)
        return crossed(total)

    def rows_at(k):
        return (k * half, (k + 1) * half)

    def out_part(d, got=()):
        return weight_grad(
            order,
            [
                (At(gated, rows=rows_at(k)), At(x, cols=(d * part, (d + 1) * part)))
                for k, x in enumerate((at["mb"], at["mb_too"]))
            ],
            got,
            min(128, local),
        )

    def summed(left_ones, right_ones, block, cols=None, lead=None, right_cols=None):
        return LineSum(
            order,
            weight_grad(
                order,
                [
                    (At(a, cols=cols), At(b, lead=lead, cols=right_cols))
                    for a, b in zip(left_ones, right_ones)
                ],
                (),
                block,
            ),
        )

    def run_bs1():
        at["bs1"] = partner(order.tied(give)[0], "tp", 1)

    def run_bs2():
        (total,) = order(
            lambda *a: whole(first_sum_kernel, [(keep.shape, bf16)], *a), keep, at["bs1"]
        )
        at["bs2"] = crossed(total)

    def column_part(d, start, stop):
        return (d * part + start, d * part + stop)

    def down_part(i, d, got=()):
        return weight_grad(
            order,
            [
                (
                    At(hidden, cols=(i * hidden_half, (i + 1) * hidden_half)),
                    At(grad_out, cols=column_part(d, 0, part)),
                )
            ],
            got,
            256,
        )

    def lin_part(lead, i, d, got=()):
        return weight_grad(
            order,
            [
                (
                    At(x, cols=column_part(d, i * part_half, (i + 1) * part_half)),
                    At(d_lin, rows=rows_at(k), lead=lead),
                )
                for k, x in enumerate((second, second_too))
            ],
            got,
            min(128, part_half),
        )

    def run_ms1():
        at["ms1"] = shared(named(share_kernel, which=1), hidden, down_w)

    def run_ms2():
        at["ms2"] = total_of(share_sum_kernel, hidden, down_w, at["ms1"])

    def run_mb():
        at["d_middle"], at["mb"], at["gain_two"] = order(
            lambda *a: whole(
                middle_back_kernel,
                [((half, width), f32), ((half, width), bf16), ((1, width), f32)],
                *a,
            ),
            grad_out,
            packs,
            middle,
            *at["bs2"],
        )
        at["mb_too"] = partner(at["mb"], "tp", 1)

    def run_gb():
        at["out_message"], at["d_raw_g"] = order(
            lambda *a: whole(
                named(gate_back_kernel, size=size),
                [((rows + row_room, local), bf16), ((rows, local), bf16)],
                *a,
            ),
            place,
            at["mb"],
            at["mb_too"],
            bundles,
            raw_g,
            attended,
            forget_q,
            lse,
        )
        at["later_outs"] = [along(at["out_message"], "ctx", -d) for d in range(1, ctxs)]

    def run_q(d):
        passed = at["queries"][-1] if d > 1 else query
        passed = order.tied(passed)[0]
        pairs = [(i, i - 1) for i in range(1, ctxs - d + 1)]
        at.setdefault("queries", []).append(lax.ppermute(passed, "ctx", pairs))

    def run_aq():
        order.hold(first_parts[1:])
        at["d_query"], at["own_grads"], at["dcq"], at["own_dck"] = order(
            query_grads, query, at["out_message"], kv_blocks, bias, forget_k
        )

    def run_ak():
        at["d_kv"], at["dck"] = order(
            key_grads,
            own_kv,
            later,
            forget_k,
            at["own_grads"],
            at["own_dck"],
            at["queries"],
            at["later_outs"],
        )

    def run_qb():
        at["d_gq"], at["gain_q"] = order(
            lambda *a: whole(
                named(query_back_kernel, size=size),
                [((rows, 2 * local), bf16), ((1, local), f32)],
                *a,
            ),
            raw_q,
            at["d_query"],
            gain_q,
            at["d_raw_g"],
        )
        at["gq"] = gathered(at["d_gq"])

    def run_fgq():
        (at["fgq"],) = order(
            lambda *a: whole(first_gq_kernel, [((rows, width), f32)], *a),
            place,
            at["d_gq"],
            bundles,
        )

    def run_sb():
        at["base"], at["message"], at["d_alpha"], at["gain_k"], at["d_forget"] = order(
            lambda *a: whole(
                named(shift_back_kernel, size=size),
                [
                    ((2, rows, local), f32),
                    ((segs_up + heads_up, 2 * local), f32),
                    ((2 * heads_up, rows), f32),
                    ((1, local), f32),
                    ((heads_up, rows), f32),
                ],
                *a,
            ),
            at["d_kv"],
            raw_kv,
            delta,
            lin,
            gain_k,
            start,
            parent,
            at["dcq"],
            at["dck"],
            onehot,
        )
        at["returned"] = [along(at["message"], "ctx", -d) for d in range(1, ctxs)]

    def run_rb():
        at["d_raw_kv"], at["d_head"], at["d_bias"] = order(
            lambda *a: whole(
                raw_back_kernel,
                [((2, rows, local), bf16), ((3 * heads_up, rows), bf16), ((heads_up, 1), f32)],
                *a,
            ),
            at["base"],
            at["message"],
            at["returned"],
            ends,
            seen,
            onehot,
            anc,
            lin,
            at["d_forget"],
            at["d_alpha"],
        )
        at["kv"] = gathered(at["d_raw_kv"])

    def first_share(which):
        return order(
            lambda *a: whole(
                named(first_share_kernel_of(part, rows), which=which), [((half, width), f32)], *a
            )[0],
            place,
            at["d_raw_kv"],
            at["d_head"],
            kv_w,
            packs,
            at["fgq"],
        )

    def run_fs1():
        at["fs1"] = partner(first_share(1), "tp", 1)

    def run_fs2():
        at["fs2"] = first_share(0)

    def run_fsum():
        at["fsum"] = total_of(first_sum_kernel, at["fs2"], at["fs1"])

    def run_eb():
        at["eb"], gain_one = order(
            lambda *a: whole(
                enter_back_kernel, [((half, width), f32), ((1, width), f32)], *a
            ),
            place,
            tree,
            packs,
            at["d_middle"],
            *at["fsum"],
        )
        at["eb_too"] = partner(at["eb"], "tp", 1)
        at["gains"] = jnp.concatenate([gain_one, at["gain_two"]], axis=0)
        at["gains_too"] = partner(at["gains"], "tp", 1)

    def settle(name, kind):
        (at[name],) = order(
            lambda *a: whole(named(settle_kernel, shards=shards), [((rows, width), kind)], *a),
            place,
            at[name],
            at[name + "_too"],
        )

    def run_lv():
        (at["lv"],) = order(
            lambda *a: whole(leave_kernel, [((half, width), bf16)], *a), middle, *at["ms2"]
        )
        at["lv_too"] = partner(at["lv"], "tp", 1)

    def run_sm():
        at["sm"] = order(
            lambda *a: whole(
                small_kernel, [((40, max(part, local)), f32) for _ in range(shards)], *a
            ),
            at["d_head"],
            first_in,
            at["gains"],
            at["gains_too"],
            at["gain_q"],
            at["gain_k"],
            at["d_bias"],
        )
        at["sm_got"] = [from_ring(at["sm"][d], "shard", shards - d) for d in range(1, shards)]

    def run_sm1():
        small = at["sm"][0]
        for got in at["sm_got"]:
            small = order(add_rows, small, got)
        at["small"] = LineSum(order, small)

    def run_smf():
        line = at["small"]
        line.step()

        def pick(total, *ends):
            if ends:
                total = jnp.where((ctx == 0) | (ctx == ctxs - 1), ends[0], total)
            table = total[: 3 * heads_up, :part].reshape(3, heads_up, part)[:, :heads]
            return (
                total[24:26, :part],
                jnp.transpose(table, (2, 0, 1)),
                total[32 : 32 + heads, 0],
                total[26:28, :local],
            )

        ends = [line.coming] if line.coming is not None else []
        found = order(pick, line.total, *ends)
        at["small_gain"], at["small_heads"], at["small_bias"], at["small_qk"] = found

    def run_out(name, *planes):
        at[name] = spread_out(order, place, [[at[n] for n in plane] for plane in planes])

    block = min(128, part)
    work = {
        "bs1": run_bs1, "bs2": run_bs2,
        "ms1": run_ms1, "ms2": run_ms2, "mb": run_mb, "gb": run_gb,
        "q1": lambda: run_q(1), "q2": lambda: run_q(2),
        "q3": lambda: [run_q(d) for d in range(3, ctxs)], "aq": run_aq, "ak": run_ak, "qb": run_qb, "fgq": run_fgq,
        "sb": run_sb, "rb": run_rb, "fs1": run_fs1, "fs2": run_fs2, "fsum": run_fsum,
        "eb": run_eb, "st": lambda: settle("eb", f32), "lv": run_lv,
        "so": lambda: settle("lv", bf16), "sm": run_sm, "sm1": run_sm1, "smf": run_smf,
        "gu": lambda: run_out("gu", ("G0", "G1"), ("U0", "U1")),
        "df": lambda: run_out("df", ("D0", "D1")), "of": lambda: run_out("of", ("O",)),
        "at": lambda: run_out("at", ("Qq",), ("K",), ("V",), ("Qg",)),
    }
    starts = {
        "Qg1": lambda: summed(first_parts, at["gq"], block, right_cols=(0, local)),
        "Qq1": lambda: summed(first_parts, at["gq"], block, right_cols=(local, 2 * local)),
        "K1": lambda: summed(first_parts, at["kv"], block, lead=0),
        "V1": lambda: summed(first_parts, at["kv"], block, lead=1),
    }
    makes = {"O": out_part}
    for i in range(2):
        makes[f"D{i}"] = functools.partial(down_part, i)
        for lead, name in enumerate("GU"):
            makes[f"{name}{i}"] = functools.partial(lin_part, lead, i)
    for name, make in makes.items():

        def hand_over(name=name, make=make):
            at[name + "0"] = [
                from_ring(make(d), "shard", shards - d) for d in range(1, shards)
            ]

        work[name + "0"] = hand_over
        starts[name + "1"] = lambda name=name, make=make: LineSum(
            order, make(0, at[name + "0"])
        )
    for name in schedule:
        if name in work:
            work[name]()
        elif name in starts:
            at[name[:-1]] = starts[name]()
        else:
            at["small" if name[:2] == "sm" else name[:-1]].step()
    return (
        settled(at["lv"])[None],
        settled(at["eb"])[None],
        at["small_gain"],
        at["at"],
        at["small_heads"],
        at["small_bias"],
        at["small_qk"],
        at["of"],
        at["gu"],
        at["df"],
    )


def first_share_kernel_of(part, rows):
    def first_share_scoped_kernel(*refs, which):
        pl.run_scoped(
            lambda scratch: first_share_kernel(*refs, scratch, which=which),
            pltpu.VMEM((rows, part), f32),
        )

    return first_share_scoped_kernel


def solution(mesh):
    in_specs = (
        P("shard", "ctx", None),
        P("shard", None),
        P("shard", None),
        P("shard", "ctx"),
        P(None, "shard"),
        P("shard", None, "tp"),
        P("shard", None, "tp"),
        P("tp"),
        P(None, "tp"),
        P("tp", "shard"),
        P("shard", None, "tp"),
        P("tp", "shard"),
        P("shard", "ctx", None),
    )
    out_specs = (
        P("shard", "ctx", None),
        P("shard", "ctx", None),
        P(None, "shard"),
        P("shard", None, "tp"),
        P("shard", None, "tp"),
        P("tp"),
        P(None, "tp"),
        P("tp", "shard"),
        P("shard", None, "tp"),
        P("tp", "shard"),
    )
    return jax.shard_map(body, mesh=mesh, in_specs=in_specs, out_specs=out_specs, check_vma=False)
```

```python
import functools

import jax
import jax.numpy as jnp
from jax import lax
from jax.experimental import pallas as pl
from jax.experimental.pallas import tpu as pltpu
from jax.sharding import PartitionSpec as P

epsilon = 1e-06
neg_large = -1e30
f32 = jnp.float32
bf16 = jnp.bfloat16
segs_up = 16


def from_ring(values, axis, step):
    count = lax.axis_size(axis)
    return lax.ppermute(values, axis, [((i + step) % count, i) for i in range(count)])


def along(values, axis, step):
    count = lax.axis_size(axis)
    return lax.ppermute(
        values, axis, [(i, i + step) for i in range(count) if 0 <= i + step < count]
    )


def partner(values, axis, bit):
    count = lax.axis_size(axis)
    return lax.ppermute(values, axis, [(i, i ^ bit) for i in range(count)])


def dot_of(dims, precision=None):
    def product(left, right):
        return lax.dot_general(
            left, right, (dims, ((), ())), precision=precision, preferred_element_type=f32
        )

    return product


mm = dot_of(((1,), (0,)))
mm_nt = dot_of(((1,), (1,)))
mm_tn = dot_of(((0,), (0,)))


def bf16_pieces(values, count):
    pieces = []
    for _ in range(count - 1):
        pieces.append(values.astype(bf16))
        values = values - pieces[-1].astype(f32)
    return pieces + [values.astype(bf16)]


def exact_by(product, side):
    def exactly(left, right, count=3):
        if side == 0:
            right = right.astype(bf16)
            return sum(product(p, right) for p in bf16_pieces(left, count))
        left = left.astype(bf16)
        return sum(product(left, p) for p in bf16_pieces(right, count))

    return exactly


left_exact, left_exact_nt, left_exact_tn = (exact_by(p, 0) for p in (mm, mm_nt, mm_tn))
right_exact, right_exact_nt, right_exact_tn = (exact_by(p, 1) for p in (mm, mm_nt, mm_tn))


def rms_scale(values):
    return lax.rsqrt(jnp.mean(values * values, axis=-1, keepdims=True) + epsilon)


def norm_grad(values, scale, gain_row, d_result):
    normed = values * scale
    d_normed = d_result * gain_row
    d_values = scale * (d_normed - normed * jnp.mean(d_normed * normed, axis=-1, keepdims=True))
    return d_values, jnp.sum(d_result * normed, axis=0, keepdims=True)


def iota(shape, axis):
    return lax.broadcasted_iota(jnp.int32, shape, axis)


def same_head(width, size):
    return jnp.where(iota((width, width), 0) // size == iota((width, width), 1) // size, 1.0, 0.0)


def head_mean(values, size):
    return left_exact(values, same_head(values.shape[1], size), 2) * (1.0 / size)


def head_scale(values, size):
    return lax.rsqrt(head_mean(values * values, size) + epsilon)


def head_grad(values, gain_row, d_result, size):
    scale = head_scale(values, size)
    normed = values * scale
    d_normed = d_result * gain_row
    d_values = scale * (d_normed - normed * head_mean(d_normed * normed, size))
    return d_values, jnp.sum(d_result * normed, axis=0, keepdims=True)


def spread_of(heads_up, width, size):
    return jnp.where(iota((heads_up, width), 0) == iota((heads_up, width), 1) // size, 1.0, 0.0)


def nbytes(leaf):
    return leaf.size * leaf.dtype.itemsize


def whole(kernel, outs, *args, extra=8):
    leaves, form = jax.tree.flatten(args)

    def flat(*refs):
        kernel(*jax.tree.unflatten(form, refs[: len(leaves)]), *refs[len(leaves) :])

    shapes = [jax.ShapeDtypeStruct(shape, kind) for shape, kind in outs]
    spaces = [
        pltpu.SMEM if leaf.ndim == 1 and leaf.dtype == jnp.int32 else pltpu.VMEM
        for leaf in leaves
    ]
    size = sum(nbytes(x) for x in leaves) + sum(nbytes(x) for x in shapes)
    found = pl.pallas_call(
        flat,
        out_shape=shapes,
        in_specs=[pl.BlockSpec(memory_space=s) for s in spaces],
        out_specs=[pl.BlockSpec(memory_space=pltpu.VMEM) for _ in shapes],
        compiler_params=pltpu.CompilerParams(
            vmem_limit_bytes=min(60 << 20, size + size // 4 + (extra << 20))
        ),
        cost_estimate=pl.CostEstimate(flops=1, transcendentals=1, bytes_accessed=1),
        name=kernel.__name__,
    )(*leaves)
    return found


def masks_kernel(place, low, high, high_col, parents_col, seg_col, bias, later, seen, key_anc, onehot, parent, start, ends, anc, key_onehot):
    rows = seg_col.shape[0]
    ctx = place[2]
    lanes = iota((segs_up, segs_up), 1)
    parent_mat = jnp.where(parents_col[...] == lanes, 1.0, 0.0)
    eye = jnp.where(iota((segs_up, segs_up), 0) == lanes, 1.0, 0.0)
    ancestry = eye + parent_mat + right_exact(parent_mat, parent_mat, 1)
    anc[...] = ancestry
    mine = jnp.where(seg_col[...] == iota((rows, segs_up), 1), 1.0, 0.0)
    onehot[...] = mine
    parent[...] = right_exact(mine, parent_mat, 1)
    mine_anc = right_exact(mine, ancestry, 1)
    query_pos = ctx * rows + iota((1, rows), 1)
    query_col = ctx * rows + iota((rows, 1), 0)
    ends[...] = jnp.where(query_pos == high_col[...] - 1, 1.0, 0.0)
    start[...] = jnp.sum(
        jnp.where(query_col == low[...], 1.0, 0.0), axis=1, keepdims=True
    )
    for d in range(bias.shape[0] // rows):
        span = slice(d * rows, (d + 1) * rows)
        key_pos = (ctx - d) * rows + iota((rows, 1), 0)
        keys = jnp.where((key_pos >= low[...]) & (key_pos < high[...]), 1.0, 0.0)
        key_anc[span, :] = right_exact(keys, ancestry, 1)
        key_onehot[span, :] = keys
        linked = mm_nt(keys.astype(bf16), mine_anc.astype(bf16)) > 0.5
        visible = linked & (key_pos <= query_pos)
        bias[span, :] = jnp.where(visible, 0.0, neg_large)
        if d == 0:
            seen[...] = jnp.where(visible, 1.0, 0.0)
            own_keys = keys.astype(bf16)
    for d in range(1, bias.shape[0] // rows):
        span = slice((d - 1) * rows, d * rows)
        query_at = (ctx + d) * rows + iota((rows, 1), 0)
        theirs = jnp.where((query_at >= low[...]) & (query_at < high[...]), 1.0, 0.0)
        theirs = right_exact(theirs, ancestry, 1).astype(bf16)
        later[span, :] = jnp.where(mm_nt(own_keys, theirs) > 0.5, 0.0, neg_large)


def turned(values, first, count):
    width = values.shape[1] // count
    pieces = [
        lax.dynamic_slice_in_dim(values, lax.rem(first + i, count) * width, width, 1)
        for i in range(count)
    ]
    return jnp.concatenate(pieces, axis=1)


def part_at(ref, shard, d, shards, rows=slice(None)):
    part = ref.shape[1] // shards
    if part % 128:
        return ref[rows, d * part : (d + 1) * part]
    start = pl.multiple_of(lax.rem(shard + d, shards) * part, 128)
    return ref[rows, pl.ds(start, part)]


def enter_kernel(place, tokens, packs, first_in):
    shards = len(packs)
    part = packs[0].shape[1]
    pieces = [part_at(tokens, place[1], d, shards).astype(f32) for d in range(shards)]
    mean = sum(jnp.sum(x * x, axis=1, keepdims=True) for x in pieces) * (
        1.0 / tokens.shape[1]
    )
    scale = lax.rsqrt(mean + epsilon)
    for d in range(shards):
        gain = packs[d][24:25, :].astype(f32)
        first_in[:, d * part : (d + 1) * part] = (pieces[d] * scale * gain).astype(bf16)


def keys_in_kernel(first_in, kv_w, packs, forget_bias, seen, onehot, ends, raw_kv, lin, message):
    part = packs[0].shape[1]
    rows = first_in.shape[0]
    local = raw_kv.shape[2]
    heads_up = forget_bias.shape[0]
    cuts = [first_in[:, d * part : (d + 1) * part] for d in range(len(packs))]
    head_lin = sum(mm_nt(p[:24, :], x) for p, x in zip(packs, cuts))
    forget_in = head_lin[:heads_up] + forget_bias[...]
    lin[...] = head_lin
    lin[:heads_up, :] = forget_in
    log_forget = jnp.minimum(forget_in, 0.0) - jnp.log1p(jnp.exp(-jnp.abs(forget_in)))
    message[...] = jnp.zeros_like(message)
    for i in range(2):
        raw = sum(mm(x, w[i]) for w, x in zip(kv_w, cuts))
        raw_kv[i] = raw
        cols = slice(i * local, (i + 1) * local)
        message[:segs_up, cols] = right_exact(ends[...], raw)
        message[segs_up - 1 : segs_up, cols] = raw[rows - 1 :]
    message[segs_up : segs_up + heads_up, :rows] = left_exact(log_forget, seen[...])
    message[segs_up : segs_up + heads_up, local : local + segs_up] = left_exact(
        log_forget, onehot[...]
    )


def keys_shift_kernel(raw_kv, lin, blocks, parent, start, key_anc, gain, own_kv, delta, fq, fk, *, size):
    rows, local = raw_kv.shape[1:]
    heads_up = lin.shape[0] // 3
    spread = spread_of(heads_up, local, size)
    seg_ends = sum((b[:segs_up, :] for b in blocks[1:]), blocks[0][:segs_up, :])
    at_start = start[...] > 0.5
    at_top = iota((rows, 1), 0) == 0
    for i in range(2):
        cols = slice(i * local, (i + 1) * local)
        alpha_rows = jax.nn.sigmoid(lin[(i + 1) * heads_up : (i + 2) * heads_up, :])
        alpha = left_exact_tn(alpha_rows, spread)
        raw = raw_kv[i]
        previous = jnp.where(
            at_top, blocks[1][segs_up - 1 : segs_up, cols], pltpu.roll(raw, 1, 0)
        )
        previous = jnp.where(at_start, right_exact(parent[...], seg_ends[:, cols]), previous)
        step = previous - raw
        delta[i] = step
        shifted = raw + alpha * step
        if i == 0:
            shifted = shifted * head_scale(shifted, size) * gain[...]
        own_kv[i] = shifted.astype(bf16)
    table = slice(segs_up, segs_up + heads_up)
    for d in range(len(blocks)):
        sums = blocks[d][table, :rows]
        span = slice(d * rows, (d + 1) * rows)
        later = blocks[d + 1 :]
        if later:
            before = sum(
                (b[table, local : local + segs_up] for b in later[1:]),
                later[0][table, local : local + segs_up],
            )
            sums = sums + left_exact_nt(before, key_anc[span, :])
        for h in range(2 * fk.shape[0]):
            fk[h // 2, h % 2 : h % 2 + 1, span] = sums[h : h + 1]
            if d == 0:
                fq[h // 2, h % 2 : h % 2 + 1, :] = sums[h : h + 1]


def queries_kernel(first_in, bundles, gain, raw_q, query, raw_g, *, size):
    part = bundles[0].shape[1]
    cuts = [first_in[:, d * part : (d + 1) * part] for d in range(len(bundles))]
    raw = sum(mm(x, w[0]) for w, x in zip(bundles, cuts))
    raw_q[...] = raw
    raw_g[...] = sum(mm(x, w[1]) for w, x in zip(bundles, cuts))
    normed = (raw * head_scale(raw, size) * gain[...]).astype(bf16)
    query[...] = (normed.astype(f32) * (size**-0.5)).astype(bf16)


def attn_share_kernel(values, bundles, out):
    half = out.shape[0]
    part = bundles[0].shape[1]
    for d, w in enumerate(bundles):
        out[:, d * part : (d + 1) * part] = mm_nt(values[half:, :], w[2])


def attn_share_sum_kernel(values, bundles, given, out):
    half = out.shape[0]
    part = bundles[0].shape[1]
    for d, w in enumerate(bundles):
        cols = slice(d * part, (d + 1) * part)
        out[:, cols] = (mm_nt(values[:half, :], w[2]) + given[:, cols]).astype(bf16)


def share_kernel(values, weights, out, *, which):
    half = out.shape[0]
    part = out.shape[1] // len(weights)
    rows = slice(which * half, (which + 1) * half)
    for d, w in enumerate(weights):
        out[:, d * part : (d + 1) * part] = mm(values[rows, :], w[...])


def share_sum_kernel(values, weights, given, out):
    half = out.shape[0]
    part = out.shape[1] // len(weights)
    for d, w in enumerate(weights):
        cols = slice(d * part, (d + 1) * part)
        out[:, cols] = (mm(values[:half, :], w[...]) + given[:, cols]).astype(bf16)


def middle_kernel(place, tokens, packs, total, other, middle, second_in):
    shards = len(packs)
    part = packs[0].shape[1]
    half = total.shape[0]
    rows = pl.ds(pl.multiple_of(place[0] * half, 16), half)
    square = jnp.zeros((half, 1), f32)
    for d in range(shards):
        cols = slice(d * part, (d + 1) * part)
        value = part_at(tokens, place[1], d, shards, rows).astype(f32) + (
            total[:, cols].astype(f32) + other[:, cols].astype(f32)
        )
        middle[:, cols] = value
        square = square + jnp.sum(value * value, axis=1, keepdims=True)
    scale = lax.rsqrt(square * (1.0 / middle.shape[1]) + epsilon)
    for d in range(shards):
        cols = slice(d * part, (d + 1) * part)
        gain = packs[d][25:26, :].astype(f32)
        second_in[:, cols] = (middle[:, cols] * scale * gain).astype(bf16)


def grad_hidden_kernel(place, cotangent, down_w, grad_out, d_hidden):
    shards = len(down_w)
    part = down_w[0].shape[1]
    half = cotangent.shape[0] // 2
    for k in range(2):
        rows = pl.ds(pl.multiple_of(lax.rem(place[0] + k, 2) * half, 16), half)
        span = slice(k * half, (k + 1) * half)
        for d in range(shards):
            grad_out[span, d * part : (d + 1) * part] = part_at(
                cotangent, place[1], d, shards, rows
            )
    d_hidden[...] = sum(
        mm_nt(grad_out[:, d * part : (d + 1) * part], w[...]) for d, w in enumerate(down_w)
    )


def mlp_kernel(*refs):
    mine, theirs = refs[:2]
    d_hidden, hidden, d_lin, keep, give, second = refs[-6:]
    weights = refs[2:-6]
    part = weights[0].shape[1]
    half = mine.shape[0]

    @pl.when(pl.program_id(0) == 0)
    def _():
        second[:half, :] = mine[...]
        second[half:, :] = theirs[...]

    lin = [
        sum(mm(second[:, d * part : (d + 1) * part], w[i]) for d, w in enumerate(weights))
        for i in range(2)
    ]
    sig = jax.nn.sigmoid(lin[0])
    silu = lin[0] * sig
    grad = d_hidden[...]
    hidden[...] = (silu * lin[1]).astype(bf16)
    d_gate = (grad * lin[1] * (sig * (1.0 + lin[0] * (1.0 - sig)))).astype(bf16)
    d_up = (grad * silu).astype(bf16)
    d_lin[0] = d_gate
    d_lin[1] = d_up
    for d, w in enumerate(weights):
        value = mm_nt(d_gate, w[0]) + mm_nt(d_up, w[1])
        for share, rows in ((keep, slice(0, half)), (give, slice(half, 2 * half))):

            @pl.when(pl.program_id(0) == 0)
            def _():
                share[d] = value[rows]

            @pl.when(pl.program_id(0) > 0)
            def _():
                share[d] = share[d] + value[rows]


def mlp(mine, theirs, weights, d_hidden):
    half, width = mine.shape
    rows, hidden_size = d_hidden.shape
    shards = len(weights)
    part = weights[0].shape[1]
    block = 512
    flat = pl.BlockSpec((half, width), lambda j: (0, 0))
    share = pl.BlockSpec((shards, half, part), lambda j: (0, 0, 0))
    return pl.pallas_call(
        mlp_kernel,
        grid=(hidden_size // block,),
        in_specs=[flat, flat]
        + [pl.BlockSpec((2, part, block), lambda j: (0, 0, j)) for _ in weights]
        + [pl.BlockSpec((rows, block), lambda j: (0, j))],
        out_specs=[
            pl.BlockSpec((rows, block), lambda j: (0, j)),
            pl.BlockSpec((2, rows, block), lambda j: (0, 0, j)),
            share,
            share,
        ],
        out_shape=[
            jax.ShapeDtypeStruct((rows, hidden_size), bf16),
            jax.ShapeDtypeStruct((2, rows, hidden_size), bf16),
            jax.ShapeDtypeStruct((shards, half, part), f32),
            jax.ShapeDtypeStruct((shards, half, part), f32),
        ],
        scratch_shapes=[pltpu.VMEM((rows, width), bf16)],
        compiler_params=pltpu.CompilerParams(vmem_limit_bytes=26 << 20),
        cost_estimate=pl.CostEstimate(flops=1, transcendentals=1, bytes_accessed=1),
        name="mlp",
    )(mine, theirs, *weights, d_hidden)


def gain_row(packs, row):
    return jnp.concatenate([p[row : row + 1, :].astype(f32) for p in packs], axis=1)


def middle_back_kernel(grad_out, packs, middle, total, other, d_middle, d_middle_b, d_gain):
    half = middle.shape[0]
    value = middle[...]
    d_second = jnp.concatenate(
        [total[d].astype(f32) + other[d].astype(f32) for d in range(total.shape[0])], axis=1
    )
    d_value, gain = norm_grad(value, rms_scale(value), gain_row(packs, 25), d_second)
    d_gain[...] = gain
    d_value = d_value + grad_out[:half, :].astype(f32)
    d_middle[...] = d_value
    d_middle_b[...] = d_value.astype(bf16)


row_room = 48


def row_pieces(values):
    return jnp.concatenate([p.astype(f32) for p in bf16_pieces(values, 3)], axis=0)


def rows_back(block, start):
    pieces = block[...].astype(f32)[start : start + 24]
    return pieces[:8] + pieces[8:16] + pieces[16:]


def head_row(rows8, head):
    return jnp.sum(jnp.where(iota(rows8.shape, 0) == head, rows8, 0.0), axis=0, keepdims=True)


def gate_back_kernel(
    place, mine, theirs, bundles, raw_g, attended, forget_q, lse, message, d_raw_g, *, size
):
    half = mine.shape[0]
    rows, local = raw_g.shape
    part = bundles[0].shape[1]
    for k, source in enumerate((mine, theirs)):
        at = pl.ds(pl.multiple_of(lax.rem(place[0] + k, 2) * half, 16), half)
        d_gated = sum(
            mm(source[:, d * part : (d + 1) * part], w[2]) for d, w in enumerate(bundles)
        )
        sig = jax.nn.sigmoid(raw_g[at, :])
        message[at, :] = (d_gated * sig).astype(bf16)
        d_raw_g[at, :] = (d_gated * attended[at, :] * sig * (1.0 - sig)).astype(bf16)
    products = message[:rows, :].astype(f32) * attended[...]
    delta = right_exact_nt(spread_of(8, local, size), products)
    heads = 2 * forget_q.shape[0]
    forget = [
        forget_q[h // 2, h % 2 : h % 2 + 1, :] - lse[h // 2, h % 2 : h % 2 + 1, :]
        for h in range(heads)
    ]
    forget = jnp.concatenate(forget + [jnp.zeros((8 - heads, rows), f32)], axis=0)
    message[rows:, :] = jnp.concatenate(
        [row_pieces(forget), row_pieces(delta)], axis=0
    ).astype(bf16)


def query_back_kernel(raw_q, d_query, gain, d_raw_g, d_gq, d_gain, *, size):
    local = raw_q.shape[1]
    d_raw, gain_grad = head_grad(raw_q[...], gain[...], d_query[...], size)
    d_gain[...] = gain_grad
    d_gq[:, :local] = d_raw_g[...]
    d_gq[:, local:] = d_raw.astype(bf16)


def shift_back_kernel(
    d_kv, raw_kv, delta, lin, gain, start, parent, dcq, dck, onehot,
    base, message, d_alpha, d_gain, d_forget, *, size,
):
    rows, local = raw_kv.shape[1:]
    heads_up = lin.shape[0] // 3
    heads = 2 * dcq.shape[0]
    spread = spread_of(heads_up, local, size)
    not_start = 1.0 - start[...]
    start_parent = parent[...] * start[...]
    message[...] = jnp.zeros_like(message)
    for i in range(2):
        cols = slice(i * local, (i + 1) * local)
        alpha_rows = jax.nn.sigmoid(lin[(i + 1) * heads_up : (i + 2) * heads_up, :])
        alpha = left_exact_tn(alpha_rows, spread)
        d_shift = d_kv[i]
        if i == 0:
            shifted = raw_kv[0] + alpha * delta[0]
            d_shift, gain_grad = head_grad(shifted, gain[...], d_shift, size)
            d_gain[...] = gain_grad
        d_alpha[i * heads_up : (i + 1) * heads_up, :] = (
            right_exact_nt(spread, d_shift * delta[i], 2) * alpha_rows * (1.0 - alpha_rows)
        )
        d_prev = alpha * d_shift
        d_step = d_prev * not_start
        base[i] = (
            d_shift
            - d_prev
            + jnp.where(iota((rows, 1), 0) == rows - 1, 0.0, pltpu.roll(d_step, rows - 1, 0))
        )
        message[:segs_up, cols] = right_exact_tn(start_parent, d_prev, 2)
        message[segs_up - 1 : segs_up, cols] = d_step[:1]
    grads = [
        dcq[h // 2, h % 2 : h % 2 + 1, :] - dck[h // 2, h % 2 : h % 2 + 1, :]
        for h in range(heads)
    ]
    grads = jnp.concatenate(grads + [jnp.zeros((heads_up - heads, rows), f32)], axis=0)
    d_forget[...] = grads
    message[segs_up : segs_up + heads_up, local : local + segs_up] = left_exact(
        grads, onehot[...]
    )


def raw_back_kernel(
    base, table_own, returned, ends, seen, onehot, anc, lin, d_forget_own, d_alpha,
    d_raw_kv, d_lin, d_bias,
):
    rows, local = base.shape[1:]
    heads_up = lin.shape[0] // 3
    tail = slice(segs_up, segs_up + heads_up)
    for i in range(2):
        cols = slice(i * local, (i + 1) * local)
        table = table_own[:segs_up, cols]
        for r in returned:
            table = table + r[:segs_up, cols]
        edge = jnp.where(
            iota((rows, 1), 0) == rows - 1, returned[0][segs_up - 1 : segs_up, cols], 0.0
        )
        d_raw_kv[i] = (base[i] + edge + right_exact_tn(ends[...], table, 2)).astype(bf16)
    own = d_forget_own[...]
    sums = jnp.zeros((heads_up, segs_up), f32)
    for r in returned:
        sums = sums + r[tail, local : local + segs_up]
    d_log = left_exact_nt(own, seen[...]) + left_exact_nt(
        left_exact(sums, anc[...]), onehot[...]
    )
    d_forget = d_log * jax.nn.sigmoid(-lin[:heads_up, :])
    d_bias[...] = jnp.sum(d_forget, axis=1, keepdims=True)
    d_lin[:heads_up, :] = d_forget.astype(bf16)
    d_lin[heads_up:, :] = d_alpha[...].astype(bf16)


def first_gq_kernel(place, d_gq, bundles, out):
    half = d_gq.shape[0] // 2
    part = bundles[0].shape[1]
    local = d_gq.shape[1] // 2
    for k in range(2):
        rows = pl.ds(pl.multiple_of(lax.rem(place[0] + k, 2) * half, 16), half)
        for d, w in enumerate(bundles):
            out[k * half : (k + 1) * half, d * part : (d + 1) * part] = mm_nt(
                d_gq[rows, :local], w[1]
            ) + mm_nt(d_gq[rows, local:], w[0])


def first_share_kernel(place, d_kv, d_lin, kv_w, packs, partial, out, heads_part, *, which):
    half = out.shape[0]
    part = packs[0].shape[1]
    rows = pl.ds(pl.multiple_of(lax.rem(place[0] + which, 2) * half, 16), half)
    for d in range(len(packs)):
        cols = slice(d * part, (d + 1) * part)
        heads_part[...] = mm_tn(d_lin[...], packs[d][:24, :])
        out[:, cols] = (
            mm_nt(d_kv[0, rows, :], kv_w[d][0])
            + mm_nt(d_kv[1, rows, :], kv_w[d][1])
            + heads_part[rows, :]
            + partial[which * half : (which + 1) * half, cols]
        ).astype(out.dtype)


def first_sum_kernel(mine, given, out):
    out[...] = (mine[...] + given[...]).astype(bf16)


def enter_back_kernel(place, tokens, packs, d_middle, total, other, d_own, d_gain):
    shards = len(packs)
    half = total.shape[0]
    rows = pl.ds(pl.multiple_of(place[0] * half, 16), half)
    value = jnp.concatenate(
        [part_at(tokens, place[1], d, shards, rows).astype(f32) for d in range(shards)], axis=1
    )
    d_first = total[...].astype(f32) + other[...].astype(f32)
    d_value, gain = norm_grad(value, rms_scale(value), gain_row(packs, 24), d_first)
    d_gain[...] = gain
    d_own[...] = d_middle[...] + d_value


def settle_kernel(place, mine, theirs, out, *, shards):
    half = mine.shape[0]
    part = mine.shape[1] // shards
    for k, source in enumerate((mine, theirs)):
        rows = pl.ds(pl.multiple_of(lax.rem(place[0] + k, 2) * half, 16), half)
        for d in range(shards):
            cols = slice(d * part, (d + 1) * part)
            if part % 128:
                out[rows, cols] = source[:, cols]
            else:
                start = pl.multiple_of(lax.rem(place[1] + d, shards) * part, 128)
                out[rows, pl.ds(start, part)] = source[:, cols]


def leave_kernel(middle, total, other, out):
    out[...] = (
        middle[...] + (total[...].astype(f32) + other[...].astype(f32))
    ).astype(bf16)


def named(kernel, **fixed):
    def bound(*refs):
        kernel(*refs, **fixed)

    bound.__name__ = kernel.__name__
    return bound


def planes_of(weights):
    rows, count, width = weights.shape
    block = 128 if rows % 128 == 0 else rows

    def planes_kernel(source, out):
        for i in range(count):
            out[i] = source[:, i, :].astype(bf16)

    return pl.pallas_call(
        planes_kernel,
        grid=(rows // block,),
        in_specs=[pl.BlockSpec((block, count, width), lambda j: (j, 0, 0))],
        out_specs=pl.BlockSpec((count, block, width), lambda j: (0, j, 0)),
        out_shape=jax.ShapeDtypeStruct((count, rows, width), bf16),
        compiler_params=pltpu.CompilerParams(vmem_limit_bytes=12 << 20),
        cost_estimate=pl.CostEstimate(flops=1, transcendentals=1, bytes_accessed=1),
        name="planes",
    )(weights)


class At:

    def __init__(self, array, rows=None, cols=None, lead=None):
        if cols and (cols[0] % 128 or cols[1] % 128):
            array, cols = array[..., cols[0] : cols[1]], None
        self.array, self.lead = array, lead
        self.rows = rows or (0, array.shape[-2])
        self.cols = cols or (0, array.shape[-1])

    def spec(self, block=None):
        start, stop = self.rows
        height = stop - start
        first, last = self.cols
        wide = block or last - first
        shape, row, col = (height, wide), start // height, first // wide

        def at(j):
            return (row, col + j if block else col)

        if self.lead is None:
            return pl.BlockSpec(shape, at)
        return pl.BlockSpec((None,) + shape, lambda j: (self.lead,) + at(j))


def weight_grad(order, pairs, got, block):
    count = len(pairs)
    rows = pairs[0][0].cols[1] - pairs[0][0].cols[0]
    width = pairs[0][1].cols[1] - pairs[0][1].cols[0]

    def weight_grad_kernel(*refs):
        total = mm_tn(refs[0][...], refs[1][...])
        for i in range(1, count):
            total = total + mm_tn(refs[2 * i][...], refs[2 * i + 1][...])
        for ref in refs[2 * count : -1]:
            total = total + ref[...].astype(f32)
        refs[-1][...] = total.astype(bf16)

    specs = [spec for a, b in pairs for spec in (a.spec(block), b.spec())]
    over = pl.BlockSpec((block, width), lambda j: (j, 0))
    call = pl.pallas_call(
        weight_grad_kernel,
        grid=(rows // block,),
        in_specs=specs + [over for _ in got],
        out_specs=over,
        out_shape=jax.ShapeDtypeStruct((rows, width), bf16),
        compiler_params=pltpu.CompilerParams(vmem_limit_bytes=20 << 20),
        cost_estimate=pl.CostEstimate(flops=1, transcendentals=1, bytes_accessed=1),
        name="weight_grad",
    )
    return order(call, *[x.array for pair in pairs for x in pair], *got)


def add_rows(left, right):
    rows, width = left.shape
    block = rows if rows % 64 else 64 if rows <= 256 else 128

    def add_kernel(left, right, out):
        out[...] = (left[...].astype(f32) + right[...].astype(f32)).astype(out.dtype)

    over = pl.BlockSpec((block, width), lambda j: (j, 0))
    return pl.pallas_call(
        add_kernel,
        grid=(rows // block,),
        in_specs=[over, over],
        out_specs=over,
        out_shape=jax.ShapeDtypeStruct((rows, width), left.dtype),
        compiler_params=pltpu.CompilerParams(vmem_limit_bytes=8 << 20),
        cost_estimate=pl.CostEstimate(flops=1, transcendentals=1, bytes_accessed=1),
        name="add",
    )(left, right)


def attend_kernel(*refs):
    place, query_ref, *kv_refs, bias_ref, cq_ref, ck_ref, gate_ref, out_ref, gated_ref, lse_ref = refs
    rows = query_ref.shape[0]
    half = rows // 2
    size = query_ref.shape[1] // 2
    key_cols = ck_ref[0].T
    outs = []
    for e in range(2):
        cols = slice(e * size, (e + 1) * size)
        query = query_ref[:, cols]
        forget_row = cq_ref[0, e : e + 1, :]
        total = jnp.zeros((1, rows), f32)
        mixed = jnp.zeros((size, rows), f32)
        for d in range(len(kv_refs) // 2):
            span = slice(d * rows, (d + 1) * rows)
            scores = mm_nt(kv_refs[2 * d][0, :, cols], query)
            scores = scores + (forget_row - key_cols[span, e : e + 1]) + bias_ref[span, :]
            weights = jnp.exp(scores)
            total = total + jnp.sum(weights, axis=0, keepdims=True)
            mixed = mixed + mm_tn(kv_refs[2 * d + 1][0, :, cols], weights.astype(bf16))
        outs.append((mixed / total).T)
        lse_ref[0, e : e + 1, :] = jnp.log(total)
    attended = jnp.concatenate(outs, axis=1)
    out_ref[...] = attended
    gated = (attended * jax.nn.sigmoid(gate_ref[...])).astype(bf16)
    for k in range(2):
        there = pl.ds(pl.multiple_of(lax.rem(place[0] + k, 2) * half, 16), half)
        gated_ref[there, :] = gated[k * half : (k + 1) * half]


def score_grads(key, value, query, d_out, forget_row, delta_row, key_col, bias):
    scores = mm_nt(key, query) + (forget_row - key_col) + bias
    probs = jnp.exp(scores)
    d_scores = probs * (mm_nt(value, d_out) - delta_row)
    return probs.astype(bf16), d_scores.astype(bf16)


def first_col(rows, size):
    return jnp.where(iota((rows, size), 1) == 0, 1.0, 0.0).astype(bf16)


def as_rows(columns):
    pad = jnp.zeros((columns[0].shape[0], 8 - len(columns)), f32)
    return jnp.concatenate(columns + [pad], axis=1).T


def query_grads_kernel(*refs):
    query_ref, d_out_ref, row_values = refs[:3]
    kv_refs = refs[3:-6]
    bias_ref, ck_ref, d_query_ref, d_kv_ref, dcq_ref, dck_ref = refs[-6:]
    rows = query_ref.shape[0]
    size = query_ref.shape[1] // 2
    key_cols = ck_ref[0].T
    forget8, delta8 = rows_back(row_values, 0), rows_back(row_values, 24)
    sums = []
    for e in range(2):
        cols = slice(e * size, (e + 1) * size)
        head = 2 * pl.program_id(0) + e
        query = query_ref[:, cols]
        d_out = d_out_ref[:, cols]
        forget_row, delta_row = head_row(forget8, head), head_row(delta8, head)
        d_query = jnp.zeros((rows, size), f32)
        d_row = jnp.zeros((1, rows), f32)
        for d in range(len(kv_refs) // 2):
            span = slice(d * rows, (d + 1) * rows)
            key = kv_refs[2 * d][0, :, cols]
            probs, d_scores = score_grads(
                key,
                kv_refs[2 * d + 1][0, :, cols],
                query,
                d_out,
                forget_row,
                delta_row,
                key_cols[span, e : e + 1],
                bias_ref[span, :],
            )
            d_query = d_query + mm_tn(d_scores, key)
            d_row = d_row + jnp.sum(d_scores.astype(f32), axis=0, keepdims=True)
            if d == 0:
                found = mm(d_scores, jnp.concatenate([query, first_col(rows, size)], axis=1))
                sums.append(found[:, size : size + 1])
                d_kv_ref[0, :, cols] = found[:, :size]
                d_kv_ref[1, :, cols] = mm(probs, d_out)
        d_query_ref[:, cols] = d_query * (size ** (-0.5))
        dcq_ref[0, e : e + 1, :] = d_row
    dck_ref[0] = as_rows(sums)


def key_grads_kernel(*refs):
    key_ref, value_ref, bias_ref, ck_ref, own_ref, own_dck_ref = refs[:6]
    sets = refs[6:-2]
    d_kv_ref, dck_ref = refs[-2:]
    count = len(sets) // 3
    rows = key_ref.shape[1]
    size = key_ref.shape[2] // 2
    key_cols = ck_ref[0].T
    forget8 = [rows_back(sets[3 * d + 2], 0) for d in range(count)]
    delta8 = [rows_back(sets[3 * d + 2], 24) for d in range(count)]
    sums = []
    for e in range(2):
        cols = slice(e * size, (e + 1) * size)
        head = 2 * pl.program_id(0) + e
        key, value = key_ref[0, :, cols], value_ref[0, :, cols]
        d_key = jnp.zeros((rows, 2 * size), f32)
        d_value = jnp.zeros((rows, size), f32)
        for d in range(count):
            query, d_out = sets[3 * d][:, cols], sets[3 * d + 1][:, cols]
            probs, d_scores = score_grads(
                key,
                value,
                query,
                d_out,
                head_row(forget8[d], head),
                head_row(delta8[d], head),
                key_cols[:, e : e + 1],
                bias_ref[d * rows : (d + 1) * rows, :],
            )
            d_key = d_key + mm(
                d_scores, jnp.concatenate([query, first_col(rows, size)], axis=1)
            )
            d_value = d_value + mm(probs, d_out)
        sums.append(d_key[:, size : size + 1])
        d_kv_ref[0, :, cols] = own_ref[0, :, cols] + d_key[:, :size]
        d_kv_ref[1, :, cols] = own_ref[1, :, cols] + d_value
    dck_ref[0] = own_dck_ref[0] + as_rows(sums)


def kv_specs(blocks, lanes):
    rows = blocks[0].shape[1]
    return [
        pl.BlockSpec((1, rows, lanes), lambda p, kind=kind: (kind, 0, p))
        for _ in blocks
        for kind in range(2)
    ]


def twice(blocks):
    return [b for b in blocks for _ in range(2)]


def attention(place, query, kv_blocks, bias, forget_q, forget_k, raw_g):
    rows, local = query.shape
    pairs = forget_q.shape[0]
    keys = bias.shape[0]
    lanes = local // pairs
    flat = pl.BlockSpec((rows, lanes), lambda p: (0, p))
    row_spec = pl.BlockSpec((1, 8, rows), lambda p: (p, 0, 0))
    return pl.pallas_call(
        attend_kernel,
        grid=(pairs,),
        in_specs=[pl.BlockSpec(memory_space=pltpu.SMEM), flat]
        + kv_specs(kv_blocks, lanes)
        + [
            pl.BlockSpec((keys, rows), lambda p: (0, 0)),
            row_spec,
            pl.BlockSpec((1, 8, keys), lambda p: (p, 0, 0)),
            flat,
        ],
        out_specs=[flat, flat, row_spec],
        out_shape=[
            jax.ShapeDtypeStruct((rows, local), f32),
            jax.ShapeDtypeStruct((rows, local), bf16),
            jax.ShapeDtypeStruct((pairs, 8, rows), f32),
        ],
        compiler_params=pltpu.CompilerParams(vmem_limit_bytes=20 << 20),
        cost_estimate=pl.CostEstimate(flops=1, transcendentals=1, bytes_accessed=1),
        name="attend",
    )(place, query, *twice(kv_blocks), bias, forget_q, forget_k, raw_g)


def message_specs(rows, lanes, width):
    return [
        pl.BlockSpec((rows, lanes), lambda p: (0, p)),
        pl.BlockSpec((row_room, width), lambda p: (rows // row_room, 0)),
    ]


def back_params():
    return {
        "compiler_params": pltpu.CompilerParams(vmem_limit_bytes=20 << 20),
        "cost_estimate": pl.CostEstimate(flops=1, transcendentals=1, bytes_accessed=1),
    }


def query_grads(own_query, own_out, kv_blocks, bias, forget_k):
    keys, rows = bias.shape
    local = own_query.shape[1]
    pairs = forget_k.shape[0]
    lanes = local // pairs
    flat, row_block = message_specs(rows, lanes, local)
    row_spec = pl.BlockSpec((1, 8, rows), lambda p: (p, 0, 0))
    return pl.pallas_call(
        query_grads_kernel,
        grid=(pairs,),
        in_specs=[flat, flat, row_block]
        + kv_specs(kv_blocks, lanes)
        + [
            pl.BlockSpec((keys, rows), lambda p: (0, 0)),
            pl.BlockSpec((1, 8, keys), lambda p: (p, 0, 0)),
        ],
        out_specs=[
            flat,
            pl.BlockSpec((2, rows, lanes), lambda p: (0, 0, p)),
            row_spec,
            row_spec,
        ],
        out_shape=[
            jax.ShapeDtypeStruct((rows, local), f32),
            jax.ShapeDtypeStruct((2, rows, local), f32),
            jax.ShapeDtypeStruct((pairs, 8, rows), f32),
            jax.ShapeDtypeStruct((pairs, 8, rows), f32),
        ],
        name="query_grads",
        **back_params(),
    )(own_query, own_out, own_out, *twice(kv_blocks), bias, forget_k)


def key_grads(own_kv, later, forget_k, own_grads, own_dck, queries, outs):
    rows, local = own_kv.shape[1:]
    pairs = forget_k.shape[0]
    lanes = local // pairs
    flat, row_block = message_specs(rows, lanes, local)
    row_spec = pl.BlockSpec((1, 8, rows), lambda p: (p, 0, 0))
    pair_spec = pl.BlockSpec((2, rows, lanes), lambda p: (0, 0, p))
    return pl.pallas_call(
        key_grads_kernel,
        grid=(pairs,),
        in_specs=kv_specs([own_kv], lanes)
        + [pl.BlockSpec(later.shape, lambda p: (0, 0)), row_spec, pair_spec, row_spec]
        + [flat, flat, row_block] * len(queries),
        out_specs=[pair_spec, row_spec],
        out_shape=[
            jax.ShapeDtypeStruct((2, rows, local), f32),
            jax.ShapeDtypeStruct((pairs, 8, rows), f32),
        ],
        name="key_grads",
        **back_params(),
    )(
        own_kv,
        own_kv,
        later,
        forget_k,
        own_grads,
        own_dck,
        *[x for q, o in zip(queries, outs) for x in (q, o, o)],
    )


def small_kernel(d_lin, first_in, gains, other, gain_q, gain_k, d_bias, *outs):
    part = first_in.shape[1] // len(outs)
    local = gain_q.shape[1]
    for d, out in enumerate(outs):
        cols = slice(d * part, (d + 1) * part)
        out[...] = jnp.zeros_like(out)
        out[:24, :part] = mm(d_lin[...], first_in[:, cols])
        out[24:26, :part] = gains[:, cols] + other[:, cols]
        out[26:27, :local] = gain_q[...]
        out[27:28, :local] = gain_k[...]
        out[32:40, :1] = d_bias[...]


def pieces_kernel(place, *refs):
    out = refs[-1]
    count = len(refs) - 1
    rows = refs[0].shape[0]
    for k, piece in enumerate(refs[:count]):
        start = pl.multiple_of(lax.rem(place[2] + k, count) * rows, 16)
        out[pl.ds(start, rows), :] = piece[...]


class Order:

    def __init__(self):
        self.last, self.held = None, []

    def tied(self, *args):
        if self.last is not None:
            args, _, _ = lax.optimization_barrier((args, self.last, self.held))
        self.held = []
        return args

    def hold(self, values):
        self.held.append(values)

    def __call__(self, work, *args):
        found = work(*self.tied(*args))
        self.last = min(jax.tree.leaves(found), key=nbytes)
        return found


class LineSum:

    def __init__(self, order, values):
        self.order, self.total = order, values
        self.count = lax.axis_size("ctx")
        self.half = self.count // 2
        self.hop, self.coming = 0, None
        self.send()

    def send(self):
        k, count, half = self.hop, self.count, self.half
        if k < half - 1:
            pairs = [(k, k + 1), (count - 1 - k, count - 2 - k)]
        elif k == half - 1:
            pairs = [(half - 1, half), (half, half - 1)]
        elif k < 2 * half - 1:
            j = 2 * half - 2 - k
            pairs = [(j + 1, j), (count - 2 - j, count - 1 - j)]
        else:
            return
        self.coming = lax.ppermute(self.total, "ctx", pairs)

    def step(self):
        k, half = self.hop, self.half
        self.hop += 1
        if k < half:
            self.total = self.order(add_rows, self.total, self.coming)
            self.coming = None
        elif k < 2 * half - 2:
            j = 2 * half - 2 - k
            index = lax.axis_index("ctx")
            at_ends = (index == j) | (index == self.count - 1 - j)
            self.total = self.order(
                lambda a, b: jnp.where(at_ends, b, a), self.total, self.coming
            )
            self.coming = None
        else:
            self.order.hold(self.coming)
            return
        self.send()

    def finish(self):
        while self.hop < 2 * self.half - 1:
            self.step()
        return self.total, self.coming


def spread_out(order, place, planes):
    sums = [s.finish() for plane in planes for s in plane]
    arrays = [x for pair in sums for x in pair if x is not None]
    each = len(arrays) // len(sums)
    height, width = planes[0][0].total.shape
    chunks = len(planes[0])
    block = 128 if height % 128 == 0 else height
    steps = height // block
    count = lax.axis_size("ctx")

    def spread_out_kernel(place, *refs):
        out = refs[-1]
        at_ends = (place[2] == 0) | (place[2] == count - 1)
        for c in range(chunks):

            @pl.when(pl.program_id(0) // steps == c)
            def _():
                for i in range(len(planes)):
                    first = (i * chunks + c) * each
                    value = refs[first][...].astype(f32)
                    if each > 1:
                        value = jnp.where(at_ends, refs[first + 1][...].astype(f32), value)
                    if len(planes) > 1:
                        out[:, i, :] = value
                    else:
                        out[...] = value

    def spec(c):
        return pl.BlockSpec(
            (block, width), lambda j: (jnp.clip(j - c * steps, 0, steps - 1), 0)
        )

    specs = [spec(c) for _ in planes for c in range(chunks) for _ in range(each)]
    middle = (len(planes),) if len(planes) > 1 else ()
    call = pl.pallas_call(
        spread_out_kernel,
        grid=(chunks * steps,),
        in_specs=[pl.BlockSpec(memory_space=pltpu.SMEM)] + specs,
        out_specs=pl.BlockSpec((block, *middle, width), lambda j: (j, *(0 for _ in middle), 0)),
        out_shape=jax.ShapeDtypeStruct((chunks * height, *middle, width), f32),
        compiler_params=pltpu.CompilerParams(vmem_limit_bytes=24 << 20),
        cost_estimate=pl.CostEstimate(flops=1, transcendentals=1, bytes_accessed=1),
        name="spread_out",
    )
    return order(call, place, *arrays)


schedule = (
    "bs1", "U10", "ms1", "bs2", "q1", "ms2", "D00", "U11", "U00", "q2", "D10", "mb", "lv", "gb",
    "D01", "G10", "U12", "q3", "aq", "qb", "G00", "ak", "G11", "sb", "G01", "D02", "U13", "D11",
    "rb", "G12", "O0", "fgq", "D03", "G02", "U1h", "U01", "fs1", "G13", "fs2", "Qq1", "D0h", "D12",
    "G03", "fsum", "G1h", "Qg1", "U02", "K1", "V1", "D13", "Qq2", "G0h", "O1", "U03", "D1h", "Qg2",
    "Qq3", "O2", "eb", "U0h", "Qg3", "V2", "Qqh", "sm", "K2", "O3", "Qgh", "V3", "df", "sm1", "Oh",
    "K3", "sm2", "st", "gu", "Vh", "sm3", "so", "of", "Kh", "at", "smf",
)


def body(
    tokens,
    seg_parents,
    seg_offsets,
    tok_seg,
    norm_gain,
    w_attn,
    w_heads,
    forget_bias,
    qk_gain,
    w_out,
    w_gate_up,
    w_down,
    cotangent,
):
    shards = lax.axis_size("shard")
    ctxs = lax.axis_size("ctx")
    ctx = lax.axis_index("ctx")
    tps = lax.axis_size("tp")
    rows, width = tokens.shape[1:]
    half = rows // 2
    part = width // shards
    local = w_attn.shape[2]
    heads = w_heads.shape[2]
    heads_up = 8
    size = local // heads
    hidden_size = w_gate_up.shape[2]
    segs = seg_parents.shape[1]
    order = Order()
    place = jnp.stack(
        [lax.axis_index("tp") % 2, lax.axis_index("shard"), ctx]
    ).astype(jnp.int32)

    def gathered(piece):
        return [piece] + [from_ring(piece, "shard", d) for d in range(1, shards)]

    def owned(piece):
        return [piece[:, :part]] + [
            from_ring(piece[:, part * (shards - d) : part * (shards - d + 1)], "shard", d)
            for d in range(1, shards)
        ]

    def crossed(total):
        bit = 2
        other = partner(total, "tp", bit)
        while bit * 2 < tps:
            total = (total.astype(f32) + other.astype(f32)).astype(bf16)
            bit = bit * 2
            other = partner(total, "tp", bit)
        return total, other

    def pack_small(w, gain):
        table = jnp.pad(
            jnp.transpose(w, (1, 2, 0)), ((0, 0), (0, heads_up - heads), (0, 0))
        ).reshape(3 * heads_up, part)
        return jnp.concatenate([table, jnp.pad(gain, ((0, 6), (0, 0)))], axis=0).astype(bf16)

    piece_rows = hidden_size // ctxs
    piece = order(
        lambda w: lax.dynamic_slice_in_dim(w, ctx * piece_rows, piece_rows, 0).astype(bf16), w_down
    )
    pieces = [from_ring(piece, "shard", d) for d in range(1, shards)]
    packs = gathered(order(pack_small, w_heads, norm_gain))
    attn_b = order(lambda w: jnp.transpose(w, (1, 0, 2)).astype(bf16), w_attn)
    kv_w = gathered(order(lambda w: w[1:3], attn_b))
    padded = jnp.full((segs_up - segs,), -1, jnp.int32)
    low = jnp.concatenate([seg_offsets[0, :segs], padded])
    high = jnp.concatenate([seg_offsets[0, 1:], padded])
    parents = jnp.concatenate([seg_parents[0], padded])
    bias, later, seen, key_anc, onehot, parent, start, ends, anc, _ = order(
        lambda *a: whole(
            masks_kernel,
            [
                ((rows * ctxs, rows), f32),
                ((rows * (ctxs - 1), rows), f32),
                ((rows, rows), f32),
                ((rows * ctxs, segs_up), f32),
                ((rows, segs_up), f32),
                ((rows, segs_up), f32),
                ((rows, 1), f32),
                ((segs_up, rows), f32),
                ((segs_up, segs_up), f32),
                ((rows * ctxs, segs_up), f32),
            ],
            *a,
        ),
        place,
        low[None],
        high[None],
        high[:, None],
        parents[:, None],
        tok_seg[0][:, None],
    )
    tree, cotangent = tokens[0], cotangent[0]
    if part % 128:
        tree = turned(tree, place[1], shards)
        cotangent = turned(cotangent, place[1], shards)

    def settled(values):
        return turned(values, shards - place[1], shards) if part % 128 else values

    for p in pieces:
        order.hold(p)
    (first_in,) = order(
        lambda *a: whole(enter_kernel, [((rows, width), bf16)], *a), place, tree, packs
    )
    pieces = order.tied(*pieces)
    piece_sets = [[p] + [from_ring(p, "ctx", k) for k in range(1, ctxs)] for p in pieces]
    bundles = gathered(
        order(lambda a, w: jnp.stack([a[0], a[3], w.T.astype(bf16)]), attn_b, w_out)
    )
    gateup_w = gathered(
        order(planes_of, w_gate_up)
    )

    own_down = order(lambda w: w.astype(bf16), w_down)

    forget_col = jnp.pad(forget_bias, (0, heads_up - heads))[:, None]
    raw_kv, lin, message = order(
        lambda *a: whole(
            keys_in_kernel,
            [
                ((2, rows, local), f32),
                ((3 * heads_up, rows), f32),
                ((segs_up + heads_up, 2 * local), f32),
            ],
            *a,
        ),
        first_in,
        kv_w,
        packs,
        forget_col,
        seen,
        onehot,
        ends,
    )
    order.hold(piece_sets)
    blocks = [message] + [along(message, "ctx", d) for d in range(1, ctxs)]
    gain_q, gain_k = qk_gain[:1], qk_gain[1:]
    own_kv, delta, forget_q, forget_k = order(
        lambda *a: whole(
            named(keys_shift_kernel, size=size),
            [
                ((2, rows, local), bf16),
                ((2, rows, local), f32),
                ((heads // 2, 8, rows), f32),
                ((heads // 2, 8, rows * ctxs), f32),
            ],
            *a,
        ),
        raw_kv,
        lin,
        blocks,
        parent,
        start,
        key_anc,
        gain_k,
    )
    kv_blocks = [own_kv] + [along(own_kv, "ctx", d) for d in range(1, ctxs)]
    down_w = [own_down] + [
        order(
            lambda *a: whole(pieces_kernel, [((hidden_size, part), bf16)], *a)[0], place, *p
        )
        for p in piece_sets
    ]
    grad_out, d_hidden = order(
        lambda *a: whole(
            grad_hidden_kernel, [((rows, width), bf16), ((rows, hidden_size), f32)], *a
        ),
        place,
        cotangent,
        down_w,
    )
    raw_q, query, raw_g = order(
        lambda *a: whole(
            named(queries_kernel, size=size),
            [((rows, local), f32), ((rows, local), bf16), ((rows, local), f32)],
            *a,
        ),
        first_in,
        bundles,
        gain_q,
    )
    attended, gated, lse = order(
        attention, place, query, kv_blocks, bias, forget_q, forget_k, raw_g
    )

    (share,) = order(
        lambda *a: whole(attn_share_kernel, [((half, width), f32)], *a), gated, bundles
    )
    given = partner(share, "tp", 1)
    (total,) = order(
        lambda *a: whole(attn_share_sum_kernel, [((half, width), bf16)], *a),
        gated,
        bundles,
        given,
    )
    total, other = crossed(total)
    middle, second = order(
        lambda *a: whole(
            middle_kernel, [((half, width), f32), ((half, width), bf16)], *a
        ),
        place,
        tree,
        packs,
        total,
        other,
    )
    second_too = partner(second, "tp", 1)
    hidden, d_lin, keep, give = order(mlp, second, second_too, gateup_w, d_hidden)
    first_parts = owned(order.tied(first_in)[0])

    at = {}
    hidden_half, part_half = hidden_size // 2, part // 2

    def core_sum(name, kernel, out, *args):
        def run(given):
            (at[name],) = order(
                lambda *a: whole(kernel, [((half, width), out)], *a), *args, *given
            )

        return run

    def shared(kernel, *args):
        (share,) = order(lambda *a: whole(kernel, [((half, width), f32)], *a), *args)
        return partner(share, "tp", 1)

    def total_of(kernel, *args):
        (total,) = order(lambda *a: whole(kernel, [((half, width), bf16)], *a), *args)
        return crossed(total)

    def rows_at(k):
        return (k * half, (k + 1) * half)

    def out_part(d, got=()):
        return weight_grad(
            order,
            [
                (At(gated, rows=rows_at(k)), At(x, cols=(d * part, (d + 1) * part)))
                for k, x in enumerate((at["mb"], at["mb_too"]))
            ],
            got,
            min(128, local),
        )

    def summed(left_ones, right_ones, block, cols=None, lead=None, right_cols=None):
        return LineSum(
            order,
            weight_grad(
                order,
                [
                    (At(a, cols=cols), At(b, lead=lead, cols=right_cols))
                    for a, b in zip(left_ones, right_ones)
                ],
                (),
                block,
            ),
        )

    def run_bs1():
        at["bs1"] = partner(order.tied(give)[0], "tp", 1)

    def run_bs2():
        (total,) = order(
            lambda *a: whole(first_sum_kernel, [(keep.shape, bf16)], *a), keep, at["bs1"]
        )
        at["bs2"] = crossed(total)

    def column_part(d, start, stop):
        return (d * part + start, d * part + stop)

    def down_part(i, d, got=()):
        return weight_grad(
            order,
            [
                (
                    At(hidden, cols=(i * hidden_half, (i + 1) * hidden_half)),
                    At(grad_out, cols=column_part(d, 0, part)),
                )
            ],
            got,
            256,
        )

    def lin_part(lead, i, d, got=()):
        return weight_grad(
            order,
            [
                (
                    At(x, cols=column_part(d, i * part_half, (i + 1) * part_half)),
                    At(d_lin, rows=rows_at(k), lead=lead),
                )
                for k, x in enumerate((second, second_too))
            ],
            got,
            min(128, part_half),
        )

    def run_ms1():
        at["ms1"] = shared(named(share_kernel, which=1), hidden, down_w)

    def run_ms2():
        at["ms2"] = total_of(share_sum_kernel, hidden, down_w, at["ms1"])

    def run_mb():
        at["d_middle"], at["mb"], at["gain_two"] = order(
            lambda *a: whole(
                middle_back_kernel,
                [((half, width), f32), ((half, width), bf16), ((1, width), f32)],
                *a,
            ),
            grad_out,
            packs,
            middle,
            *at["bs2"],
        )
        at["mb_too"] = partner(at["mb"], "tp", 1)

    def run_gb():
        at["out_message"], at["d_raw_g"] = order(
            lambda *a: whole(
                named(gate_back_kernel, size=size),
                [((rows + row_room, local), bf16), ((rows, local), bf16)],
                *a,
            ),
            place,
            at["mb"],
            at["mb_too"],
            bundles,
            raw_g,
            attended,
            forget_q,
            lse,
        )
        at["later_outs"] = [along(at["out_message"], "ctx", -d) for d in range(1, ctxs)]

    def run_q(d):
        passed = at["queries"][-1] if d > 1 else query
        passed = order.tied(passed)[0]
        pairs = [(i, i - 1) for i in range(1, ctxs - d + 1)]
        at.setdefault("queries", []).append(lax.ppermute(passed, "ctx", pairs))

    def run_aq():
        order.hold(first_parts[1:])
        at["d_query"], at["own_grads"], at["dcq"], at["own_dck"] = order(
            query_grads, query, at["out_message"], kv_blocks, bias, forget_k
        )

    def run_ak():
        at["d_kv"], at["dck"] = order(
            key_grads,
            own_kv,
            later,
            forget_k,
            at["own_grads"],
            at["own_dck"],
            at["queries"],
            at["later_outs"],
        )

    def run_qb():
        at["d_gq"], at["gain_q"] = order(
            lambda *a: whole(
                named(query_back_kernel, size=size),
                [((rows, 2 * local), bf16), ((1, local), f32)],
                *a,
            ),
            raw_q,
            at["d_query"],
            gain_q,
            at["d_raw_g"],
        )
        at["gq"] = gathered(at["d_gq"])

    def run_fgq():
        (at["fgq"],) = order(
            lambda *a: whole(first_gq_kernel, [((rows, width), f32)], *a),
            place,
            at["d_gq"],
            bundles,
        )

    def run_sb():
        at["base"], at["message"], at["d_alpha"], at["gain_k"], at["d_forget"] = order(
            lambda *a: whole(
                named(shift_back_kernel, size=size),
                [
                    ((2, rows, local), f32),
                    ((segs_up + heads_up, 2 * local), f32),
                    ((2 * heads_up, rows), f32),
                    ((1, local), f32),
                    ((heads_up, rows), f32),
                ],
                *a,
            ),
            at["d_kv"],
            raw_kv,
            delta,
            lin,
            gain_k,
            start,
            parent,
            at["dcq"],
            at["dck"],
            onehot,
        )
        at["returned"] = [along(at["message"], "ctx", -d) for d in range(1, ctxs)]

    def run_rb():
        at["d_raw_kv"], at["d_head"], at["d_bias"] = order(
            lambda *a: whole(
                raw_back_kernel,
                [((2, rows, local), bf16), ((3 * heads_up, rows), bf16), ((heads_up, 1), f32)],
                *a,
            ),
            at["base"],
            at["message"],
            at["returned"],
            ends,
            seen,
            onehot,
            anc,
            lin,
            at["d_forget"],
            at["d_alpha"],
        )
        at["kv"] = gathered(at["d_raw_kv"])

    def first_share(which):
        return order(
            lambda *a: whole(
                named(first_share_kernel_of(part, rows), which=which), [((half, width), f32)], *a
            )[0],
            place,
            at["d_raw_kv"],
            at["d_head"],
            kv_w,
            packs,
            at["fgq"],
        )

    def run_fs1():
        at["fs1"] = partner(first_share(1), "tp", 1)

    def run_fs2():
        at["fs2"] = first_share(0)

    def run_fsum():
        at["fsum"] = total_of(first_sum_kernel, at["fs2"], at["fs1"])

    def run_eb():
        at["eb"], gain_one = order(
            lambda *a: whole(
                enter_back_kernel, [((half, width), f32), ((1, width), f32)], *a
            ),
            place,
            tree,
            packs,
            at["d_middle"],
            *at["fsum"],
        )
        at["eb_too"] = partner(at["eb"], "tp", 1)
        at["gains"] = jnp.concatenate([gain_one, at["gain_two"]], axis=0)
        at["gains_too"] = partner(at["gains"], "tp", 1)

    def settle(name, kind):
        (at[name],) = order(
            lambda *a: whole(named(settle_kernel, shards=shards), [((rows, width), kind)], *a),
            place,
            at[name],
            at[name + "_too"],
        )

    def run_lv():
        (at["lv"],) = order(
            lambda *a: whole(leave_kernel, [((half, width), bf16)], *a), middle, *at["ms2"]
        )
        at["lv_too"] = partner(at["lv"], "tp", 1)

    def run_sm():
        at["sm"] = order(
            lambda *a: whole(
                small_kernel, [((40, max(part, local)), f32) for _ in range(shards)], *a
            ),
            at["d_head"],
            first_in,
            at["gains"],
            at["gains_too"],
            at["gain_q"],
            at["gain_k"],
            at["d_bias"],
        )
        at["sm_got"] = [from_ring(at["sm"][d], "shard", shards - d) for d in range(1, shards)]

    def run_sm1():
        small = at["sm"][0]
        for got in at["sm_got"]:
            small = order(add_rows, small, got)
        at["small"] = LineSum(order, small)

    def run_smf():
        line = at["small"]
        line.step()

        def pick(total, *ends):
            if ends:
                total = jnp.where((ctx == 0) | (ctx == ctxs - 1), ends[0], total)
            table = total[: 3 * heads_up, :part].reshape(3, heads_up, part)[:, :heads]
            return (
                total[24:26, :part],
                jnp.transpose(table, (2, 0, 1)),
                total[32 : 32 + heads, 0],
                total[26:28, :local],
            )

        ends = [line.coming] if line.coming is not None else []
        found = order(pick, line.total, *ends)
        at["small_gain"], at["small_heads"], at["small_bias"], at["small_qk"] = found

    def run_out(name, *planes):
        at[name] = spread_out(order, place, [[at[n] for n in plane] for plane in planes])

    block = min(128, part)
    work = {
        "bs1": run_bs1, "bs2": run_bs2,
        "ms1": run_ms1, "ms2": run_ms2, "mb": run_mb, "gb": run_gb,
        "q1": lambda: run_q(1), "q2": lambda: run_q(2),
        "q3": lambda: [run_q(d) for d in range(3, ctxs)], "aq": run_aq, "ak": run_ak, "qb": run_qb, "fgq": run_fgq,
        "sb": run_sb, "rb": run_rb, "fs1": run_fs1, "fs2": run_fs2, "fsum": run_fsum,
        "eb": run_eb, "st": lambda: settle("eb", f32), "lv": run_lv,
        "so": lambda: settle("lv", bf16), "sm": run_sm, "sm1": run_sm1, "smf": run_smf,
        "gu": lambda: run_out("gu", ("G0", "G1"), ("U0", "U1")),
        "df": lambda: run_out("df", ("D0", "D1")), "of": lambda: run_out("of", ("O",)),
        "at": lambda: run_out("at", ("Qq",), ("K",), ("V",), ("Qg",)),
    }
    starts = {
        "Qg1": lambda: summed(first_parts, at["gq"], block, right_cols=(0, local)),
        "Qq1": lambda: summed(first_parts, at["gq"], block, right_cols=(local, 2 * local)),
        "K1": lambda: summed(first_parts, at["kv"], block, lead=0),
        "V1": lambda: summed(first_parts, at["kv"], block, lead=1),
    }
    makes = {"O": out_part}
    for i in range(2):
        makes[f"D{i}"] = functools.partial(down_part, i)
        for lead, name in enumerate("GU"):
            makes[f"{name}{i}"] = functools.partial(lin_part, lead, i)
    for name, make in makes.items():

        def hand_over(name=name, make=make):
            at[name + "0"] = [
                from_ring(make(d), "shard", shards - d) for d in range(1, shards)
            ]

        work[name + "0"] = hand_over
        starts[name + "1"] = lambda name=name, make=make: LineSum(
            order, make(0, at[name + "0"])
        )
    for name in schedule:
        if name in work:
            work[name]()
        elif name in starts:
            at[name[:-1]] = starts[name]()
        else:
            at["small" if name[:2] == "sm" else name[:-1]].step()
    return (
        settled(at["lv"])[None],
        settled(at["eb"])[None],
        at["small_gain"],
        at["at"],
        at["small_heads"],
        at["small_bias"],
        at["small_qk"],
        at["of"],
        at["gu"],
        at["df"],
    )


def first_share_kernel_of(part, rows):
    def first_share_scoped_kernel(*refs, which):
        pl.run_scoped(
            lambda scratch: first_share_kernel(*refs, scratch, which=which),
            pltpu.VMEM((rows, part), f32),
        )

    return first_share_scoped_kernel


def solution(mesh):
    in_specs = (
        P("shard", "ctx", None),
        P("shard", None),
        P("shard", None),
        P("shard", "ctx"),
        P(None, "shard"),
        P("shard", None, "tp"),
        P("shard", None, "tp"),
        P("tp"),
        P(None, "tp"),
        P("tp", "shard"),
        P("shard", None, "tp"),
        P("tp", "shard"),
        P("shard", "ctx", None),
    )
    out_specs = (
        P("shard", "ctx", None),
        P("shard", "ctx", None),
        P(None, "shard"),
        P("shard", None, "tp"),
        P("shard", None, "tp"),
        P("tp"),
        P(None, "tp"),
        P("tp", "shard"),
        P("shard", None, "tp"),
        P("tp", "shard"),
    )
    return jax.shard_map(body, mesh=mesh, in_specs=in_specs, out_specs=out_specs, check_vma=False)
```

```python
import functools

import jax
import jax.numpy as jnp
from jax import lax
from jax.experimental import pallas as pl
from jax.experimental.pallas import tpu as pltpu
from jax.sharding import PartitionSpec as P

epsilon = 1e-06
neg_large = -1e30
f32 = jnp.float32
bf16 = jnp.bfloat16
segs_up = 16


def from_ring(values, axis, step):
    count = lax.axis_size(axis)
    return lax.ppermute(values, axis, [((i + step) % count, i) for i in range(count)])


def along(values, axis, step):
    count = lax.axis_size(axis)
    return lax.ppermute(
        values, axis, [(i, i + step) for i in range(count) if 0 <= i + step < count]
    )


def partner(values, axis, bit):
    count = lax.axis_size(axis)
    return lax.ppermute(values, axis, [(i, i ^ bit) for i in range(count)])


def dot_of(dims, precision=None):
    def product(left, right):
        return lax.dot_general(
            left, right, (dims, ((), ())), precision=precision, preferred_element_type=f32
        )

    return product


mm = dot_of(((1,), (0,)))
mm_nt = dot_of(((1,), (1,)))
mm_tn = dot_of(((0,), (0,)))


def bf16_pieces(values, count):
    pieces = []
    for _ in range(count - 1):
        pieces.append(values.astype(bf16))
        values = values - pieces[-1].astype(f32)
    return pieces + [values.astype(bf16)]


def exact_by(product, side):
    def exactly(left, right, count=3):
        if side == 0:
            right = right.astype(bf16)
            return sum(product(p, right) for p in bf16_pieces(left, count))
        left = left.astype(bf16)
        return sum(product(left, p) for p in bf16_pieces(right, count))

    return exactly


left_exact, left_exact_nt, left_exact_tn = (exact_by(p, 0) for p in (mm, mm_nt, mm_tn))
right_exact, right_exact_nt, right_exact_tn = (exact_by(p, 1) for p in (mm, mm_nt, mm_tn))


def rms_scale(values):
    return lax.rsqrt(jnp.mean(values * values, axis=-1, keepdims=True) + epsilon)


def norm_grad(values, scale, gain_row, d_result):
    normed = values * scale
    d_normed = d_result * gain_row
    d_values = scale * (d_normed - normed * jnp.mean(d_normed * normed, axis=-1, keepdims=True))
    return d_values, jnp.sum(d_result * normed, axis=0, keepdims=True)


def iota(shape, axis):
    return lax.broadcasted_iota(jnp.int32, shape, axis)


def same_head(width, size):
    return jnp.where(iota((width, width), 0) // size == iota((width, width), 1) // size, 1.0, 0.0)


def head_mean(values, size):
    return left_exact(values, same_head(values.shape[1], size), 2) * (1.0 / size)


def head_scale(values, size):
    return lax.rsqrt(head_mean(values * values, size) + epsilon)


def head_grad(values, gain_row, d_result, size):
    scale = head_scale(values, size)
    normed = values * scale
    d_normed = d_result * gain_row
    d_values = scale * (d_normed - normed * head_mean(d_normed * normed, size))
    return d_values, jnp.sum(d_result * normed, axis=0, keepdims=True)


def spread_of(heads_up, width, size):
    return jnp.where(iota((heads_up, width), 0) == iota((heads_up, width), 1) // size, 1.0, 0.0)


def nbytes(leaf):
    return leaf.size * leaf.dtype.itemsize


def whole(kernel, outs, *args, extra=8):
    leaves, form = jax.tree.flatten(args)

    def flat(*refs):
        kernel(*jax.tree.unflatten(form, refs[: len(leaves)]), *refs[len(leaves) :])

    shapes = [jax.ShapeDtypeStruct(shape, kind) for shape, kind in outs]
    spaces = [
        pltpu.SMEM if leaf.ndim == 1 and leaf.dtype == jnp.int32 else pltpu.VMEM
        for leaf in leaves
    ]
    size = sum(nbytes(x) for x in leaves) + sum(nbytes(x) for x in shapes)
    found = pl.pallas_call(
        flat,
        out_shape=shapes,
        in_specs=[pl.BlockSpec(memory_space=s) for s in spaces],
        out_specs=[pl.BlockSpec(memory_space=pltpu.VMEM) for _ in shapes],
        compiler_params=pltpu.CompilerParams(
            vmem_limit_bytes=min(60 << 20, size + size // 4 + (extra << 20))
        ),
        cost_estimate=pl.CostEstimate(flops=1, transcendentals=1, bytes_accessed=1),
        name=kernel.__name__,
    )(*leaves)
    return found


def masks_kernel(place, low, high, high_col, parents_col, seg_col, bias, later, seen, key_anc, onehot, parent, start, ends, anc, key_onehot):
    rows = seg_col.shape[0]
    ctx = place[2]
    lanes = iota((segs_up, segs_up), 1)
    parent_mat = jnp.where(parents_col[...] == lanes, 1.0, 0.0)
    eye = jnp.where(iota((segs_up, segs_up), 0) == lanes, 1.0, 0.0)
    ancestry = eye + parent_mat + right_exact(parent_mat, parent_mat, 1)
    anc[...] = ancestry
    mine = jnp.where(seg_col[...] == iota((rows, segs_up), 1), 1.0, 0.0)
    onehot[...] = mine
    parent[...] = right_exact(mine, parent_mat, 1)
    mine_anc = right_exact(mine, ancestry, 1)
    query_pos = ctx * rows + iota((1, rows), 1)
    query_col = ctx * rows + iota((rows, 1), 0)
    ends[...] = jnp.where(query_pos == high_col[...] - 1, 1.0, 0.0)
    start[...] = jnp.sum(
        jnp.where(query_col == low[...], 1.0, 0.0), axis=1, keepdims=True
    )
    for d in range(bias.shape[0] // rows):
        span = slice(d * rows, (d + 1) * rows)
        key_pos = (ctx - d) * rows + iota((rows, 1), 0)
        keys = jnp.where((key_pos >= low[...]) & (key_pos < high[...]), 1.0, 0.0)
        key_anc[span, :] = right_exact(keys, ancestry, 1)
        key_onehot[span, :] = keys
        linked = mm_nt(keys.astype(bf16), mine_anc.astype(bf16)) > 0.5
        visible = linked & (key_pos <= query_pos)
        bias[span, :] = jnp.where(visible, 0.0, neg_large)
        if d == 0:
            seen[...] = jnp.where(visible, 1.0, 0.0)
            own_keys = keys.astype(bf16)
    for d in range(1, bias.shape[0] // rows):
        span = slice((d - 1) * rows, d * rows)
        query_at = (ctx + d) * rows + iota((rows, 1), 0)
        theirs = jnp.where((query_at >= low[...]) & (query_at < high[...]), 1.0, 0.0)
        theirs = right_exact(theirs, ancestry, 1).astype(bf16)
        later[span, :] = jnp.where(mm_nt(own_keys, theirs) > 0.5, 0.0, neg_large)


def turned(values, first, count):
    width = values.shape[1] // count
    pieces = [
        lax.dynamic_slice_in_dim(values, lax.rem(first + i, count) * width, width, 1)
        for i in range(count)
    ]
    return jnp.concatenate(pieces, axis=1)


def part_at(ref, shard, d, shards, rows=slice(None)):
    part = ref.shape[1] // shards
    if part % 128:
        return ref[rows, d * part : (d + 1) * part]
    start = pl.multiple_of(lax.rem(shard + d, shards) * part, 128)
    return ref[rows, pl.ds(start, part)]


def enter_kernel(place, tokens, packs, first_in):
    shards = len(packs)
    part = packs[0].shape[1]
    pieces = [part_at(tokens, place[1], d, shards).astype(f32) for d in range(shards)]
    mean = sum(jnp.sum(x * x, axis=1, keepdims=True) for x in pieces) * (
        1.0 / tokens.shape[1]
    )
    scale = lax.rsqrt(mean + epsilon)
    for d in range(shards):
        gain = packs[d][24:25, :].astype(f32)
        first_in[:, d * part : (d + 1) * part] = (pieces[d] * scale * gain).astype(bf16)


def keys_in_kernel(first_in, kv_w, packs, forget_bias, seen, onehot, ends, raw_kv, lin, message):
    part = packs[0].shape[1]
    rows = first_in.shape[0]
    local = raw_kv.shape[2]
    heads_up = forget_bias.shape[0]
    cuts = [first_in[:, d * part : (d + 1) * part] for d in range(len(packs))]
    head_lin = sum(mm_nt(p[:24, :], x) for p, x in zip(packs, cuts))
    forget_in = head_lin[:heads_up] + forget_bias[...]
    lin[...] = head_lin
    lin[:heads_up, :] = forget_in
    log_forget = jnp.minimum(forget_in, 0.0) - jnp.log1p(jnp.exp(-jnp.abs(forget_in)))
    message[...] = jnp.zeros_like(message)
    for i in range(2):
        raw = sum(mm(x, w[i]) for w, x in zip(kv_w, cuts))
        raw_kv[i] = raw
        cols = slice(i * local, (i + 1) * local)
        message[:segs_up, cols] = right_exact(ends[...], raw)
        message[segs_up - 1 : segs_up, cols] = raw[rows - 1 :]
    message[segs_up : segs_up + heads_up, :rows] = left_exact(log_forget, seen[...])
    message[segs_up : segs_up + heads_up, local : local + segs_up] = left_exact(
        log_forget, onehot[...]
    )


def keys_shift_kernel(raw_kv, lin, blocks, parent, start, key_anc, gain, own_kv, delta, fq, fk, *, size):
    rows, local = raw_kv.shape[1:]
    heads_up = lin.shape[0] // 3
    spread = spread_of(heads_up, local, size)
    seg_ends = sum((b[:segs_up, :] for b in blocks[1:]), blocks[0][:segs_up, :])
    at_start = start[...] > 0.5
    at_top = iota((rows, 1), 0) == 0
    for i in range(2):
        cols = slice(i * local, (i + 1) * local)
        alpha_rows = jax.nn.sigmoid(lin[(i + 1) * heads_up : (i + 2) * heads_up, :])
        alpha = left_exact_tn(alpha_rows, spread)
        raw = raw_kv[i]
        previous = jnp.where(
            at_top, blocks[1][segs_up - 1 : segs_up, cols], pltpu.roll(raw, 1, 0)
        )
        previous = jnp.where(at_start, right_exact(parent[...], seg_ends[:, cols]), previous)
        step = previous - raw
        delta[i] = step
        shifted = raw + alpha * step
        if i == 0:
            shifted = shifted * head_scale(shifted, size) * gain[...]
        own_kv[i] = shifted.astype(bf16)
    table = slice(segs_up, segs_up + heads_up)
    for d in range(len(blocks)):
        sums = blocks[d][table, :rows]
        span = slice(d * rows, (d + 1) * rows)
        later = blocks[d + 1 :]
        if later:
            before = sum(
                (b[table, local : local + segs_up] for b in later[1:]),
                later[0][table, local : local + segs_up],
            )
            sums = sums + left_exact_nt(before, key_anc[span, :])
        for h in range(2 * fk.shape[0]):
            fk[h // 2, h % 2 : h % 2 + 1, span] = sums[h : h + 1]
            if d == 0:
                fq[h // 2, h % 2 : h % 2 + 1, :] = sums[h : h + 1]


def queries_kernel(first_in, bundles, gain, raw_q, query, raw_g, *, size):
    part = bundles[0].shape[1]
    cuts = [first_in[:, d * part : (d + 1) * part] for d in range(len(bundles))]
    raw = sum(mm(x, w[0]) for w, x in zip(bundles, cuts))
    raw_q[...] = raw
    raw_g[...] = sum(mm(x, w[1]) for w, x in zip(bundles, cuts))
    normed = (raw * head_scale(raw, size) * gain[...]).astype(bf16)
    query[...] = (normed.astype(f32) * (size**-0.5)).astype(bf16)


def attn_share_kernel(values, bundles, out):
    half = out.shape[0]
    part = bundles[0].shape[1]
    for d, w in enumerate(bundles):
        out[:, d * part : (d + 1) * part] = mm_nt(values[half:, :], w[2])


def attn_share_sum_kernel(values, bundles, given, out):
    half = out.shape[0]
    part = bundles[0].shape[1]
    for d, w in enumerate(bundles):
        cols = slice(d * part, (d + 1) * part)
        out[:, cols] = (mm_nt(values[:half, :], w[2]) + given[:, cols]).astype(bf16)


def share_kernel(values, weights, out, *, which):
    half = out.shape[0]
    part = out.shape[1] // len(weights)
    rows = slice(which * half, (which + 1) * half)
    for d, w in enumerate(weights):
        out[:, d * part : (d + 1) * part] = mm(values[rows, :], w[...])


def share_sum_kernel(values, weights, given, out):
    half = out.shape[0]
    part = out.shape[1] // len(weights)
    for d, w in enumerate(weights):
        cols = slice(d * part, (d + 1) * part)
        out[:, cols] = (mm(values[:half, :], w[...]) + given[:, cols]).astype(bf16)


def middle_kernel(place, tokens, packs, total, other, middle, second_in):
    shards = len(packs)
    part = packs[0].shape[1]
    half = total.shape[0]
    rows = pl.ds(pl.multiple_of(place[0] * half, 16), half)
    square = jnp.zeros((half, 1), f32)
    for d in range(shards):
        cols = slice(d * part, (d + 1) * part)
        value = part_at(tokens, place[1], d, shards, rows).astype(f32) + (
            total[:, cols].astype(f32) + other[:, cols].astype(f32)
        )
        middle[:, cols] = value
        square = square + jnp.sum(value * value, axis=1, keepdims=True)
    scale = lax.rsqrt(square * (1.0 / middle.shape[1]) + epsilon)
    for d in range(shards):
        cols = slice(d * part, (d + 1) * part)
        gain = packs[d][25:26, :].astype(f32)
        second_in[:, cols] = (middle[:, cols] * scale * gain).astype(bf16)


def grad_hidden_kernel(place, cotangent, down_w, grad_out, d_hidden):
    shards = len(down_w)
    part = down_w[0].shape[1]
    half = cotangent.shape[0] // 2
    for k in range(2):
        rows = pl.ds(pl.multiple_of(lax.rem(place[0] + k, 2) * half, 16), half)
        span = slice(k * half, (k + 1) * half)
        for d in range(shards):
            grad_out[span, d * part : (d + 1) * part] = part_at(
                cotangent, place[1], d, shards, rows
            )
    d_hidden[...] = sum(
        mm_nt(grad_out[:, d * part : (d + 1) * part], w[...]) for d, w in enumerate(down_w)
    )


def mlp_kernel(*refs):
    mine, theirs = refs[:2]
    d_hidden, hidden, d_lin, keep, give, second = refs[-6:]
    weights = refs[2:-6]
    part = weights[0].shape[1]
    half = mine.shape[0]

    @pl.when(pl.program_id(0) == 0)
    def _():
        second[:half, :] = mine[...]
        second[half:, :] = theirs[...]

    lin = [
        sum(mm(second[:, d * part : (d + 1) * part], w[i]) for d, w in enumerate(weights))
        for i in range(2)
    ]
    sig = jax.nn.sigmoid(lin[0])
    silu = lin[0] * sig
    grad = d_hidden[...]
    hidden[...] = (silu * lin[1]).astype(bf16)
    d_gate = (grad * lin[1] * (sig * (1.0 + lin[0] * (1.0 - sig)))).astype(bf16)
    d_up = (grad * silu).astype(bf16)
    d_lin[0] = d_gate
    d_lin[1] = d_up
    for d, w in enumerate(weights):
        value = mm_nt(d_gate, w[0]) + mm_nt(d_up, w[1])
        for share, rows in ((keep, slice(0, half)), (give, slice(half, 2 * half))):

            @pl.when(pl.program_id(0) == 0)
            def _():
                share[d] = value[rows]

            @pl.when(pl.program_id(0) > 0)
            def _():
                share[d] = share[d] + value[rows]


def mlp(mine, theirs, weights, d_hidden):
    half, width = mine.shape
    rows, hidden_size = d_hidden.shape
    shards = len(weights)
    part = weights[0].shape[1]
    block = 512
    flat = pl.BlockSpec((half, width), lambda j: (0, 0))
    share = pl.BlockSpec((shards, half, part), lambda j: (0, 0, 0))
    return pl.pallas_call(
        mlp_kernel,
        grid=(hidden_size // block,),
        in_specs=[flat, flat]
        + [pl.BlockSpec((2, part, block), lambda j: (0, 0, j)) for _ in weights]
        + [pl.BlockSpec((rows, block), lambda j: (0, j))],
        out_specs=[
            pl.BlockSpec((rows, block), lambda j: (0, j)),
            pl.BlockSpec((2, rows, block), lambda j: (0, 0, j)),
            share,
            share,
        ],
        out_shape=[
            jax.ShapeDtypeStruct((rows, hidden_size), bf16),
            jax.ShapeDtypeStruct((2, rows, hidden_size), bf16),
            jax.ShapeDtypeStruct((shards, half, part), f32),
            jax.ShapeDtypeStruct((shards, half, part), f32),
        ],
        scratch_shapes=[pltpu.VMEM((rows, width), bf16)],
        compiler_params=pltpu.CompilerParams(vmem_limit_bytes=26 << 20),
        cost_estimate=pl.CostEstimate(flops=1, transcendentals=1, bytes_accessed=1),
        name="mlp",
    )(mine, theirs, *weights, d_hidden)


def gain_row(packs, row):
    return jnp.concatenate([p[row : row + 1, :].astype(f32) for p in packs], axis=1)


def middle_back_kernel(grad_out, packs, middle, total, other, d_middle, d_middle_b, d_gain):
    half = middle.shape[0]
    value = middle[...]
    d_second = jnp.concatenate(
        [total[d].astype(f32) + other[d].astype(f32) for d in range(total.shape[0])], axis=1
    )
    d_value, gain = norm_grad(value, rms_scale(value), gain_row(packs, 25), d_second)
    d_gain[...] = gain
    d_value = d_value + grad_out[:half, :].astype(f32)
    d_middle[...] = d_value
    d_middle_b[...] = d_value.astype(bf16)


row_room = 48


def row_pieces(values):
    return jnp.concatenate([p.astype(f32) for p in bf16_pieces(values, 3)], axis=0)


def rows_back(block, start):
    pieces = block[...].astype(f32)[start : start + 24]
    return pieces[:8] + pieces[8:16] + pieces[16:]


def head_row(rows8, head):
    return jnp.sum(jnp.where(iota(rows8.shape, 0) == head, rows8, 0.0), axis=0, keepdims=True)


def gate_back_kernel(
    place, mine, theirs, bundles, raw_g, attended, forget_q, lse, message, d_raw_g, *, size
):
    half = mine.shape[0]
    rows, local = raw_g.shape
    part = bundles[0].shape[1]
    for k, source in enumerate((mine, theirs)):
        at = pl.ds(pl.multiple_of(lax.rem(place[0] + k, 2) * half, 16), half)
        d_gated = sum(
            mm(source[:, d * part : (d + 1) * part], w[2]) for d, w in enumerate(bundles)
        )
        sig = jax.nn.sigmoid(raw_g[at, :])
        message[at, :] = (d_gated * sig).astype(bf16)
        d_raw_g[at, :] = (d_gated * attended[at, :] * sig * (1.0 - sig)).astype(bf16)
    products = message[:rows, :].astype(f32) * attended[...]
    delta = right_exact_nt(spread_of(8, local, size), products)
    heads = 2 * forget_q.shape[0]
    forget = [
        forget_q[h // 2, h % 2 : h % 2 + 1, :] - lse[h // 2, h % 2 : h % 2 + 1, :]
        for h in range(heads)
    ]
    forget = jnp.concatenate(forget + [jnp.zeros((8 - heads, rows), f32)], axis=0)
    message[rows:, :] = jnp.concatenate(
        [row_pieces(forget), row_pieces(delta)], axis=0
    ).astype(bf16)


def query_back_kernel(raw_q, d_query, gain, d_raw_g, d_gq, d_gain, *, size):
    local = raw_q.shape[1]
    d_raw, gain_grad = head_grad(raw_q[...], gain[...], d_query[...], size)
    d_gain[...] = gain_grad
    d_gq[:, :local] = d_raw_g[...]
    d_gq[:, local:] = d_raw.astype(bf16)


def shift_back_kernel(
    d_kv, raw_kv, delta, lin, gain, start, parent, dcq, dck, onehot,
    base, message, d_alpha, d_gain, d_forget, *, size,
):
    rows, local = raw_kv.shape[1:]
    heads_up = lin.shape[0] // 3
    heads = 2 * dcq.shape[0]
    spread = spread_of(heads_up, local, size)
    not_start = 1.0 - start[...]
    start_parent = parent[...] * start[...]
    message[...] = jnp.zeros_like(message)
    for i in range(2):
        cols = slice(i * local, (i + 1) * local)
        alpha_rows = jax.nn.sigmoid(lin[(i + 1) * heads_up : (i + 2) * heads_up, :])
        alpha = left_exact_tn(alpha_rows, spread)
        d_shift = d_kv[i]
        if i == 0:
            shifted = raw_kv[0] + alpha * delta[0]
            d_shift, gain_grad = head_grad(shifted, gain[...], d_shift, size)
            d_gain[...] = gain_grad
        d_alpha[i * heads_up : (i + 1) * heads_up, :] = (
            right_exact_nt(spread, d_shift * delta[i], 2) * alpha_rows * (1.0 - alpha_rows)
        )
        d_prev = alpha * d_shift
        d_step = d_prev * not_start
        base[i] = (
            d_shift
            - d_prev
            + jnp.where(iota((rows, 1), 0) == rows - 1, 0.0, pltpu.roll(d_step, rows - 1, 0))
        )
        message[:segs_up, cols] = right_exact_tn(start_parent, d_prev, 2)
        message[segs_up - 1 : segs_up, cols] = d_step[:1]
    grads = [
        dcq[h // 2, h % 2 : h % 2 + 1, :] - dck[h // 2, h % 2 : h % 2 + 1, :]
        for h in range(heads)
    ]
    grads = jnp.concatenate(grads + [jnp.zeros((heads_up - heads, rows), f32)], axis=0)
    d_forget[...] = grads
    message[segs_up : segs_up + heads_up, local : local + segs_up] = left_exact(
        grads, onehot[...]
    )


def raw_back_kernel(
    base, table_own, returned, ends, seen, onehot, anc, lin, d_forget_own, d_alpha,
    d_raw_kv, d_lin, d_bias,
):
    rows, local = base.shape[1:]
    heads_up = lin.shape[0] // 3
    tail = slice(segs_up, segs_up + heads_up)
    for i in range(2):
        cols = slice(i * local, (i + 1) * local)
        table = table_own[:segs_up, cols]
        for r in returned:
            table = table + r[:segs_up, cols]
        edge = jnp.where(
            iota((rows, 1), 0) == rows - 1, returned[0][segs_up - 1 : segs_up, cols], 0.0
        )
        d_raw_kv[i] = (base[i] + edge + right_exact_tn(ends[...], table, 2)).astype(bf16)
    own = d_forget_own[...]
    sums = jnp.zeros((heads_up, segs_up), f32)
    for r in returned:
        sums = sums + r[tail, local : local + segs_up]
    d_log = left_exact_nt(own, seen[...]) + left_exact_nt(
        left_exact(sums, anc[...]), onehot[...]
    )
    d_forget = d_log * jax.nn.sigmoid(-lin[:heads_up, :])
    d_bias[...] = jnp.sum(d_forget, axis=1, keepdims=True)
    d_lin[:heads_up, :] = d_forget.astype(bf16)
    d_lin[heads_up:, :] = d_alpha[...].astype(bf16)


def first_gq_kernel(place, d_gq, bundles, out):
    half = d_gq.shape[0] // 2
    part = bundles[0].shape[1]
    local = d_gq.shape[1] // 2
    for k in range(2):
        rows = pl.ds(pl.multiple_of(lax.rem(place[0] + k, 2) * half, 16), half)
        for d, w in enumerate(bundles):
            out[k * half : (k + 1) * half, d * part : (d + 1) * part] = mm_nt(
                d_gq[rows, :local], w[1]
            ) + mm_nt(d_gq[rows, local:], w[0])


def first_share_kernel(place, d_kv, d_lin, kv_w, packs, partial, out, heads_part, *, which):
    half = out.shape[0]
    part = packs[0].shape[1]
    rows = pl.ds(pl.multiple_of(lax.rem(place[0] + which, 2) * half, 16), half)
    for d in range(len(packs)):
        cols = slice(d * part, (d + 1) * part)
        heads_part[...] = mm_tn(d_lin[...], packs[d][:24, :])
        out[:, cols] = (
            mm_nt(d_kv[0, rows, :], kv_w[d][0])
            + mm_nt(d_kv[1, rows, :], kv_w[d][1])
            + heads_part[rows, :]
            + partial[which * half : (which + 1) * half, cols]
        ).astype(out.dtype)


def first_sum_kernel(mine, given, out):
    out[...] = (mine[...] + given[...]).astype(bf16)


def enter_back_kernel(place, tokens, packs, d_middle, total, other, d_own, d_gain):
    shards = len(packs)
    half = total.shape[0]
    rows = pl.ds(pl.multiple_of(place[0] * half, 16), half)
    value = jnp.concatenate(
        [part_at(tokens, place[1], d, shards, rows).astype(f32) for d in range(shards)], axis=1
    )
    d_first = total[...].astype(f32) + other[...].astype(f32)
    d_value, gain = norm_grad(value, rms_scale(value), gain_row(packs, 24), d_first)
    d_gain[...] = gain
    d_own[...] = d_middle[...] + d_value


def settle_kernel(place, mine, theirs, out, *, shards):
    half = mine.shape[0]
    part = mine.shape[1] // shards
    for k, source in enumerate((mine, theirs)):
        rows = pl.ds(pl.multiple_of(lax.rem(place[0] + k, 2) * half, 16), half)
        for d in range(shards):
            cols = slice(d * part, (d + 1) * part)
            if part % 128:
                out[rows, cols] = source[:, cols]
            else:
                start = pl.multiple_of(lax.rem(place[1] + d, shards) * part, 128)
                out[rows, pl.ds(start, part)] = source[:, cols]


def leave_kernel(middle, total, other, out):
    out[...] = (
        middle[...] + (total[...].astype(f32) + other[...].astype(f32))
    ).astype(bf16)


def named(kernel, **fixed):
    def bound(*refs):
        kernel(*refs, **fixed)

    bound.__name__ = kernel.__name__
    return bound


def planes_of(weights):
    rows, count, width = weights.shape
    block = 128 if rows % 128 == 0 else rows

    def planes_kernel(source, out):
        for i in range(count):
            out[i] = source[:, i, :].astype(bf16)

    return pl.pallas_call(
        planes_kernel,
        grid=(rows // block,),
        in_specs=[pl.BlockSpec((block, count, width), lambda j: (j, 0, 0))],
        out_specs=pl.BlockSpec((count, block, width), lambda j: (0, j, 0)),
        out_shape=jax.ShapeDtypeStruct((count, rows, width), bf16),
        compiler_params=pltpu.CompilerParams(vmem_limit_bytes=12 << 20),
        cost_estimate=pl.CostEstimate(flops=1, transcendentals=1, bytes_accessed=1),
        name="planes",
    )(weights)


class At:

    def __init__(self, array, rows=None, cols=None, lead=None):
        if cols and (cols[0] % 128 or cols[1] % 128):
            array, cols = array[..., cols[0] : cols[1]], None
        self.array, self.lead = array, lead
        self.rows = rows or (0, array.shape[-2])
        self.cols = cols or (0, array.shape[-1])

    def spec(self, block=None):
        start, stop = self.rows
        height = stop - start
        first, last = self.cols
        wide = block or last - first
        shape, row, col = (height, wide), start // height, first // wide

        def at(j):
            return (row, col + j if block else col)

        if self.lead is None:
            return pl.BlockSpec(shape, at)
        return pl.BlockSpec((None,) + shape, lambda j: (self.lead,) + at(j))


def weight_grad(order, pairs, got, block):
    count = len(pairs)
    rows = pairs[0][0].cols[1] - pairs[0][0].cols[0]
    width = pairs[0][1].cols[1] - pairs[0][1].cols[0]

    def weight_grad_kernel(*refs):
        total = mm_tn(refs[0][...], refs[1][...])
        for i in range(1, count):
            total = total + mm_tn(refs[2 * i][...], refs[2 * i + 1][...])
        for ref in refs[2 * count : -1]:
            total = total + ref[...].astype(f32)
        refs[-1][...] = total.astype(bf16)

    specs = [spec for a, b in pairs for spec in (a.spec(block), b.spec())]
    over = pl.BlockSpec((block, width), lambda j: (j, 0))
    call = pl.pallas_call(
        weight_grad_kernel,
        grid=(rows // block,),
        in_specs=specs + [over for _ in got],
        out_specs=over,
        out_shape=jax.ShapeDtypeStruct((rows, width), bf16),
        compiler_params=pltpu.CompilerParams(vmem_limit_bytes=20 << 20),
        cost_estimate=pl.CostEstimate(flops=1, transcendentals=1, bytes_accessed=1),
        name="weight_grad",
    )
    return order(call, *[x.array for pair in pairs for x in pair], *got)


def add_rows(left, right):
    rows, width = left.shape
    block = rows if rows % 64 else 64 if rows <= 256 else 128

    def add_kernel(left, right, out):
        out[...] = (left[...].astype(f32) + right[...].astype(f32)).astype(out.dtype)

    over = pl.BlockSpec((block, width), lambda j: (j, 0))
    return pl.pallas_call(
        add_kernel,
        grid=(rows // block,),
        in_specs=[over, over],
        out_specs=over,
        out_shape=jax.ShapeDtypeStruct((rows, width), left.dtype),
        compiler_params=pltpu.CompilerParams(vmem_limit_bytes=8 << 20),
        cost_estimate=pl.CostEstimate(flops=1, transcendentals=1, bytes_accessed=1),
        name="add",
    )(left, right)


def attend_kernel(*refs):
    place, query_ref, *kv_refs, bias_ref, cq_ref, ck_ref, gate_ref, out_ref, gated_ref, lse_ref = refs
    rows = query_ref.shape[0]
    half = rows // 2
    size = query_ref.shape[1] // 2
    key_cols = ck_ref[0].T
    outs = []
    for e in range(2):
        cols = slice(e * size, (e + 1) * size)
        query = query_ref[:, cols]
        forget_row = cq_ref[0, e : e + 1, :]
        total = jnp.zeros((1, rows), f32)
        mixed = jnp.zeros((size, rows), f32)
        for d in range(len(kv_refs) // 2):
            span = slice(d * rows, (d + 1) * rows)
            scores = mm_nt(kv_refs[2 * d][0, :, cols], query)
            scores = scores + (forget_row - key_cols[span, e : e + 1]) + bias_ref[span, :]
            weights = jnp.exp(scores)
            total = total + jnp.sum(weights, axis=0, keepdims=True)
            mixed = mixed + mm_tn(kv_refs[2 * d + 1][0, :, cols], weights.astype(bf16))
        outs.append((mixed / total).T)
        lse_ref[0, e : e + 1, :] = jnp.log(total)
    attended = jnp.concatenate(outs, axis=1)
    out_ref[...] = attended
    gated = (attended * jax.nn.sigmoid(gate_ref[...])).astype(bf16)
    for k in range(2):
        there = pl.ds(pl.multiple_of(lax.rem(place[0] + k, 2) * half, 16), half)
        gated_ref[there, :] = gated[k * half : (k + 1) * half]


def score_grads(key, value, query, d_out, forget_row, delta_row, key_col, bias):
    scores = mm_nt(key, query) + (forget_row - key_col) + bias
    probs = jnp.exp(scores)
    d_scores = probs * (mm_nt(value, d_out) - delta_row)
    return probs.astype(bf16), d_scores.astype(bf16)


def first_col(rows, size):
    return jnp.where(iota((rows, size), 1) == 0, 1.0, 0.0).astype(bf16)


def as_rows(columns):
    pad = jnp.zeros((columns[0].shape[0], 8 - len(columns)), f32)
    return jnp.concatenate(columns + [pad], axis=1).T


def query_grads_kernel(*refs):
    query_ref, d_out_ref, row_values = refs[:3]
    kv_refs = refs[3:-6]
    bias_ref, ck_ref, d_query_ref, d_kv_ref, dcq_ref, dck_ref = refs[-6:]
    rows = query_ref.shape[0]
    size = query_ref.shape[1] // 2
    key_cols = ck_ref[0].T
    forget8, delta8 = rows_back(row_values, 0), rows_back(row_values, 24)
    sums = []
    for e in range(2):
        cols = slice(e * size, (e + 1) * size)
        head = 2 * pl.program_id(0) + e
        query = query_ref[:, cols]
        d_out = d_out_ref[:, cols]
        forget_row, delta_row = head_row(forget8, head), head_row(delta8, head)
        d_query = jnp.zeros((rows, size), f32)
        d_row = jnp.zeros((1, rows), f32)
        for d in range(len(kv_refs) // 2):
            span = slice(d * rows, (d + 1) * rows)
            key = kv_refs[2 * d][0, :, cols]
            probs, d_scores = score_grads(
                key,
                kv_refs[2 * d + 1][0, :, cols],
                query,
                d_out,
                forget_row,
                delta_row,
                key_cols[span, e : e + 1],
                bias_ref[span, :],
            )
            d_query = d_query + mm_tn(d_scores, key)
            d_row = d_row + jnp.sum(d_scores.astype(f32), axis=0, keepdims=True)
            if d == 0:
                found = mm(d_scores, jnp.concatenate([query, first_col(rows, size)], axis=1))
                sums.append(found[:, size : size + 1])
                d_kv_ref[0, :, cols] = found[:, :size]
                d_kv_ref[1, :, cols] = mm(probs, d_out)
        d_query_ref[:, cols] = d_query * (size ** (-0.5))
        dcq_ref[0, e : e + 1, :] = d_row
    dck_ref[0] = as_rows(sums)


def key_grads_kernel(*refs):
    key_ref, value_ref, bias_ref, ck_ref, own_ref, own_dck_ref = refs[:6]
    sets = refs[6:-2]
    d_kv_ref, dck_ref = refs[-2:]
    count = len(sets) // 3
    rows = key_ref.shape[1]
    size = key_ref.shape[2] // 2
    key_cols = ck_ref[0].T
    forget8 = [rows_back(sets[3 * d + 2], 0) for d in range(count)]
    delta8 = [rows_back(sets[3 * d + 2], 24) for d in range(count)]
    sums = []
    for e in range(2):
        cols = slice(e * size, (e + 1) * size)
        head = 2 * pl.program_id(0) + e
        key, value = key_ref[0, :, cols], value_ref[0, :, cols]
        d_key = jnp.zeros((rows, 2 * size), f32)
        d_value = jnp.zeros((rows, size), f32)
        for d in range(count):
            query, d_out = sets[3 * d][:, cols], sets[3 * d + 1][:, cols]
            probs, d_scores = score_grads(
                key,
                value,
                query,
                d_out,
                head_row(forget8[d], head),
                head_row(delta8[d], head),
                key_cols[:, e : e + 1],
                bias_ref[d * rows : (d + 1) * rows, :],
            )
            d_key = d_key + mm(
                d_scores, jnp.concatenate([query, first_col(rows, size)], axis=1)
            )
            d_value = d_value + mm(probs, d_out)
        sums.append(d_key[:, size : size + 1])
        d_kv_ref[0, :, cols] = own_ref[0, :, cols] + d_key[:, :size]
        d_kv_ref[1, :, cols] = own_ref[1, :, cols] + d_value
    dck_ref[0] = own_dck_ref[0] + as_rows(sums)


def kv_specs(blocks, lanes):
    rows = blocks[0].shape[1]
    return [
        pl.BlockSpec((1, rows, lanes), lambda p, kind=kind: (kind, 0, p))
        for _ in blocks
        for kind in range(2)
    ]


def twice(blocks):
    return [b for b in blocks for _ in range(2)]


def attention(place, query, kv_blocks, bias, forget_q, forget_k, raw_g):
    rows, local = query.shape
    pairs = forget_q.shape[0]
    keys = bias.shape[0]
    lanes = local // pairs
    flat = pl.BlockSpec((rows, lanes), lambda p: (0, p))
    row_spec = pl.BlockSpec((1, 8, rows), lambda p: (p, 0, 0))
    return pl.pallas_call(
        attend_kernel,
        grid=(pairs,),
        in_specs=[pl.BlockSpec(memory_space=pltpu.SMEM), flat]
        + kv_specs(kv_blocks, lanes)
        + [
            pl.BlockSpec((keys, rows), lambda p: (0, 0)),
            row_spec,
            pl.BlockSpec((1, 8, keys), lambda p: (p, 0, 0)),
            flat,
        ],
        out_specs=[flat, flat, row_spec],
        out_shape=[
            jax.ShapeDtypeStruct((rows, local), f32),
            jax.ShapeDtypeStruct((rows, local), bf16),
            jax.ShapeDtypeStruct((pairs, 8, rows), f32),
        ],
        compiler_params=pltpu.CompilerParams(vmem_limit_bytes=20 << 20),
        cost_estimate=pl.CostEstimate(flops=1, transcendentals=1, bytes_accessed=1),
        name="attend",
    )(place, query, *twice(kv_blocks), bias, forget_q, forget_k, raw_g)


def message_specs(rows, lanes, width):
    return [
        pl.BlockSpec((rows, lanes), lambda p: (0, p)),
        pl.BlockSpec((row_room, width), lambda p: (rows // row_room, 0)),
    ]


def back_params():
    return {
        "compiler_params": pltpu.CompilerParams(vmem_limit_bytes=20 << 20),
        "cost_estimate": pl.CostEstimate(flops=1, transcendentals=1, bytes_accessed=1),
    }


def query_grads(own_query, own_out, kv_blocks, bias, forget_k):
    keys, rows = bias.shape
    local = own_query.shape[1]
    pairs = forget_k.shape[0]
    lanes = local // pairs
    flat, row_block = message_specs(rows, lanes, local)
    row_spec = pl.BlockSpec((1, 8, rows), lambda p: (p, 0, 0))
    return pl.pallas_call(
        query_grads_kernel,
        grid=(pairs,),
        in_specs=[flat, flat, row_block]
        + kv_specs(kv_blocks, lanes)
        + [
            pl.BlockSpec((keys, rows), lambda p: (0, 0)),
            pl.BlockSpec((1, 8, keys), lambda p: (p, 0, 0)),
        ],
        out_specs=[
            flat,
            pl.BlockSpec((2, rows, lanes), lambda p: (0, 0, p)),
            row_spec,
            row_spec,
        ],
        out_shape=[
            jax.ShapeDtypeStruct((rows, local), f32),
            jax.ShapeDtypeStruct((2, rows, local), f32),
            jax.ShapeDtypeStruct((pairs, 8, rows), f32),
            jax.ShapeDtypeStruct((pairs, 8, rows), f32),
        ],
        name="query_grads",
        **back_params(),
    )(own_query, own_out, own_out, *twice(kv_blocks), bias, forget_k)


def key_grads(own_kv, later, forget_k, own_grads, own_dck, queries, outs):
    rows, local = own_kv.shape[1:]
    pairs = forget_k.shape[0]
    lanes = local // pairs
    flat, row_block = message_specs(rows, lanes, local)
    row_spec = pl.BlockSpec((1, 8, rows), lambda p: (p, 0, 0))
    pair_spec = pl.BlockSpec((2, rows, lanes), lambda p: (0, 0, p))
    return pl.pallas_call(
        key_grads_kernel,
        grid=(pairs,),
        in_specs=kv_specs([own_kv], lanes)
        + [pl.BlockSpec(later.shape, lambda p: (0, 0)), row_spec, pair_spec, row_spec]
        + [flat, flat, row_block] * len(queries),
        out_specs=[pair_spec, row_spec],
        out_shape=[
            jax.ShapeDtypeStruct((2, rows, local), f32),
            jax.ShapeDtypeStruct((pairs, 8, rows), f32),
        ],
        name="key_grads",
        **back_params(),
    )(
        own_kv,
        own_kv,
        later,
        forget_k,
        own_grads,
        own_dck,
        *[x for q, o in zip(queries, outs) for x in (q, o, o)],
    )


def small_kernel(d_lin, first_in, gains, other, gain_q, gain_k, d_bias, *outs):
    part = first_in.shape[1] // len(outs)
    local = gain_q.shape[1]
    for d, out in enumerate(outs):
        cols = slice(d * part, (d + 1) * part)
        out[...] = jnp.zeros_like(out)
        out[:24, :part] = mm(d_lin[...], first_in[:, cols])
        out[24:26, :part] = gains[:, cols] + other[:, cols]
        out[26:27, :local] = gain_q[...]
        out[27:28, :local] = gain_k[...]
        out[32:40, :1] = d_bias[...]


def pieces_kernel(place, *refs):
    out = refs[-1]
    count = len(refs) - 1
    rows = refs[0].shape[0]
    for k, piece in enumerate(refs[:count]):
        start = pl.multiple_of(lax.rem(place[2] + k, count) * rows, 16)
        out[pl.ds(start, rows), :] = piece[...]


class Order:

    def __init__(self):
        self.last, self.held = None, []

    def tied(self, *args):
        if self.last is not None:
            args, _, _ = lax.optimization_barrier((args, self.last, self.held))
        self.held = []
        return args

    def hold(self, values):
        self.held.append(values)

    def __call__(self, work, *args):
        found = work(*self.tied(*args))
        self.last = min(jax.tree.leaves(found), key=nbytes)
        return found


class LineSum:

    def __init__(self, order, values):
        self.order, self.total = order, values
        self.count = lax.axis_size("ctx")
        self.half = self.count // 2
        self.hop, self.coming = 0, None
        self.send()

    def send(self):
        k, count, half = self.hop, self.count, self.half
        if k < half - 1:
            pairs = [(k, k + 1), (count - 1 - k, count - 2 - k)]
        elif k == half - 1:
            pairs = [(half - 1, half), (half, half - 1)]
        elif k < 2 * half - 1:
            j = 2 * half - 2 - k
            pairs = [(j + 1, j), (count - 2 - j, count - 1 - j)]
        else:
            return
        self.coming = lax.ppermute(self.total, "ctx", pairs)

    def step(self):
        k, half = self.hop, self.half
        self.hop += 1
        if k < half:
            self.total = self.order(add_rows, self.total, self.coming)
            self.coming = None
        elif k < 2 * half - 2:
            j = 2 * half - 2 - k
            index = lax.axis_index("ctx")
            at_ends = (index == j) | (index == self.count - 1 - j)
            self.total = self.order(
                lambda a, b: jnp.where(at_ends, b, a), self.total, self.coming
            )
            self.coming = None
        else:
            self.order.hold(self.coming)
            return
        self.send()

    def finish(self):
        while self.hop < 2 * self.half - 1:
            self.step()
        return self.total, self.coming


def spread_out(order, place, planes):
    sums = [s.finish() for plane in planes for s in plane]
    arrays = [x for pair in sums for x in pair if x is not None]
    each = len(arrays) // len(sums)
    height, width = planes[0][0].total.shape
    chunks = len(planes[0])
    block = 128 if height % 128 == 0 else height
    steps = height // block
    count = lax.axis_size("ctx")

    def spread_out_kernel(place, *refs):
        out = refs[-1]
        at_ends = (place[2] == 0) | (place[2] == count - 1)
        for c in range(chunks):

            @pl.when(pl.program_id(0) // steps == c)
            def _():
                for i in range(len(planes)):
                    first = (i * chunks + c) * each
                    value = refs[first][...].astype(f32)
                    if each > 1:
                        value = jnp.where(at_ends, refs[first + 1][...].astype(f32), value)
                    if len(planes) > 1:
                        out[:, i, :] = value
                    else:
                        out[...] = value

    def spec(c):
        return pl.BlockSpec(
            (block, width), lambda j: (jnp.clip(j - c * steps, 0, steps - 1), 0)
        )

    specs = [spec(c) for _ in planes for c in range(chunks) for _ in range(each)]
    middle = (len(planes),) if len(planes) > 1 else ()
    call = pl.pallas_call(
        spread_out_kernel,
        grid=(chunks * steps,),
        in_specs=[pl.BlockSpec(memory_space=pltpu.SMEM)] + specs,
        out_specs=pl.BlockSpec((block, *middle, width), lambda j: (j, *(0 for _ in middle), 0)),
        out_shape=jax.ShapeDtypeStruct((chunks * height, *middle, width), f32),
        compiler_params=pltpu.CompilerParams(vmem_limit_bytes=24 << 20),
        cost_estimate=pl.CostEstimate(flops=1, transcendentals=1, bytes_accessed=1),
        name="spread_out",
    )
    return order(call, place, *arrays)


schedule = (
    "bs1", "U10", "ms1", "bs2", "q1", "ms2", "D00", "U11", "U00", "q2", "D10", "mb", "lv", "gb",
    "D01", "G10", "U12", "q3", "aq", "qb", "G00", "ak", "G11", "sb", "G01", "D02", "U13", "D11",
    "rb", "G12", "O0", "fgq", "D03", "G02", "U1h", "U01", "fs1", "G13", "fs2", "Qq1", "D0h", "D12",
    "G03", "fsum", "G1h", "Qg1", "U02", "K1", "V1", "D13", "Qq2", "G0h", "O1", "U03", "D1h", "Qg2",
    "Qq3", "O2", "eb", "U0h", "Qg3", "V2", "Qqh", "sm", "K2", "O3", "so", "gu", "Qgh", "V3", "df",
    "sm1", "Oh", "K3", "sm2", "st", "Vh", "sm3", "of", "Kh", "at", "smf",
)


def body(
    tokens,
    seg_parents,
    seg_offsets,
    tok_seg,
    norm_gain,
    w_attn,
    w_heads,
    forget_bias,
    qk_gain,
    w_out,
    w_gate_up,
    w_down,
    cotangent,
):
    shards = lax.axis_size("shard")
    ctxs = lax.axis_size("ctx")
    ctx = lax.axis_index("ctx")
    tps = lax.axis_size("tp")
    rows, width = tokens.shape[1:]
    half = rows // 2
    part = width // shards
    local = w_attn.shape[2]
    heads = w_heads.shape[2]
    heads_up = 8
    size = local // heads
    hidden_size = w_gate_up.shape[2]
    segs = seg_parents.shape[1]
    order = Order()
    place = jnp.stack(
        [lax.axis_index("tp") % 2, lax.axis_index("shard"), ctx]
    ).astype(jnp.int32)

    def gathered(piece):
        return [piece] + [from_ring(piece, "shard", d) for d in range(1, shards)]

    def owned(piece):
        return [piece[:, :part]] + [
            from_ring(piece[:, part * (shards - d) : part * (shards - d + 1)], "shard", d)
            for d in range(1, shards)
        ]

    def crossed(total):
        bit = 2
        other = partner(total, "tp", bit)
        while bit * 2 < tps:
            total = (total.astype(f32) + other.astype(f32)).astype(bf16)
            bit = bit * 2
            other = partner(total, "tp", bit)
        return total, other

    def pack_small(w, gain):
        table = jnp.pad(
            jnp.transpose(w, (1, 2, 0)), ((0, 0), (0, heads_up - heads), (0, 0))
        ).reshape(3 * heads_up, part)
        return jnp.concatenate([table, jnp.pad(gain, ((0, 6), (0, 0)))], axis=0).astype(bf16)

    piece_rows = hidden_size // ctxs
    piece = order(
        lambda w: lax.dynamic_slice_in_dim(w, ctx * piece_rows, piece_rows, 0).astype(bf16), w_down
    )
    pieces = [from_ring(piece, "shard", d) for d in range(1, shards)]
    packs = gathered(order(pack_small, w_heads, norm_gain))
    attn_b = order(lambda w: jnp.transpose(w, (1, 0, 2)).astype(bf16), w_attn)
    kv_w = gathered(order(lambda w: w[1:3], attn_b))
    padded = jnp.full((segs_up - segs,), -1, jnp.int32)
    low = jnp.concatenate([seg_offsets[0, :segs], padded])
    high = jnp.concatenate([seg_offsets[0, 1:], padded])
    parents = jnp.concatenate([seg_parents[0], padded])
    bias, later, seen, key_anc, onehot, parent, start, ends, anc, _ = order(
        lambda *a: whole(
            masks_kernel,
            [
                ((rows * ctxs, rows), f32),
                ((rows * (ctxs - 1), rows), f32),
                ((rows, rows), f32),
                ((rows * ctxs, segs_up), f32),
                ((rows, segs_up), f32),
                ((rows, segs_up), f32),
                ((rows, 1), f32),
                ((segs_up, rows), f32),
                ((segs_up, segs_up), f32),
                ((rows * ctxs, segs_up), f32),
            ],
            *a,
        ),
        place,
        low[None],
        high[None],
        high[:, None],
        parents[:, None],
        tok_seg[0][:, None],
    )
    tree, cotangent = tokens[0], cotangent[0]
    if part % 128:
        tree = turned(tree, place[1], shards)
        cotangent = turned(cotangent, place[1], shards)

    def settled(values):
        return turned(values, shards - place[1], shards) if part % 128 else values

    for p in pieces:
        order.hold(p)
    (first_in,) = order(
        lambda *a: whole(enter_kernel, [((rows, width), bf16)], *a), place, tree, packs
    )
    pieces = order.tied(*pieces)
    piece_sets = [[p] + [from_ring(p, "ctx", k) for k in range(1, ctxs)] for p in pieces]
    bundles = gathered(
        order(lambda a, w: jnp.stack([a[0], a[3], w.T.astype(bf16)]), attn_b, w_out)
    )
    gateup_w = gathered(
        order(planes_of, w_gate_up)
    )

    own_down = order(lambda w: w.astype(bf16), w_down)

    forget_col = jnp.pad(forget_bias, (0, heads_up - heads))[:, None]
    raw_kv, lin, message = order(
        lambda *a: whole(
            keys_in_kernel,
            [
                ((2, rows, local), f32),
                ((3 * heads_up, rows), f32),
                ((segs_up + heads_up, 2 * local), f32),
            ],
            *a,
        ),
        first_in,
        kv_w,
        packs,
        forget_col,
        seen,
        onehot,
        ends,
    )
    order.hold(piece_sets)
    blocks = [message] + [along(message, "ctx", d) for d in range(1, ctxs)]
    gain_q, gain_k = qk_gain[:1], qk_gain[1:]
    own_kv, delta, forget_q, forget_k = order(
        lambda *a: whole(
            named(keys_shift_kernel, size=size),
            [
                ((2, rows, local), bf16),
                ((2, rows, local), f32),
                ((heads // 2, 8, rows), f32),
                ((heads // 2, 8, rows * ctxs), f32),
            ],
            *a,
        ),
        raw_kv,
        lin,
        blocks,
        parent,
        start,
        key_anc,
        gain_k,
    )
    kv_blocks = [own_kv] + [along(own_kv, "ctx", d) for d in range(1, ctxs)]
    down_w = [own_down] + [
        order(
            lambda *a: whole(pieces_kernel, [((hidden_size, part), bf16)], *a)[0], place, *p
        )
        for p in piece_sets
    ]
    grad_out, d_hidden = order(
        lambda *a: whole(
            grad_hidden_kernel, [((rows, width), bf16), ((rows, hidden_size), f32)], *a
        ),
        place,
        cotangent,
        down_w,
    )
    raw_q, query, raw_g = order(
        lambda *a: whole(
            named(queries_kernel, size=size),
            [((rows, local), f32), ((rows, local), bf16), ((rows, local), f32)],
            *a,
        ),
        first_in,
        bundles,
        gain_q,
    )
    attended, gated, lse = order(
        attention, place, query, kv_blocks, bias, forget_q, forget_k, raw_g
    )

    (share,) = order(
        lambda *a: whole(attn_share_kernel, [((half, width), f32)], *a), gated, bundles
    )
    given = partner(share, "tp", 1)
    (total,) = order(
        lambda *a: whole(attn_share_sum_kernel, [((half, width), bf16)], *a),
        gated,
        bundles,
        given,
    )
    total, other = crossed(total)
    middle, second = order(
        lambda *a: whole(
            middle_kernel, [((half, width), f32), ((half, width), bf16)], *a
        ),
        place,
        tree,
        packs,
        total,
        other,
    )
    second_too = partner(second, "tp", 1)
    hidden, d_lin, keep, give = order(mlp, second, second_too, gateup_w, d_hidden)
    first_parts = owned(order.tied(first_in)[0])

    at = {}
    hidden_half, part_half = hidden_size // 2, part // 2

    def core_sum(name, kernel, out, *args):
        def run(given):
            (at[name],) = order(
                lambda *a: whole(kernel, [((half, width), out)], *a), *args, *given
            )

        return run

    def shared(kernel, *args):
        (share,) = order(lambda *a: whole(kernel, [((half, width), f32)], *a), *args)
        return partner(share, "tp", 1)

    def total_of(kernel, *args):
        (total,) = order(lambda *a: whole(kernel, [((half, width), bf16)], *a), *args)
        return crossed(total)

    def rows_at(k):
        return (k * half, (k + 1) * half)

    def out_part(d, got=()):
        return weight_grad(
            order,
            [
                (At(gated, rows=rows_at(k)), At(x, cols=(d * part, (d + 1) * part)))
                for k, x in enumerate((at["mb"], at["mb_too"]))
            ],
            got,
            min(128, local),
        )

    def summed(left_ones, right_ones, block, cols=None, lead=None, right_cols=None):
        return LineSum(
            order,
            weight_grad(
                order,
                [
                    (At(a, cols=cols), At(b, lead=lead, cols=right_cols))
                    for a, b in zip(left_ones, right_ones)
                ],
                (),
                block,
            ),
        )

    def run_bs1():
        at["bs1"] = partner(order.tied(give)[0], "tp", 1)

    def run_bs2():
        (total,) = order(
            lambda *a: whole(first_sum_kernel, [(keep.shape, bf16)], *a), keep, at["bs1"]
        )
        at["bs2"] = crossed(total)

    def column_part(d, start, stop):
        return (d * part + start, d * part + stop)

    def down_part(i, d, got=()):
        return weight_grad(
            order,
            [
                (
                    At(hidden, cols=(i * hidden_half, (i + 1) * hidden_half)),
                    At(grad_out, cols=column_part(d, 0, part)),
                )
            ],
            got,
            256,
        )

    def lin_part(lead, i, d, got=()):
        return weight_grad(
            order,
            [
                (
                    At(x, cols=column_part(d, i * part_half, (i + 1) * part_half)),
                    At(d_lin, rows=rows_at(k), lead=lead),
                )
                for k, x in enumerate((second, second_too))
            ],
            got,
            min(128, part_half),
        )

    def run_ms1():
        at["ms1"] = shared(named(share_kernel, which=1), hidden, down_w)

    def run_ms2():
        at["ms2"] = total_of(share_sum_kernel, hidden, down_w, at["ms1"])

    def run_mb():
        at["d_middle"], at["mb"], at["gain_two"] = order(
            lambda *a: whole(
                middle_back_kernel,
                [((half, width), f32), ((half, width), bf16), ((1, width), f32)],
                *a,
            ),
            grad_out,
            packs,
            middle,
            *at["bs2"],
        )
        at["mb_too"] = partner(at["mb"], "tp", 1)

    def run_gb():
        at["out_message"], at["d_raw_g"] = order(
            lambda *a: whole(
                named(gate_back_kernel, size=size),
                [((rows + row_room, local), bf16), ((rows, local), bf16)],
                *a,
            ),
            place,
            at["mb"],
            at["mb_too"],
            bundles,
            raw_g,
            attended,
            forget_q,
            lse,
        )
        at["later_outs"] = [along(at["out_message"], "ctx", -d) for d in range(1, ctxs)]

    def run_q(d):
        passed = at["queries"][-1] if d > 1 else query
        passed = order.tied(passed)[0]
        pairs = [(i, i - 1) for i in range(1, ctxs - d + 1)]
        at.setdefault("queries", []).append(lax.ppermute(passed, "ctx", pairs))

    def run_aq():
        order.hold(first_parts[1:])
        at["d_query"], at["own_grads"], at["dcq"], at["own_dck"] = order(
            query_grads, query, at["out_message"], kv_blocks, bias, forget_k
        )

    def run_ak():
        at["d_kv"], at["dck"] = order(
            key_grads,
            own_kv,
            later,
            forget_k,
            at["own_grads"],
            at["own_dck"],
            at["queries"],
            at["later_outs"],
        )

    def run_qb():
        at["d_gq"], at["gain_q"] = order(
            lambda *a: whole(
                named(query_back_kernel, size=size),
                [((rows, 2 * local), bf16), ((1, local), f32)],
                *a,
            ),
            raw_q,
            at["d_query"],
            gain_q,
            at["d_raw_g"],
        )
        at["gq"] = gathered(at["d_gq"])

    def run_fgq():
        (at["fgq"],) = order(
            lambda *a: whole(first_gq_kernel, [((rows, width), f32)], *a),
            place,
            at["d_gq"],
            bundles,
        )

    def run_sb():
        at["base"], at["message"], at["d_alpha"], at["gain_k"], at["d_forget"] = order(
            lambda *a: whole(
                named(shift_back_kernel, size=size),
                [
                    ((2, rows, local), f32),
                    ((segs_up + heads_up, 2 * local), f32),
                    ((2 * heads_up, rows), f32),
                    ((1, local), f32),
                    ((heads_up, rows), f32),
                ],
                *a,
            ),
            at["d_kv"],
            raw_kv,
            delta,
            lin,
            gain_k,
            start,
            parent,
            at["dcq"],
            at["dck"],
            onehot,
        )
        at["returned"] = [along(at["message"], "ctx", -d) for d in range(1, ctxs)]

    def run_rb():
        at["d_raw_kv"], at["d_head"], at["d_bias"] = order(
            lambda *a: whole(
                raw_back_kernel,
                [((2, rows, local), bf16), ((3 * heads_up, rows), bf16), ((heads_up, 1), f32)],
                *a,
            ),
            at["base"],
            at["message"],
            at["returned"],
            ends,
            seen,
            onehot,
            anc,
            lin,
            at["d_forget"],
            at["d_alpha"],
        )
        at["kv"] = gathered(at["d_raw_kv"])

    def first_share(which):
        return order(
            lambda *a: whole(
                named(first_share_kernel_of(part, rows), which=which), [((half, width), f32)], *a
            )[0],
            place,
            at["d_raw_kv"],
            at["d_head"],
            kv_w,
            packs,
            at["fgq"],
        )

    def run_fs1():
        at["fs1"] = partner(first_share(1), "tp", 1)

    def run_fs2():
        at["fs2"] = first_share(0)

    def run_fsum():
        at["fsum"] = total_of(first_sum_kernel, at["fs2"], at["fs1"])

    def run_eb():
        at["eb"], gain_one = order(
            lambda *a: whole(
                enter_back_kernel, [((half, width), f32), ((1, width), f32)], *a
            ),
            place,
            tree,
            packs,
            at["d_middle"],
            *at["fsum"],
        )
        at["eb_too"] = partner(at["eb"], "tp", 1)
        at["gains"] = jnp.concatenate([gain_one, at["gain_two"]], axis=0)
        at["gains_too"] = partner(at["gains"], "tp", 1)

    def settle(name, kind):
        (at[name],) = order(
            lambda *a: whole(named(settle_kernel, shards=shards), [((rows, width), kind)], *a),
            place,
            at[name],
            at[name + "_too"],
        )

    def run_lv():
        (at["lv"],) = order(
            lambda *a: whole(leave_kernel, [((half, width), bf16)], *a), middle, *at["ms2"]
        )
        at["lv_too"] = partner(at["lv"], "tp", 1)

    def run_sm():
        at["sm"] = order(
            lambda *a: whole(
                small_kernel, [((40, max(part, local)), f32) for _ in range(shards)], *a
            ),
            at["d_head"],
            first_in,
            at["gains"],
            at["gains_too"],
            at["gain_q"],
            at["gain_k"],
            at["d_bias"],
        )
        at["sm_got"] = [from_ring(at["sm"][d], "shard", shards - d) for d in range(1, shards)]

    def run_sm1():
        small = at["sm"][0]
        for got in at["sm_got"]:
            small = order(add_rows, small, got)
        at["small"] = LineSum(order, small)

    def run_smf():
        line = at["small"]
        line.step()

        def pick(total, *ends):
            if ends:
                total = jnp.where((ctx == 0) | (ctx == ctxs - 1), ends[0], total)
            table = total[: 3 * heads_up, :part].reshape(3, heads_up, part)[:, :heads]
            return (
                total[24:26, :part],
                jnp.transpose(table, (2, 0, 1)),
                total[32 : 32 + heads, 0],
                total[26:28, :local],
            )

        ends = [line.coming] if line.coming is not None else []
        found = order(pick, line.total, *ends)
        at["small_gain"], at["small_heads"], at["small_bias"], at["small_qk"] = found

    def run_out(name, *planes):
        at[name] = spread_out(order, place, [[at[n] for n in plane] for plane in planes])

    block = min(128, part)
    work = {
        "bs1": run_bs1, "bs2": run_bs2,
        "ms1": run_ms1, "ms2": run_ms2, "mb": run_mb, "gb": run_gb,
        "q1": lambda: run_q(1), "q2": lambda: run_q(2),
        "q3": lambda: [run_q(d) for d in range(3, ctxs)], "aq": run_aq, "ak": run_ak, "qb": run_qb, "fgq": run_fgq,
        "sb": run_sb, "rb": run_rb, "fs1": run_fs1, "fs2": run_fs2, "fsum": run_fsum,
        "eb": run_eb, "st": lambda: settle("eb", f32), "lv": run_lv,
        "so": lambda: settle("lv", bf16), "sm": run_sm, "sm1": run_sm1, "smf": run_smf,
        "gu": lambda: run_out("gu", ("G0", "G1"), ("U0", "U1")),
        "df": lambda: run_out("df", ("D0", "D1")), "of": lambda: run_out("of", ("O",)),
        "at": lambda: run_out("at", ("Qq",), ("K",), ("V",), ("Qg",)),
    }
    starts = {
        "Qg1": lambda: summed(first_parts, at["gq"], block, right_cols=(0, local)),
        "Qq1": lambda: summed(first_parts, at["gq"], block, right_cols=(local, 2 * local)),
        "K1": lambda: summed(first_parts, at["kv"], block, lead=0),
        "V1": lambda: summed(first_parts, at["kv"], block, lead=1),
    }
    makes = {"O": out_part}
    for i in range(2):
        makes[f"D{i}"] = functools.partial(down_part, i)
        for lead, name in enumerate("GU"):
            makes[f"{name}{i}"] = functools.partial(lin_part, lead, i)
    for name, make in makes.items():

        def hand_over(name=name, make=make):
            at[name + "0"] = [
                from_ring(make(d), "shard", shards - d) for d in range(1, shards)
            ]

        work[name + "0"] = hand_over
        starts[name + "1"] = lambda name=name, make=make: LineSum(
            order, make(0, at[name + "0"])
        )
    for name in schedule:
        if name in work:
            work[name]()
        elif name in starts:
            at[name[:-1]] = starts[name]()
        else:
            at["small" if name[:2] == "sm" else name[:-1]].step()
    return (
        settled(at["lv"])[None],
        settled(at["eb"])[None],
        at["small_gain"],
        at["at"],
        at["small_heads"],
        at["small_bias"],
        at["small_qk"],
        at["of"],
        at["gu"],
        at["df"],
    )


def first_share_kernel_of(part, rows):
    def first_share_scoped_kernel(*refs, which):
        pl.run_scoped(
            lambda scratch: first_share_kernel(*refs, scratch, which=which),
            pltpu.VMEM((rows, part), f32),
        )

    return first_share_scoped_kernel


def solution(mesh):
    in_specs = (
        P("shard", "ctx", None),
        P("shard", None),
        P("shard", None),
        P("shard", "ctx"),
        P(None, "shard"),
        P("shard", None, "tp"),
        P("shard", None, "tp"),
        P("tp"),
        P(None, "tp"),
        P("tp", "shard"),
        P("shard", None, "tp"),
        P("tp", "shard"),
        P("shard", "ctx", None),
    )
    out_specs = (
        P("shard", "ctx", None),
        P("shard", "ctx", None),
        P(None, "shard"),
        P("shard", None, "tp"),
        P("shard", None, "tp"),
        P("tp"),
        P(None, "tp"),
        P("tp", "shard"),
        P("shard", None, "tp"),
        P("tp", "shard"),
    )
    return jax.shard_map(body, mesh=mesh, in_specs=in_specs, out_specs=out_specs, check_vma=False)
```
